32 devices in a mesh: replica: 4 (over x, core), fsdp: 8 (over z, y).
Axes of the slice: x: 2, y: 2, z: 4, core: 2. Of those that a mesh axis runs over, the one named last changes fastest.
Arguments:
- decoder_input: bfloat16 [64, 256, 1024], P(('replica', 'fsdp')), may hold values from -6 to 6
- encoder_out: bfloat16 [64, 512, 1024], P(('replica', 'fsdp')), may hold values from -6 to 6
- prefix_length: int32 [64], P(('replica', 'fsdp')), may hold values from 25 to 128
- output_grad: bfloat16 [64, 256, 1024], P(('replica', 'fsdp')), may hold values from -6 to 6
- self_query: bfloat16 [1024, 1024], P('fsdp'), may hold values from -0.1875 to 0.1875
- self_key: bfloat16 [1024, 1024], P('fsdp'), may hold values from -0.1875 to 0.1875
- self_value: bfloat16 [1024, 1024], P('fsdp'), may hold values from -0.1875 to 0.1875
- self_output: bfloat16 [1024, 1024], P('fsdp'), may hold values from -2 to 2
- selfquery_bias: bfloat16 [1024], P('fsdp'), may hold values from -2 to 2
- selfvalue_bias: bfloat16 [1024], P('fsdp'), may hold values from -0.19921875 to 0.19921875
- self_attention_output_bias: bfloat16 [1024], P('fsdp'), may hold values from -2 to 2
- cross_query: bfloat16 [1024, 1024], P('fsdp'), may hold values from -0.1875 to 0.1875
- cross_key: bfloat16 [1024, 1024], P('fsdp'), may hold values from -0.1875 to 0.1875
- cross_value: bfloat16 [1024, 1024], P('fsdp'), may hold values from -0.1875 to 0.1875
- cross_output: bfloat16 [1024, 1024], P('fsdp'), may hold values from -3 to 3
- crossquery_bias: bfloat16 [1024], P('fsdp'), may hold values from -2 to 2
- crossvalue_bias: bfloat16 [1024], P('fsdp'), may hold values from -0.19921875 to 0.19921875
- crossoutput_bias: bfloat16 [1024], P('fsdp'), may hold values from -2 to 2
- expand_weight: bfloat16 [1024, 4096], P('fsdp'), may hold values from -0.1875 to 0.1875
- expand_bias: bfloat16 [4096], P('fsdp'), may hold values from -2 to 2
- down_projection_weight: bfloat16 [4096, 1024], P('fsdp'), may hold values from -0.09375 to 0.09375
- reduce_bias: bfloat16 [1024], P('fsdp'), may hold values from -2 to 2
- selfnorm_gain: bfloat16 [1024], P('fsdp'), may hold values from 0.25 to 1.75
- selfnorm_bias: bfloat16 [1024], P('fsdp'), may hold values from -2 to 2
- crossnorm_gain: bfloat16 [1024], P('fsdp'), may hold values from 0.25 to 1.75
- crossnorm_bias: bfloat16 [1024], P('fsdp'), may hold values from -2 to 2
- finalnorm_gain: bfloat16 [1024], P('fsdp'), may hold values from 0.25 to 1.75
- finalnorm_bias: bfloat16 [1024], P('fsdp'), may hold values from -2 to 2
Outputs:
- layer_out: bfloat16 [64, 256, 1024], P(('replica', 'fsdp'))
- input_grad: float32 [64, 256, 1024], P(('replica', 'fsdp'))
- encoder_grad: float32 [64, 512, 1024], P(('replica', 'fsdp'))
- self_query_grad: float32 [1024, 1024], P('fsdp')
- self_key_grad: float32 [1024, 1024], P('fsdp')
- self_value_grad: float32 [1024, 1024], P('fsdp')
- self_output_grad: float32 [1024, 1024], P('fsdp')
- selfquery_bias_grad: float32 [1024], P('fsdp')
- selfvalue_bias_grad: float32 [1024], P('fsdp')
- selfoutput_bias_grad: float32 [1024], P('fsdp')
- cross_query_grad: float32 [1024, 1024], P('fsdp')
- cross_key_grad: float32 [1024, 1024], P('fsdp')
- cross_value_grad: float32 [1024, 1024], P('fsdp')
- cross_output_grad: float32 [1024, 1024], P('fsdp')
- crossquery_bias_grad: float32 [1024], P('fsdp')
- crossvalue_bias_grad: float32 [1024], P('fsdp')
- crossoutput_bias_grad: float32 [1024], P('fsdp')
- expand_weight_grad: float32 [1024, 4096], P('fsdp')
- expand_bias_grad: float32 [4096], P('fsdp')
- reduce_weight_grad: float32 [4096, 1024], P('fsdp')
- reduce_bias_grad: float32 [1024], P('fsdp')
- selfnorm_gain_grad: float32 [1024], P('fsdp')
- selfnorm_bias_grad: float32 [1024], P('fsdp')
- crossnorm_gain_grad: float32 [1024], P('fsdp')
- crossnorm_bias_grad: float32 [1024], P('fsdp')
- final_norm_gain_gradient: float32 [1024], P('fsdp')
- finalnorm_bias_grad: float32 [1024], P('fsdp')
The draws below stay inside these ranges and needn't reach their ends.
All inputs are finite; a program needn't handle non-finite values.
Results may differ from the reference program's by a relative error of at most 0.023.
Values may be sent and summed in bfloat16 or wider, within the bound.
No kernel may reach another device: no remote copies, remote signals or barrier semaphores. Data moves between devices by JAX's collectives and lax.ppermute only.
A program may use at most 256 MiB of HBM per device.

```python
from functools import partial
import jax
import jax.numpy as jnp
from jax import lax

D = 1024
H = 16
HD = 64
FF = 4096
SEQ = 256
ENC = 512
NSEQ_DEV = 2
NSEQ = 64


def place_ends(array, own_key, low, top_value):
    longest = array.shape.index(max(array.shape))
    spots = []
    for shift in (0, 1):
        where = [jax.random.randint(jax.random.fold_in(own_key, axis), (), 0, length) for axis, length in enumerate(array.shape)]
        where[longest] = (where[longest] + shift) % array.shape[longest]
        spots.append(tuple(where))
    return array.at[spots[0]].set(low).at[spots[1]].set(top_value)


def block_levels(key, dims, split, least, largest):
    def one(dim, parts):
        heights = jax.random.uniform(jax.random.fold_in(jax.random.fold_in(key, 6), dim), (parts,), jnp.float32, least / len(split), largest / len(split))
        return jnp.repeat(jnp.exp(heights), dims[dim] // parts).reshape((-1,) + (1,) * (len(dims) - dim - 1))

    level = one(*split[0])
    for cut in split[1:]:
        level = level * one(*cut)
    return level


def noise(rng, shape, scale, most, split=(), held_as=jnp.bfloat16):
    gain = block_levels(rng, shape, split, -0.22, 0.18) if split else 1.0
    entries = jax.random.normal(rng, shape, jnp.float32) * scale * gain
    return jnp.minimum(jnp.maximum(entries, -most), most).astype(held_as)


def setup_inputs(seed: int = 0) -> dict:
    streams_of = jax.random.split(jax.random.key(seed), 29)
    return {
        "decoder_input": noise(streams_of[0], (NSEQ, SEQ, D), 1.0, 6.0, ((0, 32),)),
        "encoder_out": noise(streams_of[1], (NSEQ, ENC, D), 1.0, 6.0, ((0, 32),)),
        "prefix_length": place_ends(jax.random.randint(streams_of[2], (NSEQ,), max(SEQ // 10, 1), SEQ // 2 + 1), jax.random.fold_in(streams_of[2], 1), max(SEQ // 10, 1), (SEQ // 2 + 1) - 1).astype(jnp.int32),
        "output_grad": noise(streams_of[3], (NSEQ, SEQ, D), 1.0, 6.0, ((0, 32),)),
        "self_query": noise(streams_of[4], (D, D), D ** -0.5, 0.1875, ((0, 8),)),
        "self_key": noise(streams_of[5], (D, D), D ** -0.5, 0.1875, ((0, 8),)),
        "self_value": noise(streams_of[6], (D, D), D ** -0.5, 0.1875, ((0, 8),)),
        "self_output": noise(streams_of[7], (D, D), (max(D // 128, 1)) ** -0.5, 2.0, ((0, 8),)),
        "selfquery_bias": noise(streams_of[8], (D,), 0.3, 2.0, ((0, 8),)),
        "selfvalue_bias": noise(streams_of[9], (D,), 0.03, 0.19921875, ((0, 8),)),
        "self_attention_output_bias": noise(streams_of[10], (D,), 0.3, 2.0, ((0, 8),)),
        "cross_query": noise(streams_of[11], (D, D), D ** -0.5, 0.1875, ((0, 8),)),
        "cross_key": noise(streams_of[12], (D, D), D ** -0.5, 0.1875, ((0, 8),)),
        "cross_value": noise(streams_of[13], (D, D), D ** -0.5, 0.1875, ((0, 8),)),
        "cross_output": noise(streams_of[14], (D, D), (max(D // 256, 1)) ** -0.5, 3.0, ((0, 8),)),
        "crossquery_bias": noise(streams_of[15], (D,), 0.3, 2.0, ((0, 8),)),
        "crossvalue_bias": noise(streams_of[16], (D,), 0.03, 0.19921875, ((0, 8),)),
        "crossoutput_bias": noise(streams_of[17], (D,), 0.3, 2.0, ((0, 8),)),
        "expand_weight": noise(streams_of[18], (D, FF), D ** -0.5, 0.1875, ((0, 8),)),
        "expand_bias": noise(streams_of[19], (FF,), 0.3, 2.0, ((0, 8),)),
        "down_projection_weight": noise(streams_of[20], (FF, D), FF ** -0.5, 0.09375, ((0, 8),)),
        "reduce_bias": noise(streams_of[21], (D,), 0.3, 2.0, ((0, 8),)),
        "selfnorm_gain": jnp.clip(1.0 + 0.15 * jax.random.normal(streams_of[22], (D,), jnp.float32), 0.25, 1.75).astype(jnp.bfloat16),
        "selfnorm_bias": noise(streams_of[23], (D,), 0.3, 2.0, ((0, 8),)),
        "crossnorm_gain": jnp.clip(1.0 + 0.15 * jax.random.normal(streams_of[24], (D,), jnp.float32), 0.25, 1.75).astype(jnp.bfloat16),
        "crossnorm_bias": noise(streams_of[25], (D,), 0.3, 2.0, ((0, 8),)),
        "finalnorm_gain": jnp.clip(1.0 + 0.15 * jax.random.normal(streams_of[26], (D,), jnp.float32), 0.25, 1.75).astype(jnp.bfloat16),
        "finalnorm_bias": noise(streams_of[27], (D,), 0.3, 2.0, ((0, 8),)),
    }


@jax.custom_vjp
def low(v):
    return lax.optimization_barrier(v.astype(jnp.bfloat16)).astype(jnp.float32)

@jax.custom_vjp
def low_back(v):
    return v

def low_keep(v):
    return (low(v), None)

def low_pass(kept, grad):
    return (grad,)

def back_keep(v):
    return (v, None)

def back_low(kept, grad):
    return (low(grad),)
low.defvjp(low_keep, low_pass)
low_back.defvjp(back_keep, back_low)
EPSILON = 1e-05
MASKED = -1e+30

def matmul(left, right):
    return jnp.dot(left, right, precision=lax.Precision.HIGHEST, preferred_element_type=jnp.float32)

def twoway(values):
    return low(low_back(values))

def normalize(values, gain_vec, shift_vec):
    average = lax.optimization_barrier(jnp.mean(values, -1, keepdims=True))
    centered = values - average
    variance = lax.optimization_barrier(jnp.mean(centered * centered, -1, keepdims=True))
    return centered * lax.rsqrt(variance + EPSILON) * gain_vec + shift_vec

def attend(queries, key_rows, values, allowed):
    count = queries.shape[0]
    query_h = queries.reshape(count, H, HD)
    key_h = key_rows.reshape(key_rows.shape[0], H, HD)
    value_h = values.reshape(values.shape[0], H, HD)
    scores = low_back(jnp.einsum('qhd,khd->hqk', query_h, key_h, precision=lax.Precision.HIGHEST) * HD ** (-0.5))
    if allowed is not None:
        scores = jnp.where(allowed, scores, MASKED)
    row_max = lax.optimization_barrier(jnp.max(scores, -1, keepdims=True))
    exponent = jnp.exp(scores - row_max)
    probs_all = exponent / lax.optimization_barrier(jnp.sum(exponent, -1, keepdims=True))
    attended = jnp.einsum('hqk,khd->qhd', low(probs_all), value_h, precision=lax.Precision.HIGHEST)
    return twoway(attended.reshape(count, H * HD))

def layer_seq(params, rows_in, memory, limit):
    self_query, self_key, self_value, self_output, selfquery_bias, selfvalue_bias, self_attention_output_bias, cross_query, cross_key, cross_value, cross_output, crossquery_bias, crossvalue_bias, crossoutput_bias, expand_weight, expand_bias, down_projection_weight, reduce_bias, selfnorm_gain, selfnorm_bias, crossnorm_gain, crossnorm_bias, finalnorm_gain, finalnorm_bias = params
    position = jnp.arange(SEQ, dtype=jnp.int32)
    allowed = (position[None, :] < limit) | (position[None, :] <= position[:, None])
    first_activation = low(normalize(rows_in, selfnorm_gain, selfnorm_bias))
    queries = twoway(matmul(first_activation, self_query) + selfquery_bias)
    key_rows = twoway(matmul(first_activation, self_key))
    values = twoway(matmul(first_activation, self_value) + selfvalue_bias)
    middle_one = rows_in + low_back(matmul(attend(queries, key_rows, values, allowed), self_output) + self_attention_output_bias)
    act_two = low(normalize(middle_one, crossnorm_gain, crossnorm_bias))
    cross_queries = twoway(matmul(act_two, cross_query) + crossquery_bias)
    cross_keys = twoway(matmul(memory, cross_key))
    cross_values = twoway(matmul(memory, cross_value) + crossvalue_bias)
    middle_two = middle_one + low_back(matmul(attend(cross_queries, cross_keys, cross_values, None), cross_output) + crossoutput_bias)
    act_three = low(normalize(middle_two, finalnorm_gain, finalnorm_bias))
    hidden = low(jax.nn.gelu(low_back(matmul(act_three, expand_weight) + expand_bias), approximate=False))
    return middle_two + low_back(matmul(hidden, down_projection_weight) + reduce_bias)

def reference(decoder_input, encoder_out, prefix_length, output_grad, self_query, self_key, self_value, self_output, selfquery_bias, selfvalue_bias, self_attention_output_bias, cross_query, cross_key, cross_value, cross_output, crossquery_bias, crossvalue_bias, crossoutput_bias, expand_weight, expand_bias, down_projection_weight, reduce_bias, selfnorm_gain, selfnorm_bias, crossnorm_gain, crossnorm_bias, finalnorm_gain, finalnorm_bias):
    params = tuple((weight_in.astype(jnp.float32) for weight_in in (self_query, self_key, self_value, self_output, selfquery_bias, selfvalue_bias, self_attention_output_bias, cross_query, cross_key, cross_value, cross_output, crossquery_bias, crossvalue_bias, crossoutput_bias, expand_weight, expand_bias, down_projection_weight, reduce_bias, selfnorm_gain, selfnorm_bias, crossnorm_gain, crossnorm_bias, finalnorm_gain, finalnorm_bias)))
    groups = NSEQ // NSEQ_DEV
    inputs = decoder_input.astype(jnp.float32).reshape(groups, NSEQ_DEV, SEQ, D)
    encoder_states = encoder_out.astype(jnp.float32).reshape(groups, NSEQ_DEV, ENC, D)
    prefixes = prefix_length.astype(jnp.int32).reshape(groups, NSEQ_DEV)
    cotangent = output_grad.astype(jnp.float32).reshape(groups, NSEQ_DEV, SEQ, D)

    def forward(weights, row_groups, memory_groups):

        def scan_step(carried, sliced):
            rows_in, memory, limits = sliced
            return (carried, jax.vmap(partial(layer_seq, weights))(rows_in, memory, limits))
        _, produced = lax.scan(jax.checkpoint(scan_step), jnp.zeros((), jnp.float32), (row_groups, memory_groups, prefixes))
        return produced
    layer_out, backward = jax.vjp(forward, params, inputs, encoder_states)
    weight_grads, input_grad, encoder_grad = backward(cotangent)
    return (layer_out.reshape(NSEQ, SEQ, D).astype(jnp.bfloat16), input_grad.reshape(NSEQ, SEQ, D), encoder_grad.reshape(NSEQ, ENC, D), weight_grads[0], weight_grads[1], weight_grads[2], weight_grads[3], weight_grads[4], weight_grads[5], weight_grads[6], weight_grads[7], weight_grads[8], weight_grads[9], weight_grads[10], weight_grads[11], weight_grads[12], weight_grads[13], weight_grads[14], weight_grads[15], weight_grads[16], weight_grads[17], weight_grads[18], weight_grads[19], weight_grads[20], weight_grads[21], weight_grads[22], weight_grads[23])
```

```python
from functools import partial

import jax
import jax.numpy as jnp
import numpy as np
from jax import lax
from jax.experimental import pallas as pl
from jax.experimental.pallas import tpu as pltpu
from jax.sharding import PartitionSpec as P

H = 16
EPSILON = 1e-05
MASKED = -1e30
BF = jnp.bfloat16
F32 = jnp.float32


class Place:
    def __init__(self, groups, rows):
        self.groups = groups
        self.rows = rows
        self.ring = rows // 2
        rep = lax.axis_index("replica")
        row = lax.axis_index("fsdp")
        self.c = lax.rem(rep, 2)
        self.x = lax.div(rep, 2)
        self.y = lax.rem(row, 2)
        self.z = lax.div(row, 2)

    def core(self, v):
        return lax.ppermute(v, "replica", [(i, i ^ 1) for i in range(self.groups)])

    def across(self, v):
        return lax.ppermute(v, "replica", [(i, i ^ 2) for i in range(self.groups)])

    def pair(self, v):
        return lax.ppermute(v, "fsdp", [(i, i ^ 1) for i in range(self.rows)])

    def next(self, v):
        return lax.ppermute(v, "fsdp", [(i, (i + 2) % self.rows) for i in range(self.rows)])

    def ring_members(self):
        return [[2 * k + side for k in range(self.ring)] for side in range(2)]


def at(v, i, axis=0):
    return lax.dynamic_index_in_dim(v, i, axis, keepdims=False)


class Lane:
    def __init__(self, width):
        self.width = width
        self.past = []

    def __call__(self, send, v):
        if len(self.past) >= self.width:
            v, _ = lax.optimization_barrier((v, self.past[-self.width]))
        got = send(v)
        self.past.append(got)
        return got


def ring_gather(place, piece):
    if place.ring <= 4:
        copies = jnp.broadcast_to(piece[None], (place.ring,) + piece.shape)
        return lax.all_to_all(copies, "fsdp", 0, 0, axis_index_groups=place.ring_members())
    return lax.all_gather(piece, "fsdp", axis_index_groups=place.ring_members())


def order_kernel(ring, split, mine, theirs, out, sems):
    rep = lax.axis_index("replica")
    c, x = lax.rem(rep, 2), lax.div(rep, 2)
    y = lax.rem(lax.axis_index("fsdp"), 2)
    copies = []
    for dc, block in enumerate((mine, theirs)):
        cc = 1 - c if dc else c
        for dx in range(2 if split else 1):
            for dy in range(2):
                yy = 1 - y if dy else y
                for z in range(ring):
                    if split:
                        xx = 1 - x if dx else x
                        src, dst = block.at[dx, dy, z], out.at[z, yy, xx, cc]
                    else:
                        src, dst = block.at[dy, z], out.at[z, yy, cc]
                    copies.append(pltpu.make_async_copy(src, dst, sems.at[len(copies)]))
    for copy in copies:
        copy.start()
    for copy in copies:
        copy.wait()


def in_order(place, split, mine, theirs):
    ring, rows, n = mine.shape[-3:]
    dims = (ring, 2, 2, 2) if split else (ring, 2, 2)
    if rows % 16 == 0:
        count = 2 * mine.size // (rows * n)
        out = pl.pallas_call(
            partial(order_kernel, ring, split),
            out_shape=jax.ShapeDtypeStruct(dims + (rows, n), mine.dtype),
            in_specs=[pl.BlockSpec(memory_space=pl.ANY)] * 2,
            out_specs=pl.BlockSpec(memory_space=pltpu.VMEM),
            scratch_shapes=[pltpu.SemaphoreType.DMA((count,))],
            cost_estimate=pl.CostEstimate(
                flops=0, transcendentals=0, bytes_accessed=4 * count * rows * n
            ),
            name="order",
        )(mine, theirs)
    else:
        both = jnp.stack([mine, theirs])
        at_c = (place.c, 1 - place.c)
        both = jnp.stack([at(both, i, 0) for i in at_c])
        if split:
            both = jnp.stack([at(both, i, 1) for i in (place.x, 1 - place.x)], 1)
        both = jnp.stack([at(both, i, both.ndim - 4) for i in (place.y, 1 - place.y)], both.ndim - 4)
        out = jnp.transpose(both, (3, 2, 1, 0, 4, 5) if split else (2, 1, 0, 3, 4))
    return out.reshape(-1, n)


class Gather:
    def __init__(self, place, lane, ring_lane, shard, split):
        self.place, self.lane, self.ring_lane, self.split = place, lane, ring_lane, split
        m, n = shard.shape
        if split:
            self.v = at(shard.reshape(4, m // 4, n), 2 * place.x + place.c)
        else:
            self.v = at(shard.reshape(2, m // 2, n), place.c)
        self.steps = [self.ring, self.pair] + ([self.across] if split else []) + [self.core]

    def ring(self):
        self.v = self.ring_lane(partial(ring_gather, self.place), self.v)

    def pair(self):
        self.v = jnp.stack([self.v, self.lane(self.place.pair, self.v)])

    def across(self):
        self.v = jnp.stack([self.v, self.lane(self.place.across, self.v)])

    def core(self):
        self.v = in_order(self.place, self.split, self.v, self.lane(self.place.core, self.v))


def run_steps(units):
    last = max(i + len(u.steps) for i, u in enumerate(units))
    for t in range(last):
        for i, u in enumerate(units):
            if 0 <= t - i < len(u.steps):
                u.steps[t - i]()


def gather_vectors(place, packed):
    a = ring_gather(place, packed)
    b = place.pair(a)
    both = jnp.stack([jnp.where(place.y == 0, a, b), jnp.where(place.y == 0, b, a)], 1)
    return both.reshape((place.rows,) + packed.shape)


def product_t(left, right):
    return lax.dot_general(
        left, right, (((0,), (0,)), ((), ())), preferred_element_type=F32
    )


def columns(v, k, i):
    w = v.shape[1] // k
    return lax.dynamic_slice(v, (0, i * w), (v.shape[0], w))


def join2(own, other, bit):
    first = jnp.where(bit == 0, own, other)
    second = jnp.where(bit == 0, other, own)
    return jnp.concatenate([first, second], -1)


def ring_sum(place, parts):
    if place.ring <= 4:
        came = lax.all_to_all(parts, "fsdp", 0, 0, axis_index_groups=place.ring_members())
        return jnp.sum(came.astype(F32), 0).astype(BF)
    return lax.psum_scatter(
        parts, "fsdp", scatter_dimension=0, axis_index_groups=place.ring_members()
    )


class Scatter:
    def __init__(self, place, lane, ring_lane, left, right, split):
        self.place, self.lane, self.ring_lane, self.split = place, lane, ring_lane, split
        self.left, self.right = left, right
        self.steps = [self.core] + ([self.across] if split else []) + [self.pair, self.ring]

    def core(self):
        c = self.place.c
        away = product_t(self.left, columns(self.right, 2, 1 - c)).astype(BF)
        self.right = columns(self.right, 2, c)
        self.came = self.lane(self.place.core, away)

    def across(self):
        x = self.place.x
        away = product_t(self.left, columns(self.right, 2, 1 - x))
        away = (away + columns(self.came, 2, 1 - x).astype(F32)).astype(BF)
        self.right, self.came = columns(self.right, 2, x), columns(self.came, 2, x)
        self.came_x = self.lane(self.place.across, away)

    def pair(self):
        part = product_t(self.left, self.right) + self.came.astype(F32)
        if self.split:
            part = part + self.came_x.astype(F32)
        part = part.astype(BF)
        part = part.reshape(self.place.ring, 2, -1, part.shape[1])
        y = self.place.y
        came = self.lane(self.place.pair, at(part, 1 - y, 1))
        self.kept = (at(part, y, 1).astype(F32) + came.astype(F32)).astype(BF)

    def ring(self):
        self.own = self.ring_lane(partial(ring_sum, self.place), self.kept)


def finish(place, lane, units):
    flat = [u.own.reshape(-1, 128) for u in units]
    sizes = [f.shape[0] for f in flat]
    own = jnp.concatenate(flat)
    came = lane(place.across, own)
    pieces, at_row = [], 0
    for u, size in zip(units, sizes):
        mine, other = own[at_row : at_row + size], came[at_row : at_row + size]
        at_row += size
        mine, other = mine.reshape(u.own.shape), other.reshape(u.own.shape)
        if u.split:
            pieces.append(join2(mine, other, place.x))
        else:
            pieces.append((mine.astype(F32) + other.astype(F32)).astype(BF))
    own = jnp.concatenate([p.reshape(-1, 128) for p in pieces])
    came = lane(place.core, own)
    out, at_row = [], 0
    for p in pieces:
        size = p.size // 128
        out.append(join2(p, came[at_row : at_row + size].reshape(p.shape), place.c).astype(F32))
        at_row += size
    return out


def scatter_vectors(place, lane, ring_lane, v):
    own = v.astype(BF)
    own = (own.astype(F32) + lane(place.core, own).astype(F32)).astype(BF)
    own = (own.astype(F32) + lane(place.across, own).astype(F32)).astype(BF)
    own = own.reshape((place.ring, 2) + own.shape[1:])
    came = lane(place.pair, at(own, 1 - place.y, 1))
    own = (at(own, place.y, 1).astype(F32) + came.astype(F32)).astype(BF)
    return ring_lane(partial(ring_sum, place), own).astype(F32)


PAIR = 128


def half_masks(rows):
    lane = lax.broadcasted_iota(jnp.int32, (rows, PAIR), 1)
    return (lane < PAIR // 2, lane >= PAIR // 2)


def dot_nt(a, b):
    return lax.dot_general(a, b, (((1,), (1,)), ((), ())), preferred_element_type=F32)


def attend_kernel(masked, scale, prefix_ref, q_ref, k_ref, v_ref, o_ref, p_ref):
    rows, keys = q_ref.shape[0], k_ref.shape[0]
    masks = half_masks(rows)
    if masked:
        i = lax.broadcasted_iota(jnp.int32, (rows, keys), 0)
        j = lax.broadcasted_iota(jnp.int32, (rows, keys), 1)
        allowed = (j <= i) | (j < prefix_ref[pl.program_id(0)])
    for pair in range(q_ref.shape[1] // PAIR):
        lanes = slice(pair * PAIR, (pair + 1) * PAIR)
        q, k, v = q_ref[:, lanes], k_ref[:, lanes], v_ref[:, lanes]
        both = []
        for h in range(2):
            s = dot_nt(jnp.where(masks[h], q, jnp.zeros_like(q)), k)
            if masked:
                s = jnp.where(allowed, s, MASKED)
            e = jnp.exp((s - jnp.max(s, -1, keepdims=True)) * scale)
            p = (e * (1.0 / jnp.sum(e, -1, keepdims=True))).astype(BF)
            p_ref[2 * pair + h] = p
            both.append(jnp.dot(p, v, preferred_element_type=F32))
        o_ref[:, lanes] = jnp.where(masks[0], both[0], both[1]).astype(BF)


def attend(q, k, v, prefix, batch, masked, group=4):
    rows, keys, d = q.shape[0] // batch, k.shape[0] // batch, q.shape[1]
    wide = group * d // H
    spec = lambda n: pl.BlockSpec((n, wide), lambda b, g, *_: (b, g))
    return pl.pallas_call(
        partial(attend_kernel, masked, (d // H) ** -0.5),
        grid_spec=pltpu.PrefetchScalarGridSpec(
            num_scalar_prefetch=1,
            grid=(batch, H // group),
            in_specs=[spec(rows), spec(keys), spec(keys)],
            out_specs=[
                spec(rows),
                pl.BlockSpec((None, group, rows, keys), lambda b, g, *_: (b, g, 0, 0)),
            ],
        ),
        out_shape=[
            jax.ShapeDtypeStruct(q.shape, BF),
            jax.ShapeDtypeStruct((batch, H, rows, keys), BF),
        ],
        compiler_params=pltpu.CompilerParams(vmem_limit_bytes=40 * 2**20),
        cost_estimate=pl.CostEstimate(
            flops=16 * q.size * keys,
            transcendentals=batch * H * rows * keys,
            bytes_accessed=4 * q.size + 4 * k.size + 2 * batch * H * rows * keys,
        ),
        name="attend",
    )(prefix, q, k, v)


def attend_back_kernel(scale, do_ref, q_ref, k_ref, v_ref, p_ref, dq_ref, dk_ref, dv_ref):
    rows = q_ref.shape[0]
    half = PAIR // 2
    masks = half_masks(rows)
    for pair in range(q_ref.shape[1] // PAIR):
        lanes = slice(pair * PAIR, (pair + 1) * PAIR)
        do, q, k, v = do_ref[:, lanes], q_ref[:, lanes], k_ref[:, lanes], v_ref[:, lanes]
        do_t, q_t = do.T, q.T
        dq, dk_t, dv_t = [], [], []
        for h in range(2):
            p = p_ref[2 * pair + h]
            dp = dot_nt(jnp.where(masks[h], do, jnp.zeros_like(do)), v)
            pf = p.astype(F32)
            ds = (pf * (dp - jnp.sum(dp * pf, -1, keepdims=True))).astype(BF)
            dq.append(jnp.dot(ds, k, preferred_element_type=F32))
            part = slice(h * half, (h + 1) * half)
            dk_t.append(jnp.dot(q_t[part], ds, preferred_element_type=F32))
            dv_t.append(jnp.dot(do_t[part], p, preferred_element_type=F32))
        dq_ref[:, lanes] = (jnp.where(masks[0], dq[0], dq[1]) * scale).astype(BF)
        dk_ref[:, lanes] = (jnp.concatenate(dk_t, 0) * scale).astype(BF).T
        dv_ref[:, lanes] = jnp.concatenate(dv_t, 0).astype(BF).T


def attend_back(do, q, k, v, p, batch, group=4):
    rows, keys, d = q.shape[0] // batch, k.shape[0] // batch, q.shape[1]
    wide = group * d // H
    spec = lambda n: pl.BlockSpec((n, wide), lambda b, g: (b, g))
    return pl.pallas_call(
        partial(attend_back_kernel, (d // H) ** -0.5),
        grid=(batch, H // group),
        in_specs=[
            spec(rows), spec(rows), spec(keys), spec(keys),
            pl.BlockSpec((None, group, rows, keys), lambda b, g: (b, g, 0, 0)),
        ],
        out_specs=[spec(rows), spec(keys), spec(keys)],
        out_shape=[
            jax.ShapeDtypeStruct(q.shape, BF),
            jax.ShapeDtypeStruct(k.shape, BF),
            jax.ShapeDtypeStruct(v.shape, BF),
        ],
        compiler_params=pltpu.CompilerParams(vmem_limit_bytes=40 * 2**20),
        cost_estimate=pl.CostEstimate(
            flops=32 * q.size * keys,
            transcendentals=0,
            bytes_accessed=6 * q.size + 8 * k.size + 2 * batch * H * rows * keys,
        ),
        name="attend_back",
    )(do, q, k, v, p)


def product(left, right):
    return jnp.dot(left, right, preferred_element_type=F32)


def product_nt(left, right):
    return lax.dot_general(
        left, right, (((1,), (1,)), ((), ())), preferred_element_type=F32
    )


def moments(values):
    average = jnp.mean(values, -1, keepdims=True)
    centered = values - average
    variance = jnp.mean(centered * centered, -1, keepdims=True)
    inverse = lax.rsqrt(variance + EPSILON)
    return (centered * inverse, inverse)


def norm_back(grad_out, normed, inverse, gain_vec):
    gain_grad = jnp.sum(grad_out * normed, 0)
    shift_grad = jnp.sum(grad_out, 0)
    scaled = grad_out * gain_vec
    mean_one = jnp.mean(scaled, -1, keepdims=True)
    mean_two = jnp.mean(scaled * normed, -1, keepdims=True)
    return (inverse * (scaled - mean_one - normed * mean_two), gain_grad, shift_grad)


def gelu_both(u):
    cdf = 0.5 * (1.0 + lax.erf(u * np.float32(0.5**0.5)))
    pdf = jnp.exp(-0.5 * u * u) * np.float32((2 * np.pi) ** -0.5)
    return (u * cdf).astype(BF), (cdf + u * pdf).astype(BF)


def body(
    groups,
    rows,
    decoder_input,
    encoder_out,
    prefix_length,
    output_grad,
    self_query,
    self_key,
    self_value,
    self_output,
    selfquery_bias,
    selfvalue_bias,
    self_attention_output_bias,
    cross_query,
    cross_key,
    cross_value,
    cross_output,
    crossquery_bias,
    crossvalue_bias,
    crossoutput_bias,
    expand_weight,
    expand_bias,
    down_projection_weight,
    reduce_bias,
    selfnorm_gain,
    selfnorm_bias,
    crossnorm_gain,
    crossnorm_bias,
    finalnorm_gain,
    finalnorm_bias,
):
    place = Place(groups, rows)
    batch, seq, d = decoder_input.shape
    m = self_query.shape[0]
    ff = expand_weight.shape[1]
    fl = ff // rows // 2
    k4 = ff // d

    small = [
        selfnorm_gain, selfnorm_bias, selfquery_bias, selfvalue_bias, self_attention_output_bias,
        crossnorm_gain, crossnorm_bias, crossquery_bias, crossvalue_bias, crossoutput_bias,
        finalnorm_gain, finalnorm_bias, reduce_bias,
    ]
    packed = jnp.concatenate([jnp.stack(small), expand_bias.reshape(k4, m)])
    vecs = gather_vectors(place, packed).astype(F32)
    (g1, b1, bq, bv, bo, g2, b2, bcq, bcv, bco, g3, b3, br) = [
        vecs[:, i].reshape(d) for i in range(13)
    ]
    be = vecs[:, 13:].reshape(rows, 2, fl)

    expand_halves = [
        expand_weight.reshape(m, rows, 2, fl)[:, :, h].reshape(m, rows * fl) for h in range(2)
    ]
    down_halves = [down_projection_weight[h * fl : (h + 1) * fl] for h in range(2)]

    lane, ring_lane = Lane(4), Lane(2)
    gathers = [
        Gather(place, lane, ring_lane, shard, split)
        for shard, split in (
            (jnp.concatenate([self_query, self_key], 1), True),
            (self_value, False),
            (jnp.concatenate([cross_key, cross_value], 1), True),
            (self_output, False),
            (jnp.concatenate([cross_query, cross_output], 1), True),
            (expand_halves[0], True),
            (expand_halves[1], True),
            (down_halves[0], False),
            (down_halves[1], True),
        )
    ]
    run_steps(gathers)
    w_qk, w_v, w_ckv, w_o, w_cqo, *w_ff = [u.v for u in gathers]
    w_e, w_d = w_ff[:2], w_ff[2:]

    x = decoder_input.reshape(batch * seq, d).astype(F32)
    e = encoder_out.reshape(-1, d)
    dy = output_grad.reshape(batch * seq, d)

    n1, i1 = moments(x)
    act1 = (n1 * g1 + b1).astype(BF)
    qk = product(act1, w_qk)
    q = (qk[:, :d] + bq).astype(BF)
    k = qk[:, d:].astype(BF)
    v = (product(act1, w_v) + bv).astype(BF)
    o, p = attend(q, k, v, prefix_length, batch, True)
    mid1 = x + (product(o, w_o) + bo)
    n2, i2 = moments(mid1)
    act2 = (n2 * g2 + b2).astype(BF)
    w_cq, w_co = w_cqo[:, :d], w_cqo[:, d:]
    cq = (product(act2, w_cq) + bcq).astype(BF)
    ckv = product(e, w_ckv)
    ck = ckv[:, :d].astype(BF)
    cv = (ckv[:, d:] + bcv).astype(BF)
    co, cp = attend(cq, ck, cv, prefix_length, batch, False)
    mid2 = mid1 + (product(co, w_co) + bco)
    n3, i3 = moments(mid2)
    act3 = (n3 * g3 + b3).astype(BF)
    hidden, slope = [], []
    for h in range(2):
        hid, slo = gelu_both(product(act3, w_e[h]) + be[:, h].reshape(-1))
        hidden.append(hid)
        slope.append(slo)
    layer_out = (mid2 + (product(hidden[0], w_d[0]) + product(hidden[1], w_d[1]) + br)).astype(BF)

    scatter = partial(Scatter, place, lane, ring_lane)
    dyf = dy.astype(F32)
    g_down = [scatter(hidden[0], dy, True), scatter(hidden[1], dy, False)]
    dexp = [(product_nt(dy, w_d[h]) * slope[h].astype(F32)).astype(BF) for h in range(2)]
    g_exp = [scatter(act3, dexp[0], True), scatter(act3, dexp[1], False)]
    dact3 = product_nt(dexp[0], w_e[0]) + product_nt(dexp[1], w_e[1])
    dn, gg3, gb3 = norm_back(dact3, n3, i3, g3)
    dmid2 = dyf + dn
    dcross = dmid2.astype(BF)
    g_co = scatter(co, dcross, True)
    dco = product_nt(dcross, w_co).astype(BF)
    dcq, dck, dcv = attend_back(dco, cq, ck, cv, cp, batch)
    g_ck = scatter(e, dck, True)
    g_cv = scatter(e, dcv, False)
    g_cq = scatter(act2, dcq, False)
    encoder_grad = product_nt(jnp.concatenate([dck, dcv], 1), w_ckv)
    dn, gg2, gb2 = norm_back(product_nt(dcq, w_cq), n2, i2, g2)
    dmid1 = dmid2 + dn
    dself = dmid1.astype(BF)
    g_so = scatter(o, dself, True)
    dao = product_nt(dself, w_o).astype(BF)
    dq, dk, dv = attend_back(dao, q, k, v, p, batch)
    g_sv = scatter(act1, dv, False)
    g_sq = scatter(act1, dq, True)
    g_sk = scatter(act1, dk, True)
    dact1 = product_nt(jnp.concatenate([dq, dk], 1), w_qk) + product_nt(dv, w_v)
    dn, gg1, gb1 = norm_back(dact1, n1, i1, g1)
    input_grad = dmid1 + dn

    def column_sum(t):
        return jnp.sum(t.astype(F32), 0)

    dbe = jnp.stack([column_sum(t).reshape(rows, fl) for t in dexp], 1).reshape(rows, k4, m)
    early = [
        gg2, gb2, column_sum(dcq), column_sum(dcv), column_sum(dcross),
        gg3, gb3, column_sum(dy), column_sum(dself),
    ]
    early = jnp.concatenate([jnp.stack([t.reshape(rows, m) for t in early], 1), dbe], 1)
    late = [gg1, gb1, column_sum(dq), column_sum(dv)]
    late = jnp.stack([t.reshape(rows, m) for t in late], 1)

    first = g_down + g_exp + [g_co, g_cv, g_ck, g_cq, g_so]
    second = [g_sv, g_sq, g_sk]
    run_steps(first + second)
    early = scatter_vectors(place, lane, ring_lane, early)
    (*g_ff, g_co, g_cv, g_ck, g_cq, g_so) = finish(place, lane, first)
    g_down, g_exp = g_ff[:2], g_ff[2:]
    late = scatter_vectors(place, lane, ring_lane, late)
    g_sv, g_sq, g_sk = finish(place, lane, second)

    g_exp = jnp.stack([t.reshape(m, rows, fl) for t in g_exp], 2).reshape(m, ff)
    g_down = jnp.concatenate(g_down, 0)
    return (
        layer_out.reshape(batch, seq, d),
        input_grad.reshape(batch, seq, d),
        encoder_grad.reshape(encoder_out.shape),
        g_sq, g_sk, g_sv, g_so,
        late[2], late[3], early[8],
        g_cq, g_ck, g_cv, g_co,
        early[2], early[3], early[4],
        g_exp, early[9:].reshape(-1), g_down, early[7],
        late[0], late[1], early[0], early[1], early[5], early[6],
    )


def solution(mesh):
    groups, rows = mesh.shape["replica"], mesh.shape["fsdp"]
    data = P(("replica", "fsdp"), None, None)
    mat, vec = P("fsdp", None), P("fsdp")
    weights = (
        (mat,) * 4 + (vec,) * 3 + (mat,) * 4 + (vec,) * 3 + (mat, vec, mat, vec) + (vec,) * 6
    )
    return jax.shard_map(
        partial(body, groups, rows),
        mesh=mesh,
        in_specs=(data, data, P(("replica", "fsdp")), data) + weights,
        out_specs=(data, data, data) + weights,
        check_vma=False,
    )
```

```python
from functools import partial

import jax
import jax.numpy as jnp
import numpy as np
from jax import lax
from jax.experimental import pallas as pl
from jax.experimental.pallas import tpu as pltpu
from jax.sharding import PartitionSpec as P

H = 16
EPSILON = 1e-05
MASKED = -1e30
BF = jnp.bfloat16
F32 = jnp.float32


class Place:
    def __init__(self, groups, rows):
        self.groups = groups
        self.rows = rows
        self.ring = rows // 2
        rep = lax.axis_index("replica")
        row = lax.axis_index("fsdp")
        self.c = lax.rem(rep, 2)
        self.x = lax.div(rep, 2)
        self.y = lax.rem(row, 2)
        self.z = lax.div(row, 2)

    def core(self, v):
        return lax.ppermute(v, "replica", [(i, i ^ 1) for i in range(self.groups)])

    def across(self, v):
        return lax.ppermute(v, "replica", [(i, i ^ 2) for i in range(self.groups)])

    def pair(self, v):
        return lax.ppermute(v, "fsdp", [(i, i ^ 1) for i in range(self.rows)])

    def next(self, v):
        return lax.ppermute(v, "fsdp", [(i, (i + 2) % self.rows) for i in range(self.rows)])

    def ring_members(self):
        return [[2 * k + side for k in range(self.ring)] for side in range(2)]


def at(v, i, axis=0):
    return lax.dynamic_index_in_dim(v, i, axis, keepdims=False)


class Lane:
    def __init__(self, width):
        self.width = width
        self.past = []

    def __call__(self, send, v):
        if len(self.past) >= self.width:
            v, _ = lax.optimization_barrier((v, self.past[-self.width]))
        got = send(v)
        self.past.append(got)
        return got


def ring_gather(place, piece):
    if place.ring <= 4:
        copies = jnp.broadcast_to(piece[None], (place.ring,) + piece.shape)
        return lax.all_to_all(copies, "fsdp", 0, 0, axis_index_groups=place.ring_members())
    return lax.all_gather(piece, "fsdp", axis_index_groups=place.ring_members())


def order_kernel(ring, split, mine, theirs, out, sems):
    rep = lax.axis_index("replica")
    c, x = lax.rem(rep, 2), lax.div(rep, 2)
    y = lax.rem(lax.axis_index("fsdp"), 2)
    copies = []
    for dc, block in enumerate((mine, theirs)):
        cc = 1 - c if dc else c
        for dx in range(2 if split else 1):
            for dy in range(2):
                yy = 1 - y if dy else y
                for z in range(ring):
                    if split:
                        xx = 1 - x if dx else x
                        src, dst = block.at[dx, dy, z], out.at[z, yy, xx, cc]
                    else:
                        src, dst = block.at[dy, z], out.at[z, yy, cc]
                    copies.append(pltpu.make_async_copy(src, dst, sems.at[len(copies)]))
    for copy in copies:
        copy.start()
    for copy in copies:
        copy.wait()


def in_order(place, split, mine, theirs):
    ring, rows, n = mine.shape[-3:]
    dims = (ring, 2, 2, 2) if split else (ring, 2, 2)
    if rows % 16 == 0:
        count = 2 * mine.size // (rows * n)
        out = pl.pallas_call(
            partial(order_kernel, ring, split),
            out_shape=jax.ShapeDtypeStruct(dims + (rows, n), mine.dtype),
            in_specs=[pl.BlockSpec(memory_space=pl.ANY)] * 2,
            out_specs=pl.BlockSpec(memory_space=pltpu.VMEM),
            scratch_shapes=[pltpu.SemaphoreType.DMA((count,))],
            cost_estimate=pl.CostEstimate(
                flops=0, transcendentals=0, bytes_accessed=4 * count * rows * n
            ),
            name="order",
        )(mine, theirs)
    else:
        both = jnp.stack([mine, theirs])
        at_c = (place.c, 1 - place.c)
        both = jnp.stack([at(both, i, 0) for i in at_c])
        if split:
            both = jnp.stack([at(both, i, 1) for i in (place.x, 1 - place.x)], 1)
        both = jnp.stack([at(both, i, both.ndim - 4) for i in (place.y, 1 - place.y)], both.ndim - 4)
        out = jnp.transpose(both, (3, 2, 1, 0, 4, 5) if split else (2, 1, 0, 3, 4))
    return out.reshape(-1, n)


class Gather:
    def __init__(self, place, lane, ring_lane, shard, split):
        self.place, self.lane, self.ring_lane, self.split = place, lane, ring_lane, split
        m, n = shard.shape
        if split:
            self.v = at(shard.reshape(4, m // 4, n), 2 * place.x + place.c)
        else:
            self.v = at(shard.reshape(2, m // 2, n), place.c)
        self.steps = [self.ring, self.pair] + ([self.across] if split else []) + [self.core]

    def ring(self):
        self.v = self.ring_lane(partial(ring_gather, self.place), self.v)

    def pair(self):
        self.v = jnp.stack([self.v, self.lane(self.place.pair, self.v)])

    def across(self):
        self.v = jnp.stack([self.v, self.lane(self.place.across, self.v)])

    def core(self):
        self.v = in_order(self.place, self.split, self.v, self.lane(self.place.core, self.v))


def run_steps(units):
    last = max(i + len(u.steps) for i, u in enumerate(units))
    for t in range(last):
        for i, u in enumerate(units):
            if 0 <= t - i < len(u.steps):
                u.steps[t - i]()


def gather_vectors(place, packed):
    a = ring_gather(place, packed)
    b = place.pair(a)
    both = jnp.stack([jnp.where(place.y == 0, a, b), jnp.where(place.y == 0, b, a)], 1)
    return both.reshape((place.rows,) + packed.shape)


def product_t(left, right):
    return lax.dot_general(
        left, right, (((0,), (0,)), ((), ())), preferred_element_type=F32
    )


def columns(v, k, i):
    w = v.shape[1] // k
    return lax.dynamic_slice(v, (0, i * w), (v.shape[0], w))


def join2(own, other, bit):
    first = jnp.where(bit == 0, own, other)
    second = jnp.where(bit == 0, other, own)
    return jnp.concatenate([first, second], -1)


def ring_sum(place, parts):
    if place.ring <= 4:
        came = lax.all_to_all(parts, "fsdp", 0, 0, axis_index_groups=place.ring_members())
        return jnp.sum(came.astype(F32), 0).astype(BF)
    return lax.psum_scatter(
        parts, "fsdp", scatter_dimension=0, axis_index_groups=place.ring_members()
    )


class Scatter:
    def __init__(self, place, lane, ring_lane, left, right, split):
        self.place, self.lane, self.ring_lane, self.split = place, lane, ring_lane, split
        self.left, self.right = left, right
        self.steps = [self.core] + ([self.across] if split else []) + [self.pair, self.ring]

    def core(self):
        c = self.place.c
        away = product_t(self.left, columns(self.right, 2, 1 - c)).astype(BF)
        self.right = columns(self.right, 2, c)
        self.came = self.lane(self.place.core, away)

    def across(self):
        x = self.place.x
        away = product_t(self.left, columns(self.right, 2, 1 - x))
        away = (away + columns(self.came, 2, 1 - x).astype(F32)).astype(BF)
        self.right, self.came = columns(self.right, 2, x), columns(self.came, 2, x)
        self.came_x = self.lane(self.place.across, away)

    def pair(self):
        part = product_t(self.left, self.right) + self.came.astype(F32)
        if self.split:
            part = part + self.came_x.astype(F32)
        part = part.astype(BF)
        part = part.reshape(self.place.ring, 2, -1, part.shape[1])
        y = self.place.y
        came = self.lane(self.place.pair, at(part, 1 - y, 1))
        self.kept = (at(part, y, 1).astype(F32) + came.astype(F32)).astype(BF)

    def ring(self):
        self.own = self.ring_lane(partial(ring_sum, self.place), self.kept)


def finish_all(place, lane, units):
    flat = [u.own.reshape(-1, 128) for u in units]
    sizes = [f.shape[0] for f in flat]
    own = jnp.concatenate(flat)
    came = lane(place.across, own)
    pieces, at_row = [], 0
    for u, size in zip(units, sizes):
        mine, other = own[at_row : at_row + size], came[at_row : at_row + size]
        at_row += size
        mine, other = mine.reshape(u.own.shape), other.reshape(u.own.shape)
        if u.split:
            pieces.append(join2(mine, other, place.x))
        else:
            pieces.append((mine.astype(F32) + other.astype(F32)).astype(BF))
    own = jnp.concatenate([p.reshape(-1, 128) for p in pieces])
    came = lane(place.core, own)
    out, at_row = [], 0
    for p in pieces:
        size = p.size // 128
        out.append(join2(p, came[at_row : at_row + size].reshape(p.shape), place.c).astype(F32))
        at_row += size
    return out


def scatter_vectors(place, lane, ring_lane, v):
    own = v.astype(BF)
    own = (own.astype(F32) + lane(place.core, own).astype(F32)).astype(BF)
    own = (own.astype(F32) + lane(place.across, own).astype(F32)).astype(BF)
    own = own.reshape((place.ring, 2) + own.shape[1:])
    came = lane(place.pair, at(own, 1 - place.y, 1))
    own = (at(own, place.y, 1).astype(F32) + came.astype(F32)).astype(BF)
    return ring_lane(partial(ring_sum, place), own).astype(F32)


PAIR = 128


def half_masks(rows):
    lane = lax.broadcasted_iota(jnp.int32, (rows, PAIR), 1)
    return (lane < PAIR // 2, lane >= PAIR // 2)


def dot_nt(a, b):
    return lax.dot_general(a, b, (((1,), (1,)), ((), ())), preferred_element_type=F32)


def attend_kernel(masked, scale, prefix_ref, q_ref, k_ref, v_ref, o_ref, p_ref):
    rows, keys = q_ref.shape[0], k_ref.shape[0]
    masks = half_masks(rows)
    if masked:
        i = lax.broadcasted_iota(jnp.int32, (rows, keys), 0)
        j = lax.broadcasted_iota(jnp.int32, (rows, keys), 1)
        allowed = (j <= i) | (j < prefix_ref[pl.program_id(0)])
    for pair in range(q_ref.shape[1] // PAIR):
        lanes = slice(pair * PAIR, (pair + 1) * PAIR)
        q, k, v = q_ref[:, lanes], k_ref[:, lanes], v_ref[:, lanes]
        both = []
        for h in range(2):
            s = dot_nt(jnp.where(masks[h], q, jnp.zeros_like(q)), k)
            if masked:
                s = jnp.where(allowed, s, MASKED)
            e = jnp.exp((s - jnp.max(s, -1, keepdims=True)) * scale)
            p = (e * (1.0 / jnp.sum(e, -1, keepdims=True))).astype(BF)
            p_ref[2 * pair + h] = p
            both.append(jnp.dot(p, v, preferred_element_type=F32))
        o_ref[:, lanes] = jnp.where(masks[0], both[0], both[1]).astype(BF)


def attend(q, k, v, prefix, batch, masked, group=4):
    rows, keys, d = q.shape[0] // batch, k.shape[0] // batch, q.shape[1]
    wide = group * d // H
    spec = lambda n: pl.BlockSpec((n, wide), lambda b, g, *_: (b, g))
    return pl.pallas_call(
        partial(attend_kernel, masked, (d // H) ** -0.5),
        grid_spec=pltpu.PrefetchScalarGridSpec(
            num_scalar_prefetch=1,
            grid=(batch, H // group),
            in_specs=[spec(rows), spec(keys), spec(keys)],
            out_specs=[
                spec(rows),
                pl.BlockSpec((None, group, rows, keys), lambda b, g, *_: (b, g, 0, 0)),
            ],
        ),
        out_shape=[
            jax.ShapeDtypeStruct(q.shape, BF),
            jax.ShapeDtypeStruct((batch, H, rows, keys), BF),
        ],
        compiler_params=pltpu.CompilerParams(vmem_limit_bytes=40 * 2**20),
        cost_estimate=pl.CostEstimate(
            flops=16 * q.size * keys,
            transcendentals=batch * H * rows * keys,
            bytes_accessed=4 * q.size + 4 * k.size + 2 * batch * H * rows * keys,
        ),
        name="attend",
    )(prefix, q, k, v)


def attend_back_kernel(scale, do_ref, q_ref, k_ref, v_ref, p_ref, dq_ref, dk_ref, dv_ref):
    rows = q_ref.shape[0]
    half = PAIR // 2
    masks = half_masks(rows)
    for pair in range(q_ref.shape[1] // PAIR):
        lanes = slice(pair * PAIR, (pair + 1) * PAIR)
        do, q, k, v = do_ref[:, lanes], q_ref[:, lanes], k_ref[:, lanes], v_ref[:, lanes]
        do_t, q_t = do.T, q.T
        dq, dk_t, dv_t = [], [], []
        for h in range(2):
            p = p_ref[2 * pair + h]
            dp = dot_nt(jnp.where(masks[h], do, jnp.zeros_like(do)), v)
            pf = p.astype(F32)
            ds = (pf * (dp - jnp.sum(dp * pf, -1, keepdims=True))).astype(BF)
            dq.append(jnp.dot(ds, k, preferred_element_type=F32))
            part = slice(h * half, (h + 1) * half)
            dk_t.append(jnp.dot(q_t[part], ds, preferred_element_type=F32))
            dv_t.append(jnp.dot(do_t[part], p, preferred_element_type=F32))
        dq_ref[:, lanes] = (jnp.where(masks[0], dq[0], dq[1]) * scale).astype(BF)
        dk_ref[:, lanes] = (jnp.concatenate(dk_t, 0) * scale).astype(BF).T
        dv_ref[:, lanes] = jnp.concatenate(dv_t, 0).astype(BF).T


def attend_back(do, q, k, v, p, batch, group=4):
    rows, keys, d = q.shape[0] // batch, k.shape[0] // batch, q.shape[1]
    wide = group * d // H
    spec = lambda n: pl.BlockSpec((n, wide), lambda b, g: (b, g))
    return pl.pallas_call(
        partial(attend_back_kernel, (d // H) ** -0.5),
        grid=(batch, H // group),
        in_specs=[
            spec(rows), spec(rows), spec(keys), spec(keys),
            pl.BlockSpec((None, group, rows, keys), lambda b, g: (b, g, 0, 0)),
        ],
        out_specs=[spec(rows), spec(keys), spec(keys)],
        out_shape=[
            jax.ShapeDtypeStruct(q.shape, BF),
            jax.ShapeDtypeStruct(k.shape, BF),
            jax.ShapeDtypeStruct(v.shape, BF),
        ],
        compiler_params=pltpu.CompilerParams(vmem_limit_bytes=40 * 2**20),
        cost_estimate=pl.CostEstimate(
            flops=32 * q.size * keys,
            transcendentals=0,
            bytes_accessed=6 * q.size + 8 * k.size + 2 * batch * H * rows * keys,
        ),
        name="attend_back",
    )(do, q, k, v, p)


BIG = pltpu.CompilerParams(vmem_limit_bytes=58 * 2**20)
SPOT = pl.BlockSpec(memory_space=pl.ANY)
WHOLE = pl.BlockSpec(memory_space=pltpu.VMEM)
CHUNK = 128


def here():
    rep, row = lax.axis_index("replica"), lax.axis_index("fsdp")
    return lax.div(rep, 2), lax.rem(rep, 2), lax.div(row, 2), lax.rem(row, 2)


def flip(bit, by):
    return 1 - bit if by else bit


def pieces_of(refs, number, w, sems, act):
    x, c, _, y = here()
    rows, half = w.shape[2], w.shape[3] // 2
    dx, dc = flip(x, number // 2), flip(c, number % 2)

    def copy(ref, i, dy, g):
        src, to = ref.at[i, :, pl.ds(0, rows)], w.at[:, flip(y, dy), :, pl.ds(g * half, half)]
        getattr(pltpu.make_async_copy(src, to, sems.at[2 * dy + g]), act)()

    if act == "wait":
        for dy in range(2):
            for g in range(2):
                copy(refs[0], 0, dy, g)
        return
    for far in range(2):
        p0, q0, p1, q1 = refs[4 * far : 4 * far + 4]

        @pl.when(dc == far)
        def _(p1=p1, q1=q1):
            copy(p1, dx, 0, 1)
            copy(q1, dx, 1, 1)

        for ref, side in ((p0, 0), (q0, 1)):

            @pl.when((dc == far) & (dx == side))
            def _(ref=ref):
                copy(ref, 0, 0, 0)
                copy(ref, 1, 1, 0)


def row_sum(v):
    return jnp.sum(v, 0, keepdims=True)


def normal(v):
    centered = v - jnp.mean(v, -1, keepdims=True)
    inverse = lax.rsqrt(jnp.mean(centered * centered, -1, keepdims=True) + EPSILON)
    return centered * inverse, inverse


def chunks(rows, step, do):
    def one(i, carry):
        do(pl.ds(pl.multiple_of(i * step, step), step))
        return carry

    lax.fori_loop(0, rows // step, one, 0)


def weight(w_ref, *lead):
    v = w_ref[lead] if lead else w_ref[...]
    return v.reshape(v.shape[-4] * v.shape[-3] * v.shape[-2], v.shape[-1])


def times(a_ref, w_ref, put, tile=256):
    def one(i, carry):
        lanes = pl.ds(pl.multiple_of(i * tile, tile), tile)
        w = w_ref[:, :, :, lanes]
        w = w.reshape(w.shape[0] * w.shape[1] * w.shape[2], tile)
        put(lanes, jnp.dot(a_ref[...], w, preferred_element_type=F32))
        return carry

    lax.fori_loop(0, w_ref.shape[3] // tile, one, 0)


def times_t(pairs, put):
    wide = pairs[0][1].shape[1] * pairs[0][1].shape[2]

    def one(i, carry):
        total = None
        for a_ref, w_ref in pairs:
            w = w_ref[i].reshape(wide, w_ref.shape[3])
            part = dot_nt(a_ref[...], w)
            total = part if total is None else total + part
        put(pl.ds(pl.multiple_of(i * wide, wide), wide), total)
        return carry

    lax.fori_loop(0, pairs[0][1].shape[0], one, 0)


def loaded(m, n, count):
    return [pltpu.VMEM((4, 2, m, n), BF)] * count + [pltpu.SemaphoreType.DMA((count, 4))]


def cost(flops, *arrays):
    return pl.CostEstimate(
        flops=flops,
        transcendentals=0,
        bytes_accessed=sum(a.size * a.dtype.itemsize for a in arrays),
    )


def shape(dims, dtype):
    return jax.ShapeDtypeStruct(dims, dtype)


def first_kernel(x_ref, vec_ref, *rest):
    refs, (act_ref, q_ref, k_ref, v_ref), (wq, wk, wv, sems) = rest[:8], rest[8:12], rest[12:]
    for i, w in enumerate((wq, wk, wv)):
        pieces_of(refs, i, w, sems.at[i], "start")

    def norm(rows):
        n, _ = normal(x_ref[rows, :].astype(F32))
        act_ref[rows, :] = (n * vec_ref[0:1] + vec_ref[1:2]).astype(BF)

    chunks(x_ref.shape[0], CHUNK, norm)
    for i, (w, out, bias) in enumerate(((wq, q_ref, 2), (wk, k_ref, None), (wv, v_ref, 3))):
        pieces_of(refs, i, w, sems.at[i], "wait")

        def put(lanes, v, out=out, bias=bias):
            if bias is not None:
                v = v + vec_ref[bias : bias + 1, lanes]
            out[:, lanes] = v.astype(BF)

        times(act_ref, w, put)


def first(x, vecs, unit, m):
    like = shape(x.shape, BF)
    return pl.pallas_call(
        first_kernel,
        in_specs=[WHOLE, WHOLE] + [SPOT] * 8,
        out_specs=[WHOLE] * 4,
        out_shape=[like] * 4,
        scratch_shapes=loaded(m, x.shape[1], 3),
        compiler_params=BIG,
        cost_estimate=cost(6 * x.size * x.shape[1], x, x, x, x, x, *unit),
        name="first",
    )(x, vecs, *unit)


def project_kernel(second, numbers, rows_of, a_ref, res_ref, vec_ref, *rest):
    refs = rest[:16] if second else rest[:8]
    rest = rest[len(refs) :]
    outs, (w1, *rest) = rest[: 3 if second else 2], rest[3 if second else 2 :]
    mid_ref, act_ref = outs[:2]
    sems = rest[-1]
    bias, gain, shift, bias2 = rows_of
    pieces_of(refs[:8], numbers[0], w1, sems.at[0], "start")
    if second:
        w2 = rest[0]
        pieces_of(refs[8:], numbers[1], w2, sems.at[1], "start")
    pieces_of(refs[:8], numbers[0], w1, sems.at[0], "wait")

    def put(lanes, v):
        mid_ref[:, lanes] = res_ref[:, lanes].astype(F32) + (v + vec_ref[bias : bias + 1, lanes])

    times(a_ref, w1, put)

    def norm(rows):
        n, _ = normal(mid_ref[rows, :])
        act_ref[rows, :] = (n * vec_ref[gain : gain + 1] + vec_ref[shift : shift + 1]).astype(BF)

    chunks(a_ref.shape[0], CHUNK, norm)
    if second:
        pieces_of(refs[8:], numbers[1], w2, sems.at[1], "wait")

        def put2(lanes, v):
            outs[2][:, lanes] = (v + vec_ref[bias2 : bias2 + 1, lanes]).astype(BF)

        times(act_ref, w2, put2)


def project(a, residual, vecs, rows_of, units, numbers, m, name):
    second = len(units) == 2
    refs = [r for u in units for r in u]
    return pl.pallas_call(
        partial(project_kernel, second, numbers, rows_of),
        in_specs=[WHOLE] * 3 + [SPOT] * len(refs),
        out_specs=[WHOLE] * (3 if second else 2),
        out_shape=[shape(a.shape, F32), shape(a.shape, BF)] + ([shape(a.shape, BF)] if second else []),
        scratch_shapes=loaded(m, a.shape[1], len(units)),
        compiler_params=BIG,
        cost_estimate=cost(2 * len(units) * a.size * a.shape[1], a, a, a, a, a, a, *refs[:4]),
        name=name,
    )(a, residual, vecs, *refs)


def query_kernel(bias, a_ref, vec_ref, *rest):
    refs, out_ref, (w, sems) = rest[:8], rest[8], rest[9:]
    pieces_of(refs, 0, w, sems.at[0], "start")
    pieces_of(refs, 0, w, sems.at[0], "wait")

    def put(lanes, v):
        out_ref[:, lanes] = (v + vec_ref[bias : bias + 1, lanes]).astype(BF)

    times(a_ref, w, put)


def query(a, vecs, bias, unit, m):
    return pl.pallas_call(
        partial(query_kernel, bias),
        in_specs=[WHOLE] * 2 + [SPOT] * 8,
        out_specs=WHOLE,
        out_shape=shape(a.shape, BF),
        scratch_shapes=loaded(m, a.shape[1], 1),
        compiler_params=BIG,
        cost_estimate=cost(2 * a.size * a.shape[1], a, a, *unit[:2]),
        name="query",
    )(a, vecs, *unit)


def memory_kernel(e_ref, vec_ref, *rest):
    refs, (k_ref, v_ref), (wk, wv, sems) = rest[:8], rest[8:10], rest[10:]

    @pl.when(pl.program_id(0) == 0)
    def _():
        for i, w in enumerate((wk, wv)):
            pieces_of(refs, i + 1, w, sems.at[i], "start")
        for i, w in enumerate((wk, wv)):
            pieces_of(refs, i + 1, w, sems.at[i], "wait")

    def put_k(lanes, v):
        k_ref[:, lanes] = v.astype(BF)

    def put_v(lanes, v):
        v_ref[:, lanes] = (v + vec_ref[8:9, lanes]).astype(BF)

    times(e_ref, wk, put_k)
    times(e_ref, wv, put_v)


def memory(e, vecs, unit, m, step=512):
    d = e.shape[1]
    blk = pl.BlockSpec((step, d), lambda i: (i, 0))
    return pl.pallas_call(
        memory_kernel,
        grid=(e.shape[0] // step,),
        in_specs=[blk, pl.BlockSpec(vecs.shape, lambda i: (0, 0))] + [SPOT] * 8,
        out_specs=[blk, blk],
        out_shape=[shape(e.shape, BF)] * 2,
        scratch_shapes=loaded(m, d, 2),
        compiler_params=BIG,
        cost_estimate=cost(4 * e.size * d, e, e, e, *unit),
        name="memory",
    )(e, vecs, *unit)


def memory_back_kernel(dk_ref, dv_ref, *rest):
    refs, (out_ref, sum_ref), (wk, wv, sems) = rest[:8], rest[8:10], rest[10:]

    @pl.when(pl.program_id(0) == 0)
    def _():
        for i, w in enumerate((wk, wv)):
            pieces_of(refs, i + 1, w, sems.at[i], "start")
        sum_ref[...] = jnp.zeros_like(sum_ref)
        for i, w in enumerate((wk, wv)):
            pieces_of(refs, i + 1, w, sems.at[i], "wait")

    def put(lanes, v):
        out_ref[:, lanes] = v

    times_t([(dk_ref, wk), (dv_ref, wv)], put)
    sum_ref[0:1] += row_sum(dv_ref[...].astype(F32))


def memory_back(dk, dv, unit, m, step=512):
    d = dk.shape[1]
    blk = pl.BlockSpec((step, d), lambda i: (i, 0))
    return pl.pallas_call(
        memory_back_kernel,
        grid=(dk.shape[0] // step,),
        in_specs=[blk, blk] + [SPOT] * 8,
        out_specs=[blk, pl.BlockSpec((8, d), lambda i: (0, 0))],
        out_shape=[shape(dk.shape, F32), shape((8, d), F32)],
        scratch_shapes=loaded(m, d, 2),
        compiler_params=BIG,
        cost_estimate=cost(4 * dk.size * d, dk, dk, dk, dk, *unit),
        name="memory_back",
    )(dk, dv, *unit)


def apply_norm_back(rows, dact, v, gain, residual, sums):
    n, inverse = normal(v)
    sums[0:1] += row_sum(dact * n)
    sums[1:2] += row_sum(dact)
    q = dact * gain
    mean_one = jnp.mean(q, -1, keepdims=True)
    mean_two = jnp.mean(q * n, -1, keepdims=True)
    return residual + inverse * (q - mean_one - n * mean_two)


def cross_back_kernel(dq_ref, mid_ref, dmid_ref, vec_ref, *rest):
    refs, (out_ref, low_ref, do_ref, sum_ref), (dact, w1, w2, sems) = rest[:16], rest[16:20], rest[20:]
    pieces_of(refs[:8], 0, w1, sems.at[0], "start")
    pieces_of(refs[8:], 3, w2, sems.at[1], "start")
    sum_ref[...] = jnp.zeros_like(sum_ref)
    sum_ref[2:3] = row_sum(dq_ref[...].astype(F32))
    pieces_of(refs[:8], 0, w1, sems.at[0], "wait")

    def put(lanes, v):
        dact[:, lanes] = v

    times_t([(dq_ref, w1)], put)

    def back(rows):
        total = apply_norm_back(
            rows, dact[rows, :], mid_ref[rows, :], vec_ref[5:6], dmid_ref[rows, :], sum_ref
        )
        out_ref[rows, :] = total
        low = total.astype(BF)
        low_ref[rows, :] = low
        sum_ref[3:4] += row_sum(low.astype(F32))

    chunks(dq_ref.shape[0], CHUNK, back)
    pieces_of(refs[8:], 3, w2, sems.at[1], "wait")

    def put2(lanes, v):
        do_ref[:, lanes] = v.astype(BF)

    times_t([(low_ref, w2)], put2)


def cross_back(dq, mid, dmid, vecs, cross_unit, self_unit, m):
    d = dq.shape[1]
    return pl.pallas_call(
        cross_back_kernel,
        in_specs=[WHOLE] * 4 + [SPOT] * 16,
        out_specs=[WHOLE] * 4,
        out_shape=[shape(dq.shape, F32), shape(dq.shape, BF), shape(dq.shape, BF), shape((8, d), F32)],
        scratch_shapes=[pltpu.VMEM(dq.shape, F32)] + loaded(m, d, 2),
        compiler_params=BIG,
        cost_estimate=cost(4 * dq.size * d, mid, mid, mid, dq, dq, dq, *cross_unit[:4]),
        name="cross_back",
    )(dq, mid, dmid, vecs, *cross_unit, *self_unit)


def self_back_kernel(dq_ref, dk_ref, dv_ref, x_ref, dmid_ref, vec_ref, *rest):
    refs, (out_ref, sum_ref), (dact, wq, wk, wv, sems) = rest[:8], rest[8:10], rest[10:]
    for i, w in enumerate((wq, wk, wv)):
        pieces_of(refs, i, w, sems.at[i], "start")
    sum_ref[...] = jnp.zeros_like(sum_ref)
    sum_ref[2:3] = row_sum(dq_ref[...].astype(F32))
    sum_ref[3:4] = row_sum(dv_ref[...].astype(F32))
    for i, w in enumerate((wq, wk, wv)):
        pieces_of(refs, i, w, sems.at[i], "wait")

    def put(lanes, v):
        dact[:, lanes] = v

    times_t([(dq_ref, wq), (dk_ref, wk), (dv_ref, wv)], put)

    def back(rows):
        out_ref[rows, :] = apply_norm_back(
            rows, dact[rows, :], x_ref[rows, :].astype(F32), vec_ref[0:1], dmid_ref[rows, :], sum_ref
        )

    chunks(dq_ref.shape[0], CHUNK, back)


def self_back(dq, dk, dv, x, dmid, vecs, unit, m):
    d = dq.shape[1]
    return pl.pallas_call(
        self_back_kernel,
        in_specs=[WHOLE] * 6 + [SPOT] * 8,
        out_specs=[WHOLE] * 2,
        out_shape=[shape(dq.shape, F32), shape((8, d), F32)],
        scratch_shapes=[pltpu.VMEM(dq.shape, F32)] + loaded(m, d, 3),
        compiler_params=BIG,
        cost_estimate=cost(6 * dq.size * d, dmid, dmid, dq, dq, dq, dq, *unit),
        name="self_back",
    )(dq, dk, dv, x, dmid, vecs, *unit)


def output_back_kernel(d_ref, *rest):
    refs, do_ref, (w, sems) = rest[:8], rest[8], rest[9:]
    pieces_of(refs, 3, w, sems.at[0], "start")
    pieces_of(refs, 3, w, sems.at[0], "wait")

    def put(lanes, v):
        do_ref[:, lanes] = v.astype(BF)

    times_t([(d_ref, w)], put)


def output_back(dlow, unit, m):
    d = dlow.shape[1]
    return pl.pallas_call(
        output_back_kernel,
        in_specs=[WHOLE] + [SPOT] * 8,
        out_specs=WHOLE,
        out_shape=shape(dlow.shape, BF),
        scratch_shapes=loaded(m, d, 1),
        compiler_params=BIG,
        cost_estimate=cost(2 * dlow.size * d, dlow, dlow, *unit[:2]),
        name="output_back",
    )(dlow, *unit)


def send_off(block, away, keep, dx, dc, spot, sem):
    @pl.when(dc == 1)
    def _():
        pltpu.make_async_copy(block, away.at[(dx,) + spot], sem).start()

    @pl.when(dc == 0)
    def _():
        pltpu.make_async_copy(block, keep.at[(dx,) + spot], sem).start()


def grads_kernel(sides, *rest):
    lefts = sorted({l for l, _ in sides})
    n_in = len(lefts) + len(sides)
    left_refs, right_refs = rest[: len(lefts)], rest[len(lefts) : n_in]
    away, keep = rest[n_in : n_in + 2]
    out, sems = rest[-2], rest[-1]
    turned = rest[n_in + 2 : -2]
    x, c, z, y = here()
    done = set()
    for number, (l, _) in enumerate(sides):
        t_ref = turned[l]
        if l not in done:
            done.add(l)
            for f in range(left_refs[l].shape[1] // 256):
                t_ref[f * 256 : (f + 1) * 256, :] = left_refs[l][:, f * 256 : (f + 1) * 256].T
        r_ref = right_refs[number]
        half = out.shape[-1]
        for g in range(2):

            def one(zz, carry, g=g, number=number, t_ref=t_ref, r_ref=r_ref):
                rows = t_ref[pl.ds(pl.multiple_of(zz * 256, 256), 256), :]
                v = jnp.dot(rows, r_ref[:, g * half : (g + 1) * half], preferred_element_type=F32).astype(BF)
                out[number, g, y, zz] = v[:128]
                out[number, g, 1 - y, zz] = v[128:]
                return carry

            lax.fori_loop(0, 4, one, 0)
        dx, dc = flip(x, number // 2), flip(c, number % 2)
        send_off(out.at[number], away, keep, dx, dc, (), sems.at[number])
    for number in range(4):
        pltpu.make_async_copy(out.at[number], keep.at[0], sems.at[number]).wait()


def grads(lefts, rights, sides, name):
    d, n = lefts[0].shape[1], rights[0].shape[1]
    dims = (2, 2, 2, 4, d // 8, n // 2)
    sides = tuple((l, i) for i, l in enumerate(sides))
    return pl.pallas_call(
        partial(grads_kernel, sides),
        in_specs=[WHOLE] * (len(lefts) + 4),
        out_specs=[SPOT] * 2,
        out_shape=[shape(dims, BF)] * 2,
        scratch_shapes=[pltpu.VMEM((d, l.shape[0]), BF) for l in lefts]
        + [pltpu.VMEM((4,) + dims[1:], BF), pltpu.SemaphoreType.DMA((4,))],
        compiler_params=BIG,
        cost_estimate=cost(2 * sum(r.size for r in rights) * d, *lefts, *rights, *rights, *rights),
        name=name,
    )(*lefts, *rights)


def grads_of(left, lefts, rights, sides, name):
    return grads([left] + list(lefts), rights, sides, name)


def ffn_kernel(last, first_row, act_ref, dy_ref, mid_ref, vec_ref, *rest):
    begin = rest[:2] if last else ()
    rest = rest[len(begin) :]
    refs, rest = rest[:8], rest[8:]
    outs, rest = rest[: 4 if last else 2], rest[4 if last else 2 :]
    dbe_ref, away, keep = rest[:3]
    act_t, hid_ref, dexp_ref, acc, dact, out, we0, wd0, we1, wd1, sems, out_sems = rest[3:]
    i = pl.program_id(0)
    s = lax.rem(i, 2)
    rows, d = act_ref.shape
    ff = d // 2
    x, c, z, y = here()
    mats = ((we0, wd0), (we1, wd1))

    @pl.when(i == 0)
    def _():
        for t in range(2):
            for n in range(2):
                pieces_of(refs, 2 * t + n, mats[t][n], sems.at[2 * t + n], "start")
        for f in range(d // 256):
            act_t[f * 256 : (f + 1) * 256, :] = act_ref[:, f * 256 : (f + 1) * 256].T
        if last:
            acc[...] = begin[0][...]
            dact[...] = begin[1][...]
            outs[3][...] = jnp.zeros_like(outs[3])
        else:
            acc[...] = jnp.zeros_like(acc)
            dact[...] = jnp.zeros_like(dact)

    dbe_ref[...] = jnp.zeros_like(dbe_ref)

    def block(t):
        we_ref, wd_ref = mats[t]

        @pl.when(s == 0)
        def _():
            for n in range(2):
                pieces_of(refs, 2 * t + n, mats[t][n], sems.at[2 * t + n], "wait")

        lanes = pl.ds(pl.multiple_of(s * ff, ff), ff)
        bias = vec_ref[first_row + t : first_row + t + 1, lanes]

        def half(r):
            we = we_ref[:, :, :, lanes].reshape(d, ff)
            wd = wd_ref[pl.ds(2 * s, 2)].reshape(ff, d)
            u = jnp.dot(act_ref[r, :], we, preferred_element_type=F32) + bias
            cdf = 0.5 * (1.0 + lax.erf(u * np.float32(0.5**0.5)))
            pdf = jnp.exp(-0.5 * u * u) * np.float32((2 * np.pi) ** -0.5)
            hid = (u * cdf).astype(BF)
            hid_ref[r, :] = hid
            dexp = (dot_nt(dy_ref[r, :], wd) * (cdf + u * pdf)).astype(BF)
            dexp_ref[r, :] = dexp
            dbe_ref[0] += row_sum(dexp.astype(F32))
            acc[r, :] += jnp.dot(hid, wd, preferred_element_type=F32)
            dact[r, :] += dot_nt(dexp, we)

        chunks(rows, 256, half)

        def e_part(zz, carry):
            at_rows = pl.ds(pl.multiple_of(zz * 256, 256), 256)
            v = jnp.dot(act_t[at_rows, :], dexp_ref[...], preferred_element_type=F32).astype(BF)
            out[2 * t, s, y, zz] = v[:128]
            out[2 * t, s, 1 - y, zz] = v[128:]
            return carry

        lax.fori_loop(0, 4, e_part, 0)
        hid_t = hid_ref[...].T
        for zz in range(2):
            for yy in range(2):
                n = 2 * zz + yy
                v = jnp.dot(hid_t[n * 128 : (n + 1) * 128], dy_ref[...], preferred_element_type=F32).astype(BF)
                for g in range(2):
                    out[2 * t + 1, g, flip(y, yy), 2 * s + zz] = v[:, g * ff : (g + 1) * ff]

        @pl.when(s == 1)
        def _():
            for n in range(2):
                number = 2 * t + n
                dx, dc = flip(x, number // 2), flip(c, number % 2)
                send_off(out.at[number], away, keep, dx, dc, (), out_sems.at[number])

    for t in range(2):
        pl.when(lax.div(i, 2) == t)(partial(block, t))

    @pl.when(i == pl.num_programs(0) - 1)
    def _():
        if last:
            out_ref, dmid_ref, low_ref, sum_ref = outs

            def back(r):
                mid = mid_ref[r, :]
                out_ref[r, :] = (mid + (acc[r, :] + vec_ref[12:13])).astype(BF)
                dy = dy_ref[r, :].astype(F32)
                total = apply_norm_back(r, dact[r, :], mid, vec_ref[10:11], dy, sum_ref)
                dmid_ref[r, :] = total
                low = total.astype(BF)
                low_ref[r, :] = low
                sum_ref[2:3] += row_sum(dy)
                sum_ref[3:4] += row_sum(low.astype(F32))

            chunks(rows, CHUNK, back)
        else:
            outs[0][...] = acc[...]
            outs[1][...] = dact[...]
        for number in range(4):
            pltpu.make_async_copy(out.at[number], keep.at[0], out_sems.at[number]).wait()


def ffn(act, dy, mid, vecs, unit, m, begin, first_row):
    rows, d = act.shape
    last = bool(begin)
    still = lambda s: pl.BlockSpec(s.shape, lambda j: (0,) * len(s.shape))
    dims = (2, 2, 2, 4, m, d // 2)
    if last:
        heads = [shape(act.shape, BF), shape(act.shape, F32), shape(act.shape, BF), shape((8, d), F32)]
    else:
        heads = [shape(act.shape, F32)] * 2
    return pl.pallas_call(
        partial(ffn_kernel, last, first_row),
        grid=(4,),
        in_specs=[still(v) for v in (act, dy, mid, vecs, *begin)] + [SPOT] * 8,
        out_specs=[still(s) for s in heads]
        + [pl.BlockSpec((1, 1, d // 2), lambda j: (j, 0, 0))]
        + [SPOT] * 2,
        out_shape=heads + [shape((4, 1, d // 2), F32)] + [shape(dims, BF)] * 2,
        scratch_shapes=[
            pltpu.VMEM((d, rows), BF),
            pltpu.VMEM((rows, d // 2), BF),
            pltpu.VMEM((rows, d // 2), BF),
            pltpu.VMEM((rows, d), F32),
            pltpu.VMEM((rows, d), F32),
            pltpu.VMEM((4,) + dims[1:], BF),
        ]
        + loaded(m, d, 4)
        + [pltpu.SemaphoreType.DMA((4,))],
        compiler_params=BIG,
        cost_estimate=cost(24 * act.size * d, *unit, *unit, mid, mid),
        name="ffn",
    )(act, dy, mid, vecs, *begin, *unit)


def finish_kernel(count, *rest):
    units, outs, held = [rest[3 * i : 3 * i + 3] for i in range(count)], rest[3 * count : -1], rest[-1]
    x, c, _, _ = here()
    half = units[0][0].shape[-1]
    for i, (own_ref, x_ref, core_ref) in enumerate(units):
        held[0], held[2] = own_ref[...], x_ref[...]
        held[1], held[3] = core_ref[0], core_ref[1]
        for number in range(4):
            j = flip(x, number // 2) * 2 + flip(c, number % 2)
            for g in range(2):
                v = held[j, g].astype(F32)
                if count == 1:
                    outs[number][:, g * half : (g + 1) * half] = v
                elif number % 2:
                    t = 2 * i + number // 2
                    outs[1][t * v.shape[0] : (t + 1) * v.shape[0], g * half : (g + 1) * half] = v
                else:
                    t = 2 * i + number // 2
                    for f in range(half // 128):
                        to = ((g * (half // 128) + f) * 4 + t) * 128
                        outs[0][:, to : to + 128] = v[:, f * 128 : (f + 1) * 128]


def finish(*units):
    _, m, half = units[0][0].shape
    n = 2 * half
    dims = [(m, n)] * 4 if len(units) == 1 else [(m, 4 * n), (4 * m, n)]
    return pl.pallas_call(
        partial(finish_kernel, len(units)),
        in_specs=[WHOLE] * (3 * len(units)),
        out_specs=[WHOLE] * len(dims),
        out_shape=[shape(s, F32) for s in dims],
        scratch_shapes=[pltpu.VMEM((4, 2, m, half), BF)],
        compiler_params=BIG,
        cost_estimate=cost(0, *[v for u in units for v in u] * 3),
        name="finish",
    )(*[v for u in units for v in u])


def product(left, right):
    return jnp.dot(left, right, preferred_element_type=F32)


def product_nt(left, right):
    return lax.dot_general(
        left, right, (((1,), (1,)), ((), ())), preferred_element_type=F32
    )


def moments(values):
    average = jnp.mean(values, -1, keepdims=True)
    centered = values - average
    variance = jnp.mean(centered * centered, -1, keepdims=True)
    inverse = lax.rsqrt(variance + EPSILON)
    return (centered * inverse, inverse)


def norm_back(grad_out, normed, inverse, gain_vec):
    gain_grad = jnp.sum(grad_out * normed, 0)
    shift_grad = jnp.sum(grad_out, 0)
    scaled = grad_out * gain_vec
    mean_one = jnp.mean(scaled, -1, keepdims=True)
    mean_two = jnp.mean(scaled * normed, -1, keepdims=True)
    return (inverse * (scaled - mean_one - normed * mean_two), gain_grad, shift_grad)


def gelu_both(u):
    cdf = 0.5 * (1.0 + lax.erf(u * np.float32(0.5**0.5)))
    pdf = jnp.exp(-0.5 * u * u) * np.float32((2 * np.pi) ** -0.5)
    return (u * cdf).astype(BF), (cdf + u * pdf).astype(BF)


def body(
    groups,
    rows,
    decoder_input,
    encoder_out,
    prefix_length,
    output_grad,
    self_query,
    self_key,
    self_value,
    self_output,
    selfquery_bias,
    selfvalue_bias,
    self_attention_output_bias,
    cross_query,
    cross_key,
    cross_value,
    cross_output,
    crossquery_bias,
    crossvalue_bias,
    crossoutput_bias,
    expand_weight,
    expand_bias,
    down_projection_weight,
    reduce_bias,
    selfnorm_gain,
    selfnorm_bias,
    crossnorm_gain,
    crossnorm_bias,
    finalnorm_gain,
    finalnorm_bias,
):
    place = Place(groups, rows)
    batch, seq, d = decoder_input.shape
    m = self_query.shape[0]
    ff = expand_weight.shape[1]
    fl = ff // rows // 2
    k4 = ff // d

    small = [
        selfnorm_gain, selfnorm_bias, selfquery_bias, selfvalue_bias, self_attention_output_bias,
        crossnorm_gain, crossnorm_bias, crossquery_bias, crossvalue_bias, crossoutput_bias,
        finalnorm_gain, finalnorm_bias, reduce_bias,
    ]
    packed = jnp.concatenate([jnp.stack(small), expand_bias.reshape(k4, m)])
    vecs = gather_vectors(place, packed).astype(F32)
    (g1, b1, bq, bv, bo, g2, b2, bcq, bcv, bco, g3, b3, br) = [
        vecs[:, i].reshape(d) for i in range(13)
    ]
    be = vecs[:, 13:].reshape(rows, 2, fl)

    expand_halves = [
        expand_weight.reshape(m, rows, 2, fl)[:, :, h].reshape(m, rows * fl) for h in range(2)
    ]
    down_halves = [down_projection_weight[h * fl : (h + 1) * fl] for h in range(2)]

    lane, ring_lane = Lane(4), Lane(2)
    gathers = [
        Gather(place, lane, ring_lane, shard, split)
        for shard, split in (
            (jnp.concatenate([self_query, self_key], 1), True),
            (self_value, False),
            (jnp.concatenate([cross_key, cross_value], 1), True),
            (self_output, False),
            (jnp.concatenate([cross_query, cross_output], 1), True),
            (expand_halves[0], True),
            (expand_halves[1], True),
            (down_halves[0], False),
            (down_halves[1], True),
        )
    ]
    run_steps(gathers)
    w_qk, w_v, w_ckv, w_o, w_cqo, *w_ff = [u.v for u in gathers]
    w_e, w_d = w_ff[:2], w_ff[2:]

    x = decoder_input.reshape(batch * seq, d).astype(F32)
    e = encoder_out.reshape(-1, d)
    dy = output_grad.reshape(batch * seq, d)

    n1, i1 = moments(x)
    act1 = (n1 * g1 + b1).astype(BF)
    qk = product(act1, w_qk)
    q = (qk[:, :d] + bq).astype(BF)
    k = qk[:, d:].astype(BF)
    v = (product(act1, w_v) + bv).astype(BF)
    o, p = attend(q, k, v, prefix_length, batch, True)
    mid1 = x + (product(o, w_o) + bo)
    n2, i2 = moments(mid1)
    act2 = (n2 * g2 + b2).astype(BF)
    w_cq, w_co = w_cqo[:, :d], w_cqo[:, d:]
    cq = (product(act2, w_cq) + bcq).astype(BF)
    ckv = product(e, w_ckv)
    ck = ckv[:, :d].astype(BF)
    cv = (ckv[:, d:] + bcv).astype(BF)
    co, cp = attend(cq, ck, cv, prefix_length, batch, False)
    mid2 = mid1 + (product(co, w_co) + bco)
    n3, i3 = moments(mid2)
    act3 = (n3 * g3 + b3).astype(BF)
    hidden, slope = [], []
    for h in range(2):
        hid, slo = gelu_both(product(act3, w_e[h]) + be[:, h].reshape(-1))
        hidden.append(hid)
        slope.append(slo)
    layer_out = (mid2 + (product(hidden[0], w_d[0]) + product(hidden[1], w_d[1]) + br)).astype(BF)

    scatter = partial(Scatter, place, lane, ring_lane)
    dyf = dy.astype(F32)
    g_down = [scatter(hidden[0], dy, True), scatter(hidden[1], dy, False)]
    dexp = [(product_nt(dy, w_d[h]) * slope[h].astype(F32)).astype(BF) for h in range(2)]
    g_exp = [scatter(act3, dexp[0], True), scatter(act3, dexp[1], False)]
    dact3 = product_nt(dexp[0], w_e[0]) + product_nt(dexp[1], w_e[1])
    dn, gg3, gb3 = norm_back(dact3, n3, i3, g3)
    dmid2 = dyf + dn
    dcross = dmid2.astype(BF)
    g_co = scatter(co, dcross, True)
    dco = product_nt(dcross, w_co).astype(BF)
    dcq, dck, dcv = attend_back(dco, cq, ck, cv, cp, batch)
    g_ck = scatter(e, dck, True)
    g_cv = scatter(e, dcv, False)
    g_cq = scatter(act2, dcq, False)
    encoder_grad = product_nt(jnp.concatenate([dck, dcv], 1), w_ckv)
    dn, gg2, gb2 = norm_back(product_nt(dcq, w_cq), n2, i2, g2)
    dmid1 = dmid2 + dn
    dself = dmid1.astype(BF)
    g_so = scatter(o, dself, True)
    dao = product_nt(dself, w_o).astype(BF)
    dq, dk, dv = attend_back(dao, q, k, v, p, batch)
    g_sv = scatter(act1, dv, False)
    g_sq = scatter(act1, dq, True)
    g_sk = scatter(act1, dk, True)
    dact1 = product_nt(jnp.concatenate([dq, dk], 1), w_qk) + product_nt(dv, w_v)
    dn, gg1, gb1 = norm_back(dact1, n1, i1, g1)
    input_grad = dmid1 + dn

    def column_sum(t):
        return jnp.sum(t.astype(F32), 0)

    dbe = jnp.stack([column_sum(t).reshape(rows, fl) for t in dexp], 1).reshape(rows, k4, m)
    early = [
        gg2, gb2, column_sum(dcq), column_sum(dcv), column_sum(dcross),
        gg3, gb3, column_sum(dy), column_sum(dself),
    ]
    early = jnp.concatenate([jnp.stack([t.reshape(rows, m) for t in early], 1), dbe], 1)
    late = [gg1, gb1, column_sum(dq), column_sum(dv)]
    late = jnp.stack([t.reshape(rows, m) for t in late], 1)

    first = g_down + g_exp + [g_co, g_cv, g_ck, g_cq, g_so]
    second = [g_sv, g_sq, g_sk]
    run_steps(first + second)
    early = scatter_vectors(place, lane, ring_lane, early)
    (*g_ff, g_co, g_cv, g_ck, g_cq, g_so) = finish_all(place, lane, first)
    g_down, g_exp = g_ff[:2], g_ff[2:]
    late = scatter_vectors(place, lane, ring_lane, late)
    g_sv, g_sq, g_sk = finish_all(place, lane, second)

    g_exp = jnp.stack([t.reshape(m, rows, fl) for t in g_exp], 2).reshape(m, ff)
    g_down = jnp.concatenate(g_down, 0)
    return (
        layer_out.reshape(batch, seq, d),
        input_grad.reshape(batch, seq, d),
        encoder_grad.reshape(encoder_out.shape),
        g_sq, g_sk, g_sv, g_so,
        late[2], late[3], early[8],
        g_cq, g_ck, g_cv, g_co,
        early[2], early[3], early[4],
        g_exp, early[9:].reshape(-1), g_down, early[7],
        late[0], late[1], early[0], early[1], early[5], early[6],
    )


class Order:
    def __init__(self, width):
        self.width, self.past, self.sent, self.ran = width, [], [], []

    def send(self, move, v):
        after = list(self.ran)
        if len(self.past) >= self.width:
            after.append(self.past[-self.width])
        if after:
            v, *_ = lax.optimization_barrier((v, *after))
        got = move(v)
        self.past.append(got)
        self.sent.append(v)
        return got

    def swap(self, move, v):
        if self.ran:
            v, *_ = lax.optimization_barrier((v, *self.ran))
        self.sent.append(v)
        return move(v)

    def run(self, kernel, v, *rest, **named):
        if self.sent or self.ran:
            v, *_ = lax.optimization_barrier((v, *self.sent, *self.ran))
        out = kernel(v, *rest, **named)
        self.sent, self.ran = [], [out[0] if isinstance(out, (list, tuple)) else out]
        return out


class Unit:
    def __init__(self, place, order, piece):
        self.place, self.order, self.piece = place, order, piece
        self.steps = [self.ring, self.one, self.two, self.core]

    def ring(self):
        a = self.order.swap(partial(ring_gather, self.place), self.piece)
        self.a0, self.a1 = a[:, 0], a[:, 1]

    def one(self):
        self.p0 = jnp.stack([self.a0, self.order.send(self.place.pair, self.a0)])
        self.p1 = jnp.stack([self.a1, self.order.send(self.place.across, self.a1)])

    def two(self):
        self.q0 = self.order.send(self.place.across, self.p0)
        self.q1 = self.order.send(self.place.pair, self.p1)
        self.c0 = self.order.send(self.place.core, self.p0)
        self.c1 = self.order.send(self.place.core, self.p1)

    def core(self):
        d0 = self.order.send(self.place.core, self.q0)
        d1 = self.order.send(self.place.core, self.q1)
        self.refs = (self.p0, self.q0, self.p1, self.q1, self.c0, d0, self.c1, d1)


def low_sum(*parts):
    total = parts[0].astype(F32)
    for p in parts[1:]:
        total = total + p.astype(F32)
    return total.astype(BF)


class Sum:
    def __init__(self, place, order, away, keep):
        self.place, self.order = place, order
        self.away, self.keep = away, keep
        self.steps = [self.core, self.one, self.two, self.ring, self.last_x, self.last_core]

    def core(self):
        self.came = self.order.send(self.place.core, self.away)

    def one(self):
        k, r = self.keep, self.came
        self.from_x = self.order.send(self.place.across, low_sum(k[1, 0], r[1, 0]))
        self.from_y = self.order.send(self.place.pair, low_sum(k[:, 1, 1], r[:, 1, 1]))

    def two(self):
        k, r, fx, fy = self.keep, self.came, self.from_x, self.from_y
        self.next_y = self.order.send(self.place.pair, low_sum(k[0, 0, 1], r[0, 0, 1], fx[1]))
        self.next_x = self.order.send(self.place.across, low_sum(k[1, 1, 0], r[1, 1, 0], fy[1]))

    def ring(self):
        k, r, fx, fy = self.keep, self.came, self.from_x, self.from_y
        first = low_sum(k[0, 0, 0], r[0, 0, 0], fx[0], self.next_y)
        second = low_sum(k[0, 1, 0], r[0, 1, 0], fy[0], self.next_x)
        self.own = self.order.swap(partial(ring_sum, self.place), jnp.stack([first, second], 1))

    def last_x(self):
        self.own_x = self.order.send(self.place.across, self.own)

    def last_core(self):
        came = self.order.send(self.place.core, jnp.stack([self.own, self.own_x]))
        self.parts = (self.own, self.own_x, came)


def fast_body(
    groups,
    rows,
    decoder_input,
    encoder_out,
    prefix_length,
    output_grad,
    self_query,
    self_key,
    self_value,
    self_output,
    selfquery_bias,
    selfvalue_bias,
    self_attention_output_bias,
    cross_query,
    cross_key,
    cross_value,
    cross_output,
    crossquery_bias,
    crossvalue_bias,
    crossoutput_bias,
    expand_weight,
    expand_bias,
    down_projection_weight,
    reduce_bias,
    selfnorm_gain,
    selfnorm_bias,
    crossnorm_gain,
    crossnorm_bias,
    finalnorm_gain,
    finalnorm_bias,
):
    place = Place(groups, rows)
    batch, seq, d = decoder_input.shape
    m = self_query.shape[0]
    ff = expand_weight.shape[1]
    rank = 2 * place.x + place.c
    order = Order(5)

    small = [
        selfnorm_gain, selfnorm_bias, selfquery_bias, selfvalue_bias, self_attention_output_bias,
        crossnorm_gain, crossnorm_bias, crossquery_bias, crossvalue_bias, crossoutput_bias,
        finalnorm_gain, finalnorm_bias, reduce_bias, expand_bias,
    ]
    packed = jnp.concatenate(small)
    count = 13 + ff // d
    packed = jnp.pad(packed, (0, 8 * d - packed.shape[0])).reshape(2, 8, d // 2)

    def pick(*shards):
        v = at(jnp.stack(shards), rank)
        return v.reshape(m, 2, d // 2).transpose(1, 0, 2)

    w_e = expand_weight.reshape(m, rows, 4, -1).transpose(2, 0, 1, 3).reshape(4, m, d)
    w_d = down_projection_weight.reshape(4, m, d)
    unit = partial(Unit, place, order)
    u_self = unit(jnp.concatenate([pick(self_query, self_key, self_value, self_output), packed], 1))
    u_cross = unit(pick(cross_query, cross_key, cross_value, cross_output))
    u_low = unit(pick(w_e[0], w_d[0], w_e[1], w_d[1]))
    u_high = unit(pick(w_e[2], w_d[2], w_e[3], w_d[3]))

    x = decoder_input.reshape(batch * seq, d)
    e = encoder_out.reshape(-1, d)
    dy = output_grad.reshape(batch * seq, d)
    run = order.run

    u_self.ring()
    u_self.one()
    u_cross.ring()
    u_self.two()
    u_low.ring()
    u_self.core()
    u_cross.one()
    self_w = u_self.refs
    both = jnp.stack([v[:, :, m:] for v in (u_self.p0[:, :, :], jnp.stack([u_self.p1[0], u_self.q1[0]]))])
    both = both.transpose(2, 1, 0, 3, 4)
    both = jnp.where(place.y == 0, both, both[:, ::-1]).transpose(0, 1, 2, 3, 4).reshape(rows, -1)
    vecs = both[:, : count * m].reshape(rows, count, m).transpose(1, 0, 2).reshape(count, d).astype(F32)
    act1, q, k, v = run(first, x, vecs, self_w, m)
    u_cross.two()
    o, p = run(attend, q, k, v, prefix_length, batch, True)
    u_high.ring()
    u_cross.core()
    cross_w = u_cross.refs
    u_low.one()
    mid1, act2 = run(project, o, x, vecs, (4, 5, 6, None), (self_w,), (3,), m, "self_out")
    u_low.two()
    ck, cv = run(memory, e, vecs, cross_w, m)
    cq = run(query, act2, vecs, 7, cross_w, m)
    u_low.core()
    u_high.one()
    co, cp = run(attend, cq, ck, cv, prefix_length, batch, False)
    u_high.two()
    mid2, act3 = run(project, co, mid1, vecs, (9, 10, 11, None), (cross_w,), (3,), m, "cross_out")
    low_w = u_low.refs

    *begin, dbe_low, away, keep = run(ffn, act3, dy, mid2, vecs, low_w, m, (), 13)
    total = partial(Sum, place, order)
    g_low = total(away, keep)
    u_high.core()
    g_low.core()
    layer_out, dmid2, dcross, sums3, dbe_high, away, keep = run(
        ffn, act3, dy, mid2, vecs, u_high.refs, m, tuple(begin), 15
    )
    g_high = total(away, keep)
    g_low.one()
    g_high.core()
    dco = run(output_back, dcross, cross_w, m)
    dcq, dck, dcv = run(attend_back, dco, cq, ck, cv, cp, batch)
    g_low.two()
    g_high.one()
    g_cross = total(*run(grads_of, act2, [e, co], [dcq, dck, dcv, dcross], (0, 1, 1, 2), "cross_grads"))
    g_cross.core()
    g_low.ring()
    dmid1, dself, dao, sums2 = run(cross_back, dcq, mid1, dmid2, vecs, cross_w, self_w, m)
    g_high.two()
    dq, dk, dv = run(attend_back, dao, q, k, v, p, batch)
    g_cross.one()
    g_high.ring()
    g_self = total(*run(grads_of, act1, [o], [dq, dk, dv, dself], (0, 0, 0, 1), "self_grads"))
    g_self.core()
    g_cross.two()
    encoder_grad, sums_e = run(memory_back, dck, dcv, cross_w, m)
    g_self.one()
    g_cross.ring()
    input_grad, sums1 = run(self_back, dq, dk, dv, x, dmid1, vecs, self_w, m)
    g_self.two()

    def by_shard(v):
        return v.reshape(-1, rows, m).transpose(1, 0, 2)

    dbe = jnp.concatenate([dbe_low, dbe_high]).reshape(4, d)
    sums = by_shard(jnp.concatenate([sums1[:4], sums2[:4], sums3[:4], sums_e[:1], dbe]))
    sums = (sums.astype(BF).astype(F32) + order.send(place.core, sums.astype(BF)).astype(F32)).astype(BF)
    g_low.last_x()
    g_high.last_x()
    sums = (sums.astype(F32) + order.send(place.across, sums).astype(F32)).astype(BF)
    g_self.ring()
    g_low.last_core()
    g_high.last_core()
    sums = sums.reshape((place.ring, 2) + sums.shape[1:])
    came = order.send(place.pair, at(sums, 1 - place.y, 1))
    sums = (at(sums, place.y, 1).astype(F32) + came.astype(F32)).astype(BF)
    g_expand, g_down = finish(g_low.parts, g_high.parts)
    g_cross.last_x()
    sums = order.swap(partial(ring_sum, place), sums).astype(F32)
    g_cross.last_core()
    g_cq, g_ck, g_cv, g_co = finish(g_cross.parts)
    g_self.last_x()
    g_self.last_core()
    g_sq, g_sk, g_sv, g_so = finish(g_self.parts)
    return (
        layer_out.reshape(batch, seq, d),
        input_grad.reshape(batch, seq, d),
        encoder_grad.reshape(encoder_out.shape),
        g_sq, g_sk, g_sv, g_so,
        sums[2], sums[3], sums[7],
        g_cq, g_ck, g_cv, g_co,
        sums[6], sums[12], sums[11],
        g_expand, sums[13:].reshape(-1), g_down, sums[10],
        sums[0], sums[1], sums[4], sums[5], sums[8], sums[9],
    )


def solution(mesh):
    groups, rows = mesh.shape["replica"], mesh.shape["fsdp"]
    data = P(("replica", "fsdp"), None, None)
    mat, vec = P("fsdp", None), P("fsdp")
    weights = (
        (mat,) * 4 + (vec,) * 3 + (mat,) * 4 + (vec,) * 3 + (mat, vec, mat, vec) + (vec,) * 6
    )
    return jax.shard_map(
        partial(fast_body if rows == 8 else body, groups, rows),
        mesh=mesh,
        in_specs=(data, data, P(("replica", "fsdp")), data) + weights,
        out_specs=(data, data, data) + weights,
        check_vma=False,
    )
```

```python
from functools import partial

import jax
import jax.numpy as jnp
import numpy as np
from jax import lax
from jax.experimental import pallas as pl
from jax.experimental.pallas import tpu as pltpu
from jax.sharding import PartitionSpec as P

H = 16
EPSILON = 1e-05
MASKED = -1e30
BF = jnp.bfloat16
F32 = jnp.float32


class Place:
    def __init__(self, groups, rows):
        self.groups = groups
        self.rows = rows
        self.ring = rows // 2
        rep = lax.axis_index("replica")
        row = lax.axis_index("fsdp")
        self.c = lax.rem(rep, 2)
        self.x = lax.div(rep, 2)
        self.y = lax.rem(row, 2)
        self.z = lax.div(row, 2)

    def core(self, v):
        return lax.ppermute(v, "replica", [(i, i ^ 1) for i in range(self.groups)])

    def across(self, v):
        return lax.ppermute(v, "replica", [(i, i ^ 2) for i in range(self.groups)])

    def pair(self, v):
        return lax.ppermute(v, "fsdp", [(i, i ^ 1) for i in range(self.rows)])

    def next(self, v):
        return lax.ppermute(v, "fsdp", [(i, (i + 2) % self.rows) for i in range(self.rows)])

    def ring_members(self):
        return [[2 * k + side for k in range(self.ring)] for side in range(2)]


def at(v, i, axis=0):
    return lax.dynamic_index_in_dim(v, i, axis, keepdims=False)


class Lane:
    def __init__(self, width):
        self.width = width
        self.past = []

    def __call__(self, send, v):
        if len(self.past) >= self.width:
            v, _ = lax.optimization_barrier((v, self.past[-self.width]))
        got = send(v)
        self.past.append(got)
        return got


def ring_gather(place, piece):
    if place.ring <= 4:
        copies = jnp.broadcast_to(piece[None], (place.ring,) + piece.shape)
        return lax.all_to_all(copies, "fsdp", 0, 0, axis_index_groups=place.ring_members())
    return lax.all_gather(piece, "fsdp", axis_index_groups=place.ring_members())


def order_kernel(ring, split, mine, theirs, out, sems):
    rep = lax.axis_index("replica")
    c, x = lax.rem(rep, 2), lax.div(rep, 2)
    y = lax.rem(lax.axis_index("fsdp"), 2)
    copies = []
    for dc, block in enumerate((mine, theirs)):
        cc = 1 - c if dc else c
        for dx in range(2 if split else 1):
            for dy in range(2):
                yy = 1 - y if dy else y
                for z in range(ring):
                    if split:
                        xx = 1 - x if dx else x
                        src, dst = block.at[dx, dy, z], out.at[z, yy, xx, cc]
                    else:
                        src, dst = block.at[dy, z], out.at[z, yy, cc]
                    copies.append(pltpu.make_async_copy(src, dst, sems.at[len(copies)]))
    for copy in copies:
        copy.start()
    for copy in copies:
        copy.wait()


def in_order(place, split, mine, theirs):
    ring, rows, n = mine.shape[-3:]
    dims = (ring, 2, 2, 2) if split else (ring, 2, 2)
    if rows % 16 == 0:
        count = 2 * mine.size // (rows * n)
        out = pl.pallas_call(
            partial(order_kernel, ring, split),
            out_shape=jax.ShapeDtypeStruct(dims + (rows, n), mine.dtype),
            in_specs=[pl.BlockSpec(memory_space=pl.ANY)] * 2,
            out_specs=pl.BlockSpec(memory_space=pltpu.VMEM),
            scratch_shapes=[pltpu.SemaphoreType.DMA((count,))],
            cost_estimate=pl.CostEstimate(
                flops=0, transcendentals=0, bytes_accessed=4 * count * rows * n
            ),
            name="order",
        )(mine, theirs)
    else:
        both = jnp.stack([mine, theirs])
        at_c = (place.c, 1 - place.c)
        both = jnp.stack([at(both, i, 0) for i in at_c])
        if split:
            both = jnp.stack([at(both, i, 1) for i in (place.x, 1 - place.x)], 1)
        both = jnp.stack([at(both, i, both.ndim - 4) for i in (place.y, 1 - place.y)], both.ndim - 4)
        out = jnp.transpose(both, (3, 2, 1, 0, 4, 5) if split else (2, 1, 0, 3, 4))
    return out.reshape(-1, n)


class Gather:
    def __init__(self, place, lane, ring_lane, shard, split):
        self.place, self.lane, self.ring_lane, self.split = place, lane, ring_lane, split
        m, n = shard.shape
        if split:
            self.v = at(shard.reshape(4, m // 4, n), 2 * place.x + place.c)
        else:
            self.v = at(shard.reshape(2, m // 2, n), place.c)
        self.steps = [self.ring, self.pair] + ([self.across] if split else []) + [self.core]

    def ring(self):
        self.v = self.ring_lane(partial(ring_gather, self.place), self.v)

    def pair(self):
        self.v = jnp.stack([self.v, self.lane(self.place.pair, self.v)])

    def across(self):
        self.v = jnp.stack([self.v, self.lane(self.place.across, self.v)])

    def core(self):
        self.v = in_order(self.place, self.split, self.v, self.lane(self.place.core, self.v))


def run_steps(units):
    last = max(i + len(u.steps) for i, u in enumerate(units))
    for t in range(last):
        for i, u in enumerate(units):
            if 0 <= t - i < len(u.steps):
                u.steps[t - i]()


def gather_vectors(place, packed):
    a = ring_gather(place, packed)
    b = place.pair(a)
    both = jnp.stack([jnp.where(place.y == 0, a, b), jnp.where(place.y == 0, b, a)], 1)
    return both.reshape((place.rows,) + packed.shape)


def product_t(left, right):
    return lax.dot_general(
        left, right, (((0,), (0,)), ((), ())), preferred_element_type=F32
    )


def columns(v, k, i):
    w = v.shape[1] // k
    return lax.dynamic_slice(v, (0, i * w), (v.shape[0], w))


def join2(own, other, bit):
    first = jnp.where(bit == 0, own, other)
    second = jnp.where(bit == 0, other, own)
    return jnp.concatenate([first, second], -1)


def ring_sum(place, parts):
    if place.ring <= 4:
        came = lax.all_to_all(parts, "fsdp", 0, 0, axis_index_groups=place.ring_members())
        return jnp.sum(came.astype(F32), 0).astype(BF)
    return lax.psum_scatter(
        parts, "fsdp", scatter_dimension=0, axis_index_groups=place.ring_members()
    )


class Scatter:
    def __init__(self, place, lane, ring_lane, left, right, split):
        self.place, self.lane, self.ring_lane, self.split = place, lane, ring_lane, split
        self.left, self.right = left, right
        self.steps = [self.core] + ([self.across] if split else []) + [self.pair, self.ring]

    def core(self):
        c = self.place.c
        away = product_t(self.left, columns(self.right, 2, 1 - c)).astype(BF)
        self.right = columns(self.right, 2, c)
        self.came = self.lane(self.place.core, away)

    def across(self):
        x = self.place.x
        away = product_t(self.left, columns(self.right, 2, 1 - x))
        away = (away + columns(self.came, 2, 1 - x).astype(F32)).astype(BF)
        self.right, self.came = columns(self.right, 2, x), columns(self.came, 2, x)
        self.came_x = self.lane(self.place.across, away)

    def pair(self):
        part = product_t(self.left, self.right) + self.came.astype(F32)
        if self.split:
            part = part + self.came_x.astype(F32)
        part = part.astype(BF)
        part = part.reshape(self.place.ring, 2, -1, part.shape[1])
        y = self.place.y
        came = self.lane(self.place.pair, at(part, 1 - y, 1))
        self.kept = (at(part, y, 1).astype(F32) + came.astype(F32)).astype(BF)

    def ring(self):
        self.own = self.ring_lane(partial(ring_sum, self.place), self.kept)


def finish_all(place, lane, units):
    flat = [u.own.reshape(-1, 128) for u in units]
    sizes = [f.shape[0] for f in flat]
    own = jnp.concatenate(flat)
    came = lane(place.across, own)
    pieces, at_row = [], 0
    for u, size in zip(units, sizes):
        mine, other = own[at_row : at_row + size], came[at_row : at_row + size]
        at_row += size
        mine, other = mine.reshape(u.own.shape), other.reshape(u.own.shape)
        if u.split:
            pieces.append(join2(mine, other, place.x))
        else:
            pieces.append((mine.astype(F32) + other.astype(F32)).astype(BF))
    own = jnp.concatenate([p.reshape(-1, 128) for p in pieces])
    came = lane(place.core, own)
    out, at_row = [], 0
    for p in pieces:
        size = p.size // 128
        out.append(join2(p, came[at_row : at_row + size].reshape(p.shape), place.c).astype(F32))
        at_row += size
    return out


def scatter_vectors(place, lane, ring_lane, v):
    own = v.astype(BF)
    own = (own.astype(F32) + lane(place.core, own).astype(F32)).astype(BF)
    own = (own.astype(F32) + lane(place.across, own).astype(F32)).astype(BF)
    own = own.reshape((place.ring, 2) + own.shape[1:])
    came = lane(place.pair, at(own, 1 - place.y, 1))
    own = (at(own, place.y, 1).astype(F32) + came.astype(F32)).astype(BF)
    return ring_lane(partial(ring_sum, place), own).astype(F32)


PAIR = 128


def half_masks(rows):
    lane = lax.broadcasted_iota(jnp.int32, (rows, PAIR), 1)
    return (lane < PAIR // 2, lane >= PAIR // 2)


def dot_nt(a, b):
    return lax.dot_general(a, b, (((1,), (1,)), ((), ())), preferred_element_type=F32)


def attend_kernel(masked, scale, prefix_ref, q_ref, k_ref, v_ref, o_ref, p_ref):
    rows, keys = q_ref.shape[0], k_ref.shape[0]
    masks = half_masks(rows)
    if masked:
        i = lax.broadcasted_iota(jnp.int32, (rows, keys), 0)
        j = lax.broadcasted_iota(jnp.int32, (rows, keys), 1)
        allowed = (j <= i) | (j < prefix_ref[pl.program_id(0)])
    for pair in range(q_ref.shape[1] // PAIR):
        lanes = slice(pair * PAIR, (pair + 1) * PAIR)
        q, k, v = q_ref[:, lanes], k_ref[:, lanes], v_ref[:, lanes]
        both = []
        for h in range(2):
            s = dot_nt(jnp.where(masks[h], q, jnp.zeros_like(q)), k)
            if masked:
                s = jnp.where(allowed, s, MASKED)
            e = jnp.exp((s - jnp.max(s, -1, keepdims=True)) * scale)
            p = (e * (1.0 / jnp.sum(e, -1, keepdims=True))).astype(BF)
            p_ref[2 * pair + h] = p
            both.append(jnp.dot(p, v, preferred_element_type=F32))
        o_ref[:, lanes] = jnp.where(masks[0], both[0], both[1]).astype(BF)


def attend(q, k, v, prefix, batch, masked, group=4):
    rows, keys, d = q.shape[0] // batch, k.shape[0] // batch, q.shape[1]
    wide = group * d // H
    spec = lambda n: pl.BlockSpec((n, wide), lambda b, g, *_: (b, g))
    return pl.pallas_call(
        partial(attend_kernel, masked, (d // H) ** -0.5),
        grid_spec=pltpu.PrefetchScalarGridSpec(
            num_scalar_prefetch=1,
            grid=(batch, H // group),
            in_specs=[spec(rows), spec(keys), spec(keys)],
            out_specs=[
                spec(rows),
                pl.BlockSpec((None, group, rows, keys), lambda b, g, *_: (b, g, 0, 0)),
            ],
        ),
        out_shape=[
            jax.ShapeDtypeStruct(q.shape, BF),
            jax.ShapeDtypeStruct((batch, H, rows, keys), BF),
        ],
        compiler_params=pltpu.CompilerParams(vmem_limit_bytes=40 * 2**20),
        cost_estimate=pl.CostEstimate(
            flops=16 * q.size * keys * URGENT,
            transcendentals=0,
            bytes_accessed=(4 * q.size + 4 * k.size + 2 * batch * H * rows * keys) * URGENT,
        ),
        name="attend",
    )(prefix, q, k, v)


def attend_back_kernel(scale, do_ref, q_ref, k_ref, v_ref, p_ref, dq_ref, dk_ref, dv_ref):
    rows = q_ref.shape[0]
    half = PAIR // 2
    masks = half_masks(rows)
    for pair in range(q_ref.shape[1] // PAIR):
        lanes = slice(pair * PAIR, (pair + 1) * PAIR)
        do, q, k, v = do_ref[:, lanes], q_ref[:, lanes], k_ref[:, lanes], v_ref[:, lanes]
        do_t, q_t = do.T, q.T
        dq, dk_t, dv_t = [], [], []
        for h in range(2):
            p = p_ref[2 * pair + h]
            dp = dot_nt(jnp.where(masks[h], do, jnp.zeros_like(do)), v)
            pf = p.astype(F32)
            ds = (pf * (dp - jnp.sum(dp * pf, -1, keepdims=True))).astype(BF)
            dq.append(jnp.dot(ds, k, preferred_element_type=F32))
            part = slice(h * half, (h + 1) * half)
            dk_t.append(jnp.dot(q_t[part], ds, preferred_element_type=F32))
            dv_t.append(jnp.dot(do_t[part], p, preferred_element_type=F32))
        dq_ref[:, lanes] = (jnp.where(masks[0], dq[0], dq[1]) * scale).astype(BF)
        dk_ref[:, lanes] = (jnp.concatenate(dk_t, 0) * scale).astype(BF).T
        dv_ref[:, lanes] = jnp.concatenate(dv_t, 0).astype(BF).T


def attend_back(do, q, k, v, p, batch, group=4):
    rows, keys, d = q.shape[0] // batch, k.shape[0] // batch, q.shape[1]
    wide = group * d // H
    spec = lambda n: pl.BlockSpec((n, wide), lambda b, g: (b, g))
    return pl.pallas_call(
        partial(attend_back_kernel, (d // H) ** -0.5),
        grid=(batch, H // group),
        in_specs=[
            spec(rows), spec(rows), spec(keys), spec(keys),
            pl.BlockSpec((None, group, rows, keys), lambda b, g: (b, g, 0, 0)),
        ],
        out_specs=[spec(rows), spec(keys), spec(keys)],
        out_shape=[
            jax.ShapeDtypeStruct(q.shape, BF),
            jax.ShapeDtypeStruct(k.shape, BF),
            jax.ShapeDtypeStruct(v.shape, BF),
        ],
        compiler_params=pltpu.CompilerParams(vmem_limit_bytes=40 * 2**20),
        cost_estimate=pl.CostEstimate(
            flops=32 * q.size * keys * URGENT,
            transcendentals=0,
            bytes_accessed=(6 * q.size + 8 * k.size + 2 * batch * H * rows * keys) * URGENT,
        ),
        name="attend_back",
    )(do, q, k, v, p)


BIG = pltpu.CompilerParams(vmem_limit_bytes=58 * 2**20)
SPOT = pl.BlockSpec(memory_space=pl.ANY)
WHOLE = pl.BlockSpec(memory_space=pltpu.VMEM)
CHUNK = 128


def here():
    rep, row = lax.axis_index("replica"), lax.axis_index("fsdp")
    return lax.div(rep, 2), lax.rem(rep, 2), lax.div(row, 2), lax.rem(row, 2)


def flip(bit, by):
    return 1 - bit if by else bit


def pieces_of(refs, number, w, sems, act):
    x, c, _, y = here()
    rows, half = w.shape[2], w.shape[3] // 2
    dx, dc = flip(x, number // 2), flip(c, number % 2)
    halves = len(refs[0].shape) == 4

    def copy(src, dy, g):
        to = w.at[:, flip(y, dy), :, pl.ds(g * half, half)] if halves else w.at[:, flip(y, dy)]
        src = src.at[:, pl.ds(0, rows)]
        getattr(pltpu.make_async_copy(src, to, sems.at[2 * dy + g]), act)()

    if act == "wait":
        for dy in range(2):
            for g in range(2 if halves else 1):
                copy(refs[0].at[0] if halves else refs[0], dy, g)
        return
    for far in range(2):
        group = refs[4 * far : 4 * far + 4]
        if halves:
            p0, q0, p1, q1 = group

            @pl.when(dc == far)
            def _(p1=p1, q1=q1):
                copy(p1.at[dx], 0, 1)
                copy(q1.at[dx], 1, 1)

        for side in range(2):

            @pl.when((dc == far) & (dx == side))
            def _(group=group, side=side):
                if halves:
                    copy(group[side].at[0], 0, 0)
                    copy(group[side].at[1], 1, 0)
                else:
                    copy(group[2 * side], 0, 0)
                    copy(group[2 * side + 1], 1, 0)


def row_sum(v):
    return jnp.sum(v, 0, keepdims=True)


def normal(v):
    centered = v - jnp.mean(v, -1, keepdims=True)
    inverse = lax.rsqrt(jnp.mean(centered * centered, -1, keepdims=True) + EPSILON)
    return centered * inverse, inverse


def chunks(rows, step, do):
    def one(i, carry):
        do(pl.ds(pl.multiple_of(i * step, step), step))
        return carry

    lax.fori_loop(0, rows // step, one, 0)


def weight(w_ref, *lead):
    v = w_ref[lead] if lead else w_ref[...]
    return v.reshape(v.shape[-4] * v.shape[-3] * v.shape[-2], v.shape[-1])


def times(a_ref, w_ref, put):
    put(slice(None), jnp.dot(a_ref[...], weight(w_ref), preferred_element_type=F32))


def times_t(pairs, put):
    total = None
    for a_ref, w_ref in pairs:
        part = dot_nt(a_ref[...], weight(w_ref))
        total = part if total is None else total + part
    put(slice(None), total)


def loaded(m, n, count):
    return [pltpu.VMEM((4, 2, m, n), BF)] * count + [pltpu.SemaphoreType.DMA((count, 4))]


URGENT = 400


def cost(flops, *arrays):
    return pl.CostEstimate(
        flops=flops * URGENT,
        transcendentals=0,
        bytes_accessed=sum(a.size * a.dtype.itemsize for a in arrays) * URGENT,
    )


def shape(dims, dtype):
    return jax.ShapeDtypeStruct(dims, dtype)


def pack_kernel(count, *rest):
    mats, vectors, out = rest[:4], rest[4 : 4 + count], rest[-1]
    x, c, _, _ = here()
    m, n = mats[0].shape
    half = n // 2
    for number, mat in enumerate(mats):

        @pl.when(2 * x + c == number)
        def _(mat=mat):
            for g in range(2):
                out[g, :m, :] = mat[:, g * half : (g + 1) * half]

    parts = []
    for v in vectors:
        parts += [v[i : i + m].reshape(1, m) for i in range(0, v.shape[0], m)]
    parts += [jnp.zeros((1, m), BF)] * (8 * n // m - len(parts))
    row = half // m
    rows = [jnp.concatenate(parts[row * i : row * (i + 1)], 1) for i in range(16)]
    for g in range(2):
        out[g, m:, :] = jnp.concatenate(rows[8 * g : 8 * g + 8], 0)


def pack(mats, vectors):
    m, n = mats[0].shape
    return pl.pallas_call(
        partial(pack_kernel, len(vectors)),
        in_specs=[WHOLE] * (4 + len(vectors)),
        out_specs=WHOLE,
        out_shape=shape((2, m + 8, n // 2), BF),
        compiler_params=BIG,
        name="pack",
    )(*mats, *vectors)


def first_kernel(x_ref, vec_ref, *rest):
    refs, (act_ref, q_ref, k_ref, v_ref), (wq, wk, wv, sems) = rest[:8], rest[8:12], rest[12:]
    for i, w in enumerate((wq, wk, wv)):
        pieces_of(refs, i, w, sems.at[i], "start")

    def norm(rows):
        n, _ = normal(x_ref[rows, :].astype(F32))
        act_ref[rows, :] = (n * vec_ref[0:1] + vec_ref[1:2]).astype(BF)

    chunks(x_ref.shape[0], CHUNK, norm)
    for i, (w, out, bias) in enumerate(((wq, q_ref, 2), (wk, k_ref, None), (wv, v_ref, 3))):
        pieces_of(refs, i, w, sems.at[i], "wait")

        def put(lanes, v, out=out, bias=bias):
            if bias is not None:
                v = v + vec_ref[bias : bias + 1, lanes]
            out[:, lanes] = v.astype(BF)

        times(act_ref, w, put)


def first(x, vecs, unit, m):
    like = shape(x.shape, BF)
    return pl.pallas_call(
        first_kernel,
        in_specs=[WHOLE, WHOLE] + [SPOT] * 8,
        out_specs=[WHOLE] * 4,
        out_shape=[like] * 4,
        scratch_shapes=loaded(m, x.shape[1], 3),
        compiler_params=BIG,
        cost_estimate=cost(6 * x.size * x.shape[1], x, x, x, x, x, *unit),
        name="first",
    )(x, vecs, *unit)


def project_kernel(second, numbers, rows_of, a_ref, res_ref, vec_ref, *rest):
    refs = rest[:16] if second else rest[:8]
    rest = rest[len(refs) :]
    outs, (w1, *rest) = rest[: 3 if second else 2], rest[3 if second else 2 :]
    mid_ref, act_ref = outs[:2]
    sems = rest[-1]
    bias, gain, shift, bias2 = rows_of
    pieces_of(refs[:8], numbers[0], w1, sems.at[0], "start")
    if second:
        w2 = rest[0]
        pieces_of(refs[8:], numbers[1], w2, sems.at[1], "start")
    pieces_of(refs[:8], numbers[0], w1, sems.at[0], "wait")

    def put(lanes, v):
        mid_ref[:, lanes] = res_ref[:, lanes].astype(F32) + (v + vec_ref[bias : bias + 1, lanes])

    times(a_ref, w1, put)

    def norm(rows):
        n, _ = normal(mid_ref[rows, :])
        act_ref[rows, :] = (n * vec_ref[gain : gain + 1] + vec_ref[shift : shift + 1]).astype(BF)

    chunks(a_ref.shape[0], CHUNK, norm)
    if second:
        pieces_of(refs[8:], numbers[1], w2, sems.at[1], "wait")

        def put2(lanes, v):
            outs[2][:, lanes] = (v + vec_ref[bias2 : bias2 + 1, lanes]).astype(BF)

        times(act_ref, w2, put2)


def project(a, residual, vecs, rows_of, units, numbers, m, name):
    second = len(units) == 2
    refs = [r for u in units for r in u]
    return pl.pallas_call(
        partial(project_kernel, second, numbers, rows_of),
        in_specs=[WHOLE] * 3 + [SPOT] * len(refs),
        out_specs=[WHOLE] * (3 if second else 2),
        out_shape=[shape(a.shape, F32), shape(a.shape, BF)] + ([shape(a.shape, BF)] if second else []),
        scratch_shapes=loaded(m, a.shape[1], len(units)),
        compiler_params=BIG,
        cost_estimate=cost(2 * len(units) * a.size * a.shape[1], a, a, a, a, a, a, *refs[:4]),
        name=name,
    )(a, residual, vecs, *refs)


def query_kernel(bias, a_ref, vec_ref, *rest):
    refs, out_ref, (w, sems) = rest[:8], rest[8], rest[9:]
    pieces_of(refs, 0, w, sems.at[0], "start")
    pieces_of(refs, 0, w, sems.at[0], "wait")

    def put(lanes, v):
        out_ref[:, lanes] = (v + vec_ref[bias : bias + 1, lanes]).astype(BF)

    times(a_ref, w, put)


def query(a, vecs, bias, unit, m):
    return pl.pallas_call(
        partial(query_kernel, bias),
        in_specs=[WHOLE] * 2 + [SPOT] * 8,
        out_specs=WHOLE,
        out_shape=shape(a.shape, BF),
        scratch_shapes=loaded(m, a.shape[1], 1),
        compiler_params=BIG,
        cost_estimate=cost(2 * a.size * a.shape[1], a, a, *unit[:2]),
        name="query",
    )(a, vecs, *unit)


def memory_kernel(e_ref, vec_ref, *rest):
    refs, (k_ref, v_ref), (wk, wv, sems) = rest[:8], rest[8:10], rest[10:]

    @pl.when(pl.program_id(0) == 0)
    def _():
        for i, w in enumerate((wk, wv)):
            pieces_of(refs, i + 1, w, sems.at[i], "start")
        for i, w in enumerate((wk, wv)):
            pieces_of(refs, i + 1, w, sems.at[i], "wait")

    def put_k(lanes, v):
        k_ref[:, lanes] = v.astype(BF)

    def put_v(lanes, v):
        v_ref[:, lanes] = (v + vec_ref[8:9, lanes]).astype(BF)

    times(e_ref, wk, put_k)
    times(e_ref, wv, put_v)


def memory(e, vecs, unit, m, step=512):
    d = e.shape[1]
    blk = pl.BlockSpec((step, d), lambda i: (i, 0))
    return pl.pallas_call(
        memory_kernel,
        grid=(e.shape[0] // step,),
        in_specs=[blk, pl.BlockSpec(vecs.shape, lambda i: (0, 0))] + [SPOT] * 8,
        out_specs=[blk, blk],
        out_shape=[shape(e.shape, BF)] * 2,
        scratch_shapes=loaded(m, d, 2),
        compiler_params=BIG,
        cost_estimate=cost(4 * e.size * d, e, e, e, *unit),
        name="memory",
    )(e, vecs, *unit)


def memory_back_kernel(dk_ref, dv_ref, *rest):
    refs, (out_ref, sum_ref), (wk, wv, sems) = rest[:8], rest[8:10], rest[10:]

    @pl.when(pl.program_id(0) == 0)
    def _():
        for i, w in enumerate((wk, wv)):
            pieces_of(refs, i + 1, w, sems.at[i], "start")
        sum_ref[...] = jnp.zeros_like(sum_ref)
        for i, w in enumerate((wk, wv)):
            pieces_of(refs, i + 1, w, sems.at[i], "wait")

    def put(lanes, v):
        out_ref[:, lanes] = v

    times_t([(dk_ref, wk), (dv_ref, wv)], put)
    sum_ref[0:1] += row_sum(dv_ref[...].astype(F32))


def memory_back(dk, dv, unit, m, step=512):
    d = dk.shape[1]
    blk = pl.BlockSpec((step, d), lambda i: (i, 0))
    return pl.pallas_call(
        memory_back_kernel,
        grid=(dk.shape[0] // step,),
        in_specs=[blk, blk] + [SPOT] * 8,
        out_specs=[blk, pl.BlockSpec((8, d), lambda i: (0, 0))],
        out_shape=[shape(dk.shape, F32), shape((8, d), F32)],
        scratch_shapes=loaded(m, d, 2),
        compiler_params=BIG,
        cost_estimate=cost(4 * dk.size * d, dk, dk, dk, dk, *unit),
        name="memory_back",
    )(dk, dv, *unit)


def apply_norm_back(rows, dact, v, gain, residual, sums):
    n, inverse = normal(v)
    sums[0:1] += row_sum(dact * n)
    sums[1:2] += row_sum(dact)
    q = dact * gain
    mean_one = jnp.mean(q, -1, keepdims=True)
    mean_two = jnp.mean(q * n, -1, keepdims=True)
    return residual + inverse * (q - mean_one - n * mean_two)


def cross_back_kernel(dq_ref, mid_ref, dmid_ref, vec_ref, *rest):
    refs, (out_ref, low_ref, do_ref, sum_ref), (dact, w1, w2, sems) = rest[:16], rest[16:20], rest[20:]
    pieces_of(refs[:8], 0, w1, sems.at[0], "start")
    pieces_of(refs[8:], 3, w2, sems.at[1], "start")
    sum_ref[...] = jnp.zeros_like(sum_ref)
    sum_ref[2:3] = row_sum(dq_ref[...].astype(F32))
    pieces_of(refs[:8], 0, w1, sems.at[0], "wait")

    def put(lanes, v):
        dact[:, lanes] = v

    times_t([(dq_ref, w1)], put)

    def back(rows):
        total = apply_norm_back(
            rows, dact[rows, :], mid_ref[rows, :], vec_ref[5:6], dmid_ref[rows, :], sum_ref
        )
        out_ref[rows, :] = total
        low = total.astype(BF)
        low_ref[rows, :] = low
        sum_ref[3:4] += row_sum(low.astype(F32))

    chunks(dq_ref.shape[0], CHUNK, back)
    pieces_of(refs[8:], 3, w2, sems.at[1], "wait")

    def put2(lanes, v):
        do_ref[:, lanes] = v.astype(BF)

    times_t([(low_ref, w2)], put2)


def cross_back(dq, mid, dmid, vecs, cross_unit, self_unit, m):
    d = dq.shape[1]
    return pl.pallas_call(
        cross_back_kernel,
        in_specs=[WHOLE] * 4 + [SPOT] * 16,
        out_specs=[WHOLE] * 4,
        out_shape=[shape(dq.shape, F32), shape(dq.shape, BF), shape(dq.shape, BF), shape((8, d), F32)],
        scratch_shapes=[pltpu.VMEM(dq.shape, F32)] + loaded(m, d, 2),
        compiler_params=BIG,
        cost_estimate=cost(4 * dq.size * d, mid, mid, mid, dq, dq, dq, *cross_unit[:4]),
        name="cross_back",
    )(dq, mid, dmid, vecs, *cross_unit, *self_unit)


def self_back_kernel(dq_ref, dk_ref, dv_ref, x_ref, dmid_ref, vec_ref, *rest):
    refs, (out_ref, sum_ref), (dact, wq, wk, wv, sems) = rest[:8], rest[8:10], rest[10:]
    for i, w in enumerate((wq, wk, wv)):
        pieces_of(refs, i, w, sems.at[i], "start")
    sum_ref[...] = jnp.zeros_like(sum_ref)
    sum_ref[2:3] = row_sum(dq_ref[...].astype(F32))
    sum_ref[3:4] = row_sum(dv_ref[...].astype(F32))
    for i, w in enumerate((wq, wk, wv)):
        pieces_of(refs, i, w, sems.at[i], "wait")

    def put(lanes, v):
        dact[:, lanes] = v

    times_t([(dq_ref, wq), (dk_ref, wk), (dv_ref, wv)], put)

    def back(rows):
        out_ref[rows, :] = apply_norm_back(
            rows, dact[rows, :], x_ref[rows, :].astype(F32), vec_ref[0:1], dmid_ref[rows, :], sum_ref
        )

    chunks(dq_ref.shape[0], CHUNK, back)


def self_back(dq, dk, dv, x, dmid, vecs, unit, m):
    d = dq.shape[1]
    return pl.pallas_call(
        self_back_kernel,
        in_specs=[WHOLE] * 6 + [SPOT] * 8,
        out_specs=[WHOLE] * 2,
        out_shape=[shape(dq.shape, F32), shape((8, d), F32)],
        scratch_shapes=[pltpu.VMEM(dq.shape, F32)] + loaded(m, d, 3),
        compiler_params=BIG,
        cost_estimate=cost(6 * dq.size * d, dmid, dmid, dq, dq, dq, dq, *unit),
        name="self_back",
    )(dq, dk, dv, x, dmid, vecs, *unit)


def output_back_kernel(d_ref, *rest):
    refs, do_ref, (w, sems) = rest[:8], rest[8], rest[9:]
    pieces_of(refs, 3, w, sems.at[0], "start")
    pieces_of(refs, 3, w, sems.at[0], "wait")

    def put(lanes, v):
        do_ref[:, lanes] = v.astype(BF)

    times_t([(d_ref, w)], put)


def output_back(dlow, unit, m):
    d = dlow.shape[1]
    return pl.pallas_call(
        output_back_kernel,
        in_specs=[WHOLE] + [SPOT] * 8,
        out_specs=WHOLE,
        out_shape=shape(dlow.shape, BF),
        scratch_shapes=loaded(m, d, 1),
        compiler_params=BIG,
        cost_estimate=cost(2 * dlow.size * d, dlow, dlow, *unit[:2]),
        name="output_back",
    )(dlow, *unit)


def send_off(block, away, keep, dx, dc, spot, sem):
    @pl.when(dc == 1)
    def _():
        pltpu.make_async_copy(block, away.at[(dx,) + spot], sem).start()

    @pl.when(dc == 0)
    def _():
        pltpu.make_async_copy(block, keep.at[(dx,) + spot], sem).start()


def dot_tn(a, b):
    return lax.dot_general(a, b, (((0,), (0,)), ((), ())), preferred_element_type=F32)


def grads_kernel(sides, *rest):
    count = 1 + max(sides)
    left_refs, right_refs = rest[:count], rest[count : count + 4]
    away, keep, out, sems = rest[count + 4 :]
    x, c, z, y = here()
    half = out.shape[-1]
    for number, side in enumerate(sides):
        for zz in range(4):
            v = dot_tn(left_refs[side][:, zz * 256 : (zz + 1) * 256], right_refs[number][...]).astype(BF)
            for yy in range(2):
                for g in range(2):
                    out[number, g, flip(y, yy), zz] = v[yy * 128 : (yy + 1) * 128, g * half : (g + 1) * half]
        dx, dc = flip(x, number // 2), flip(c, number % 2)
        send_off(out.at[number], away, keep, dx, dc, (), sems.at[number])
    for number in range(4):
        pltpu.make_async_copy(out.at[number], keep.at[0], sems.at[number]).wait()


def grads(lefts, rights, sides, name):
    d, n = lefts[0].shape[1], rights[0].shape[1]
    dims = (2, 2, 2, 4, d // 8, n // 2)
    return pl.pallas_call(
        partial(grads_kernel, sides),
        in_specs=[WHOLE] * (len(lefts) + 4),
        out_specs=[SPOT] * 2,
        out_shape=[shape(dims, BF)] * 2,
        scratch_shapes=[pltpu.VMEM((4,) + dims[1:], BF), pltpu.SemaphoreType.DMA((4,))],
        compiler_params=BIG,
        cost_estimate=cost(2 * sum(r.size for r in rights) * d, *lefts, *rights, *rights, *rights),
        name=name,
    )(*lefts, *rights)


def sums_kernel(counts, *rest):
    ins, outs = rest[: sum(counts)], rest[sum(counts) :]
    at_in = 0
    for out, count in zip(outs, counts):
        total = ins[at_in][...].astype(F32)
        for r in ins[at_in + 1 : at_in + count]:
            total = total + r[...].astype(F32)
        out[...] = total.astype(BF).reshape(out.shape)
        at_in += count


def sums(steps, *groups):
    ins = [i for _, _, _, members in groups for i in members]
    return pl.pallas_call(
        partial(sums_kernel, tuple(len(g[3]) for g in groups)),
        grid=(steps,),
        in_specs=[pl.BlockSpec(block, to) for _, block, to in ins],
        out_specs=[pl.BlockSpec(g[1], g[2]) for g in groups],
        out_shape=[shape(g[0], BF) for g in groups],
        cost_estimate=pl.CostEstimate(
            flops=0,
            transcendentals=0,
            bytes_accessed=2 * URGENT * sum(int(np.prod(g[0])) * (1 + len(g[3])) for g in groups),
        ),
        name="sums",
    )(*[v for v, _, _ in ins])


def grads_of(left, lefts, rights, sides, name):
    return grads([left] + list(lefts), rights, sides, name)


def ffn_kernel(last, first_row, act_ref, dy_ref, mid_ref, vec_ref, *rest):
    begin = rest[:2] if last else ()
    rest = rest[len(begin) :]
    refs, rest = rest[:8], rest[8:]
    outs, rest = rest[: 4 if last else 2], rest[4 if last else 2 :]
    dbe_ref, away, keep = rest[:3]
    hid_ref, dexp_ref, acc, dact, out, we0, wd0, we1, wd1, sems, out_sems = rest[3:]
    rows, d = act_ref.shape
    half_n = d // 2
    x, c, z, y = here()
    mats = ((we0, wd0), (we1, wd1))
    for t in range(2):
        for n in range(2):
            pieces_of(refs, 2 * t + n, mats[t][n], sems.at[2 * t + n], "start")
    dbe_ref[...] = jnp.zeros_like(dbe_ref)
    if last:
        outs[3][...] = jnp.zeros_like(outs[3])
    for t in range(2):
        for n in range(2):
            pieces_of(refs, 2 * t + n, mats[t][n], sems.at[2 * t + n], "wait")
        bias = vec_ref[first_row + t : first_row + t + 1]

        def half(r, t=t, bias=bias):
            we, wd = weight(mats[t][0]), weight(mats[t][1])
            u = jnp.dot(act_ref[r, :], we, preferred_element_type=F32) + bias
            cdf = 0.5 * (1.0 + lax.erf(u * np.float32(0.5**0.5)))
            pdf = jnp.exp(-0.5 * u * u) * np.float32((2 * np.pi) ** -0.5)
            hid = (u * cdf).astype(BF)
            hid_ref[r, :] = hid
            dexp = (dot_nt(dy_ref[r, :], wd) * (cdf + u * pdf)).astype(BF)
            dexp_ref[r, :] = dexp
            dbe_ref[t : t + 1] += row_sum(dexp.astype(F32))
            down, back = jnp.dot(hid, wd, preferred_element_type=F32), dot_nt(dexp, we)
            if t == 0 and not last:
                acc[r, :], dact[r, :] = down, back
            elif t == 0:
                acc[r, :], dact[r, :] = begin[0][r, :] + down, begin[1][r, :] + back
            else:
                acc[r, :] += down
                dact[r, :] += back

        chunks(rows, 256, half)
        for number, (a_ref, b_ref) in ((2 * t, (act_ref, dexp_ref)), (2 * t + 1, (hid_ref, dy_ref))):
            for zz in range(4):
                v = dot_tn(a_ref[:, zz * 256 : (zz + 1) * 256], b_ref[...]).astype(BF)
                for yy in range(2):
                    for g in range(2):
                        part = v[yy * 128 : (yy + 1) * 128, g * half_n : (g + 1) * half_n]
                        out[number, g, flip(y, yy), zz] = part
            dx, dc = flip(x, number // 2), flip(c, number % 2)
            send_off(out.at[number], away, keep, dx, dc, (), out_sems.at[number])
    if last:
        out_ref, dmid_ref, low_ref, sum_ref = outs

        def back(r):
            mid = mid_ref[r, :]
            out_ref[r, :] = (mid + (acc[r, :] + vec_ref[12:13])).astype(BF)
            dy = dy_ref[r, :].astype(F32)
            total = apply_norm_back(r, dact[r, :], mid, vec_ref[10:11], dy, sum_ref)
            dmid_ref[r, :] = total
            low = total.astype(BF)
            low_ref[r, :] = low
            sum_ref[2:3] += row_sum(dy)
            sum_ref[3:4] += row_sum(low.astype(F32))

        chunks(rows, CHUNK, back)
    else:
        outs[0][...] = acc[...]
        outs[1][...] = dact[...]
    for number in range(4):
        pltpu.make_async_copy(out.at[number], keep.at[0], out_sems.at[number]).wait()


def ffn(act, dy, mid, vecs, unit, m, begin, first_row):
    rows, d = act.shape
    last = bool(begin)
    dims = (2, 2, 2, 4, m, d // 2)
    if last:
        heads = [shape(act.shape, BF), shape(act.shape, F32), shape(act.shape, BF), shape((8, d), F32)]
    else:
        heads = [shape(act.shape, F32)] * 2
    return pl.pallas_call(
        partial(ffn_kernel, last, first_row),
        in_specs=[WHOLE] * (4 + len(begin)) + [SPOT] * 8,
        out_specs=[WHOLE] * (len(heads) + 1) + [SPOT] * 2,
        out_shape=heads + [shape((8, d), F32)] + [shape(dims, BF)] * 2,
        scratch_shapes=[
            pltpu.VMEM((rows, d), BF),
            pltpu.VMEM((rows, d), BF),
            pltpu.VMEM((rows, d), F32),
            pltpu.VMEM((rows, d), F32),
            pltpu.VMEM((4,) + dims[1:], BF),
        ]
        + loaded(m, d, 4)
        + [pltpu.SemaphoreType.DMA((4,))],
        compiler_params=BIG,
        cost_estimate=cost(24 * act.size * d, *unit, *unit, mid, mid),
        name="ffn",
    )(act, dy, mid, vecs, *begin, *unit)


def finish_kernel(count, *rest):
    units, outs, held = [rest[3 * i : 3 * i + 3] for i in range(count)], rest[3 * count : -1], rest[-1]
    x, c, _, _ = here()
    m, n = units[0][0].shape
    for i, (own_ref, x_ref, core_ref) in enumerate(units):
        held[0], held[2] = own_ref[...], x_ref[...]
        held[1], held[3] = core_ref[0], core_ref[1]
        for number in range(4):
            j = flip(x, number // 2) * 2 + flip(c, number % 2)
            v = held[j].astype(F32)
            t = 2 * i + number // 2
            if count == 1:
                outs[number][...] = v
            elif number % 2:
                outs[1][t * m : (t + 1) * m] = v
            else:
                for f in range(n // 128):
                    to = (f * 4 + t) * 128
                    outs[0][:, to : to + 128] = v[:, f * 128 : (f + 1) * 128]


def finish(own, from_x, from_core, parts=()):
    units = ((own, from_x, from_core), *parts)
    m, n = own.shape
    dims = [(m, n)] * 4 if len(units) == 1 else [(m, 4 * n), (4 * m, n)]
    return pl.pallas_call(
        partial(finish_kernel, len(units)),
        in_specs=[WHOLE] * (3 * len(units)),
        out_specs=[WHOLE] * len(dims),
        out_shape=[shape(s, F32) for s in dims],
        scratch_shapes=[pltpu.VMEM((4, m, n), BF)],
        compiler_params=BIG,
        cost_estimate=cost(0, *[v for u in units for v in u] * 3),
        name="finish",
    )(*[v for u in units for v in u])


def product(left, right):
    return jnp.dot(left, right, preferred_element_type=F32)


def product_nt(left, right):
    return lax.dot_general(
        left, right, (((1,), (1,)), ((), ())), preferred_element_type=F32
    )


def moments(values):
    average = jnp.mean(values, -1, keepdims=True)
    centered = values - average
    variance = jnp.mean(centered * centered, -1, keepdims=True)
    inverse = lax.rsqrt(variance + EPSILON)
    return (centered * inverse, inverse)


def norm_back(grad_out, normed, inverse, gain_vec):
    gain_grad = jnp.sum(grad_out * normed, 0)
    shift_grad = jnp.sum(grad_out, 0)
    scaled = grad_out * gain_vec
    mean_one = jnp.mean(scaled, -1, keepdims=True)
    mean_two = jnp.mean(scaled * normed, -1, keepdims=True)
    return (inverse * (scaled - mean_one - normed * mean_two), gain_grad, shift_grad)


def gelu_both(u):
    cdf = 0.5 * (1.0 + lax.erf(u * np.float32(0.5**0.5)))
    pdf = jnp.exp(-0.5 * u * u) * np.float32((2 * np.pi) ** -0.5)
    return (u * cdf).astype(BF), (cdf + u * pdf).astype(BF)


def body(
    groups,
    rows,
    decoder_input,
    encoder_out,
    prefix_length,
    output_grad,
    self_query,
    self_key,
    self_value,
    self_output,
    selfquery_bias,
    selfvalue_bias,
    self_attention_output_bias,
    cross_query,
    cross_key,
    cross_value,
    cross_output,
    crossquery_bias,
    crossvalue_bias,
    crossoutput_bias,
    expand_weight,
    expand_bias,
    down_projection_weight,
    reduce_bias,
    selfnorm_gain,
    selfnorm_bias,
    crossnorm_gain,
    crossnorm_bias,
    finalnorm_gain,
    finalnorm_bias,
):
    place = Place(groups, rows)
    batch, seq, d = decoder_input.shape
    m = self_query.shape[0]
    ff = expand_weight.shape[1]
    fl = ff // rows // 2
    k4 = ff // d

    small = [
        selfnorm_gain, selfnorm_bias, selfquery_bias, selfvalue_bias, self_attention_output_bias,
        crossnorm_gain, crossnorm_bias, crossquery_bias, crossvalue_bias, crossoutput_bias,
        finalnorm_gain, finalnorm_bias, reduce_bias,
    ]
    packed = jnp.concatenate([jnp.stack(small), expand_bias.reshape(k4, m)])
    vecs = gather_vectors(place, packed).astype(F32)
    (g1, b1, bq, bv, bo, g2, b2, bcq, bcv, bco, g3, b3, br) = [
        vecs[:, i].reshape(d) for i in range(13)
    ]
    be = vecs[:, 13:].reshape(rows, 2, fl)

    expand_halves = [
        expand_weight.reshape(m, rows, 2, fl)[:, :, h].reshape(m, rows * fl) for h in range(2)
    ]
    down_halves = [down_projection_weight[h * fl : (h + 1) * fl] for h in range(2)]

    lane, ring_lane = Lane(4), Lane(2)
    gathers = [
        Gather(place, lane, ring_lane, shard, split)
        for shard, split in (
            (jnp.concatenate([self_query, self_key], 1), True),
            (self_value, False),
            (jnp.concatenate([cross_key, cross_value], 1), True),
            (self_output, False),
            (jnp.concatenate([cross_query, cross_output], 1), True),
            (expand_halves[0], True),
            (expand_halves[1], True),
            (down_halves[0], False),
            (down_halves[1], True),
        )
    ]
    run_steps(gathers)
    w_qk, w_v, w_ckv, w_o, w_cqo, *w_ff = [u.v for u in gathers]
    w_e, w_d = w_ff[:2], w_ff[2:]

    x = decoder_input.reshape(batch * seq, d).astype(F32)
    e = encoder_out.reshape(-1, d)
    dy = output_grad.reshape(batch * seq, d)

    n1, i1 = moments(x)
    act1 = (n1 * g1 + b1).astype(BF)
    qk = product(act1, w_qk)
    q = (qk[:, :d] + bq).astype(BF)
    k = qk[:, d:].astype(BF)
    v = (product(act1, w_v) + bv).astype(BF)
    o, p = attend(q, k, v, prefix_length, batch, True)
    mid1 = x + (product(o, w_o) + bo)
    n2, i2 = moments(mid1)
    act2 = (n2 * g2 + b2).astype(BF)
    w_cq, w_co = w_cqo[:, :d], w_cqo[:, d:]
    cq = (product(act2, w_cq) + bcq).astype(BF)
    ckv = product(e, w_ckv)
    ck = ckv[:, :d].astype(BF)
    cv = (ckv[:, d:] + bcv).astype(BF)
    co, cp = attend(cq, ck, cv, prefix_length, batch, False)
    mid2 = mid1 + (product(co, w_co) + bco)
    n3, i3 = moments(mid2)
    act3 = (n3 * g3 + b3).astype(BF)
    hidden, slope = [], []
    for h in range(2):
        hid, slo = gelu_both(product(act3, w_e[h]) + be[:, h].reshape(-1))
        hidden.append(hid)
        slope.append(slo)
    layer_out = (mid2 + (product(hidden[0], w_d[0]) + product(hidden[1], w_d[1]) + br)).astype(BF)

    scatter = partial(Scatter, place, lane, ring_lane)
    dyf = dy.astype(F32)
    g_down = [scatter(hidden[0], dy, True), scatter(hidden[1], dy, False)]
    dexp = [(product_nt(dy, w_d[h]) * slope[h].astype(F32)).astype(BF) for h in range(2)]
    g_exp = [scatter(act3, dexp[0], True), scatter(act3, dexp[1], False)]
    dact3 = product_nt(dexp[0], w_e[0]) + product_nt(dexp[1], w_e[1])
    dn, gg3, gb3 = norm_back(dact3, n3, i3, g3)
    dmid2 = dyf + dn
    dcross = dmid2.astype(BF)
    g_co = scatter(co, dcross, True)
    dco = product_nt(dcross, w_co).astype(BF)
    dcq, dck, dcv = attend_back(dco, cq, ck, cv, cp, batch)
    g_ck = scatter(e, dck, True)
    g_cv = scatter(e, dcv, False)
    g_cq = scatter(act2, dcq, False)
    encoder_grad = product_nt(jnp.concatenate([dck, dcv], 1), w_ckv)
    dn, gg2, gb2 = norm_back(product_nt(dcq, w_cq), n2, i2, g2)
    dmid1 = dmid2 + dn
    dself = dmid1.astype(BF)
    g_so = scatter(o, dself, True)
    dao = product_nt(dself, w_o).astype(BF)
    dq, dk, dv = attend_back(dao, q, k, v, p, batch)
    g_sv = scatter(act1, dv, False)
    g_sq = scatter(act1, dq, True)
    g_sk = scatter(act1, dk, True)
    dact1 = product_nt(jnp.concatenate([dq, dk], 1), w_qk) + product_nt(dv, w_v)
    dn, gg1, gb1 = norm_back(dact1, n1, i1, g1)
    input_grad = dmid1 + dn

    def column_sum(t):
        return jnp.sum(t.astype(F32), 0)

    dbe = jnp.stack([column_sum(t).reshape(rows, fl) for t in dexp], 1).reshape(rows, k4, m)
    early = [
        gg2, gb2, column_sum(dcq), column_sum(dcv), column_sum(dcross),
        gg3, gb3, column_sum(dy), column_sum(dself),
    ]
    early = jnp.concatenate([jnp.stack([t.reshape(rows, m) for t in early], 1), dbe], 1)
    late = [gg1, gb1, column_sum(dq), column_sum(dv)]
    late = jnp.stack([t.reshape(rows, m) for t in late], 1)

    first = g_down + g_exp + [g_co, g_cv, g_ck, g_cq, g_so]
    second = [g_sv, g_sq, g_sk]
    run_steps(first + second)
    early = scatter_vectors(place, lane, ring_lane, early)
    (*g_ff, g_co, g_cv, g_ck, g_cq, g_so) = finish_all(place, lane, first)
    g_down, g_exp = g_ff[:2], g_ff[2:]
    late = scatter_vectors(place, lane, ring_lane, late)
    g_sv, g_sq, g_sk = finish_all(place, lane, second)

    g_exp = jnp.stack([t.reshape(m, rows, fl) for t in g_exp], 2).reshape(m, ff)
    g_down = jnp.concatenate(g_down, 0)
    return (
        layer_out.reshape(batch, seq, d),
        input_grad.reshape(batch, seq, d),
        encoder_grad.reshape(encoder_out.shape),
        g_sq, g_sk, g_sv, g_so,
        late[2], late[3], early[8],
        g_cq, g_ck, g_cv, g_co,
        early[2], early[3], early[4],
        g_exp, early[9:].reshape(-1), g_down, early[7],
        late[0], late[1], early[0], early[1], early[5], early[6],
    )


class Order:
    def __init__(self):
        self.sent, self.ran, self.open = [], [], []

    def send(self, move, v, hold=2):
        v = self.see(v)
        got = move(v)
        self.sent.append(v)
        self.open.append([hold, got])
        return got

    def see(self, v):
        return lax.optimization_barrier((v, *self.ran))[0] if self.ran else v

    def run(self, kernel, v, *rest, **named):
        due = [got for hold, got in self.open if hold == 0]
        self.open = [[hold - 1, got] for hold, got in self.open if hold > 0]
        before = (*self.sent, *self.ran, *due)
        if before:
            v, *_ = lax.optimization_barrier((v, *before))
        out = kernel(v, *rest, **named)
        self.sent, self.ran = [], [out[0] if isinstance(out, (list, tuple)) else out]
        return out


class HalfUnit:
    def __init__(self, place, order, piece):
        self.place, self.order, self.piece = place, order, piece

    def ring(self):
        a = self.order.send(partial(ring_gather, self.place), self.piece)
        self.a0, self.a1 = a[:, 0], a[:, 1]

    def one(self):
        self.p0 = jnp.stack([self.a0, self.order.send(self.place.pair, self.a0)])
        self.p1 = jnp.stack([self.a1, self.order.send(self.place.across, self.a1)])

    def two(self):
        self.q0 = self.order.send(self.place.across, self.p0)
        self.q1 = self.order.send(self.place.pair, self.p1)
        self.c0 = self.order.send(self.place.core, self.p0)
        self.c1 = self.order.send(self.place.core, self.p1)

    def core(self):
        d0 = self.order.send(self.place.core, self.q0)
        d1 = self.order.send(self.place.core, self.q1)
        self.refs = (self.p0, self.q0, self.p1, self.q1, self.c0, d0, self.c1, d1)


class Unit:
    def __init__(self, place, order, piece, flat):
        self.place, self.order, self.piece, self.flat = place, order, piece, flat

    def ring(self):
        self.a = self.order.send(partial(ring_gather, self.place), self.piece)

    def pair(self):
        self.b = self.order.send(self.place.pair, self.order.see(self.a))

    def across(self):
        self.ax = self.order.send(self.place.across, self.order.see(self.a))

    def near(self):
        self.ca = self.order.send(self.place.core, self.order.see(self.a), 1)

    def two(self):
        see, send = self.order.see, self.order.send
        if self.flat:
            self.bx = send(self.place.pair, see(self.ax))
        else:
            self.bx = send(self.place.across, see(self.b))

    def both(self):
        see, send = self.order.see, self.order.send
        self.cb, self.cax = send(self.place.core, see(self.b), 1), send(self.place.core, see(self.ax), 1)

    def core(self):
        far = self.order.send(self.place.core, self.order.see(self.bx))
        self.refs = (self.a, self.b, self.ax, self.bx, self.ca, self.cb, self.cax, far)


class Sum:
    def __init__(self, place, order, away, keep):
        self.place, self.order = place, order
        self.away, self.keep = away, keep

    def core(self):
        self.came = self.order.send(self.place.core, self.away)

    def one(self):
        see, k = self.order.see, self.keep
        self.came = see(self.came)
        block, dims = (None, None, None) + k.shape[3:], k.shape[2:]
        half = (None,) + dims[1:]
        first, second = (lambda i: (1, 0, i, 0, 0, 0)), (lambda i: (i, 1, 1, 0, 0, 0))
        to = lambda i: (i, 0, 0, 0)
        to_x, to_y = sums(
            2,
            (dims, half, to, [(k, block, first), (self.came, block, first)]),
            (dims, half, to, [(k, block, second), (self.came, block, second)]),
        )
        self.from_x = self.order.send(self.place.across, to_x)
        self.from_y = self.order.send(self.place.pair, to_y)

    def rest(self, name, extra):
        k, r = self.keep, self.came
        _, m, half = k.shape[3:]
        block, part = (None, None, None, 2, m, half), (None, 2, m, half)
        first = (lambda i: (0, 0, 1, i, 0, 0)) if name == "go" else (lambda i: (0, 0, 0, i, 0, 0))
        second = (lambda i: (1, 1, 0, i, 0, 0)) if name == "go" else (lambda i: (0, 1, 0, i, 0, 0))
        side = 1 if name == "go" else 0
        third = lambda i: (side, i, 0, 0)
        plain = lambda i: (i, 0, 0)
        groups = []
        for at_k, came, more in ((first, self.from_x, extra[:1]), (second, self.from_y, extra[1:])):
            members = [(k, block, at_k), (r, block, at_k), (came, part, third)]
            members += [(v, (2, m, half), plain) for v in more]
            groups.append(((4, m, half), (2, m, half), plain, members))
        return sums(2, *groups)

    def two(self):
        self.from_x, self.from_y = self.order.see(self.from_x), self.order.see(self.from_y)
        to_y, to_x = self.rest("go", [])
        self.next_y = self.order.send(self.place.pair, to_y)
        self.next_x = self.order.send(self.place.across, to_x)

    def ring(self):
        see = self.order.see
        first, second = self.rest("stay", [see(self.next_y), see(self.next_x)])
        self.own = self.order.send(partial(ring_sum, self.place), jnp.concatenate([first, second], 2))

    def last_x(self):
        self.own = self.order.see(self.own)
        self.own_x = self.order.send(self.place.across, self.own)

    def last_core(self):
        came = self.order.send(self.place.core, jnp.stack([self.own, self.order.see(self.own_x)]))
        self.parts = (self.own, self.own_x, came)


def fast_body(
    groups,
    rows,
    decoder_input,
    encoder_out,
    prefix_length,
    output_grad,
    self_query,
    self_key,
    self_value,
    self_output,
    selfquery_bias,
    selfvalue_bias,
    self_attention_output_bias,
    cross_query,
    cross_key,
    cross_value,
    cross_output,
    crossquery_bias,
    crossvalue_bias,
    crossoutput_bias,
    expand_weight,
    expand_bias,
    down_projection_weight,
    reduce_bias,
    selfnorm_gain,
    selfnorm_bias,
    crossnorm_gain,
    crossnorm_bias,
    finalnorm_gain,
    finalnorm_bias,
):
    place = Place(groups, rows)
    batch, seq, d = decoder_input.shape
    m = self_query.shape[0]
    ff = expand_weight.shape[1]
    rank = 2 * place.x + place.c
    order = Order()

    small = [
        selfnorm_gain, selfnorm_bias, selfquery_bias, selfvalue_bias, self_attention_output_bias,
        crossnorm_gain, crossnorm_bias, crossquery_bias, crossvalue_bias, crossoutput_bias,
        finalnorm_gain, finalnorm_bias, reduce_bias, expand_bias,
    ]
    count = 13 + ff // d

    def pick(*shards):
        return at(jnp.stack(shards), rank)

    u_self = HalfUnit(place, order, pack((self_query, self_key, self_value, self_output), small))
    u_self.ring()
    later = (cross_query, cross_key, cross_value, cross_output, expand_weight, down_projection_weight)
    *later, _ = lax.optimization_barrier((*later, u_self.a0))
    w_e = later[4].reshape(m, rows, 4, -1).transpose(2, 0, 1, 3).reshape(4, m, d)
    w_d = later[5].reshape(4, m, d)
    unit = partial(Unit, place, order)
    u_cross = unit(pick(*later[:4]), True)
    u_low = unit(pick(w_e[0], w_d[0], w_e[1], w_d[1]), False)
    u_high = unit(pick(w_e[2], w_d[2], w_e[3], w_d[3]), True)

    x = decoder_input.reshape(batch * seq, d)
    e = encoder_out.reshape(-1, d)
    dy = output_grad.reshape(batch * seq, d)
    run = order.run

    u_self.one()
    u_cross.ring()
    u_self.two()
    u_self.core()
    u_low.ring()
    u_cross.pair()
    u_cross.across()
    u_cross.near()
    self_w = u_self.refs
    both = jnp.stack([v[:, :, m:] for v in (u_self.p0, jnp.stack([u_self.p1[0], u_self.q1[0]]))])
    both = both.transpose(2, 1, 0, 3, 4)
    both = jnp.where(place.y == 0, both, both[:, ::-1]).reshape(rows, -1)
    vecs = both[:, : count * m].reshape(rows, count, m).transpose(1, 0, 2).reshape(count, d).astype(F32)
    act1, q, k, v = run(first, x, vecs, self_w, m)
    o, p = run(attend, q, k, v, prefix_length, batch, True)
    u_cross.two()
    u_low.across()
    u_cross.both()
    u_high.ring()
    mid1, act2 = run(project, o, x, vecs, (4, 5, 6, None), (self_w,), (3,), m, "self_out")
    u_low.pair()
    u_low.near()
    u_cross.core()
    cross_w = u_cross.refs
    ck, cv = run(memory, e, vecs, cross_w, m)
    cq = run(query, act2, vecs, 7, cross_w, m)
    u_high.across()
    u_high.pair()
    u_low.two()
    co, cp = run(attend, cq, ck, cv, prefix_length, batch, False)
    u_high.two()
    u_low.both()
    u_high.near()
    mid2, act3 = run(project, co, mid1, vecs, (9, 10, 11, None), (cross_w,), (3,), m, "cross_out")
    u_low.core()
    low_w = u_low.refs
    u_high.both()

    *begin, dbe_low, away, keep = run(ffn, act3, dy, mid2, vecs, low_w, m, (), 13)
    total = partial(Sum, place, order)
    g_low = total(away, keep)
    u_high.core()
    g_low.core()
    layer_out, dmid2, dcross, sums3, dbe_high, away, keep = run(
        ffn, act3, dy, mid2, vecs, u_high.refs, m, tuple(begin), 15
    )
    g_high = total(away, keep)
    g_low.one()
    g_high.core()
    dco = run(output_back, dcross, cross_w, m)
    dcq, dck, dcv = run(attend_back, dco, cq, ck, cv, cp, batch)
    g_high.one()
    g_cross = total(*run(grads_of, act2, [e, co], [dcq, dck, dcv, dcross], (0, 1, 1, 2), "cross_grads"))
    g_low.two()
    g_cross.core()
    dmid1, dself, dao, sums2 = run(cross_back, dcq, mid1, dmid2, vecs, cross_w, self_w, m)
    g_cross.one()
    dq, dk, dv = run(attend_back, dao, q, k, v, p, batch)
    g_high.two()
    g_low.ring()
    g_self = total(*run(grads_of, act1, [o], [dq, dk, dv, dself], (0, 0, 0, 1), "self_grads"))
    g_self.core()
    input_grad, sums1 = run(self_back, dq, dk, dv, x, dmid1, vecs, self_w, m)

    def by_shard(v):
        return v.reshape(-1, rows, m).transpose(1, 0, 2)

    g_self.one()
    g_cross.two()
    g_high.ring()
    encoder_grad, sums_e = run(memory_back, dck, dcv, cross_w, m)
    dbe = jnp.concatenate([dbe_low[:2], dbe_high[:2]])
    vec = by_shard(jnp.concatenate([sums1[:4], sums2[:4], sums3[:4], sums_e[:1], dbe]))
    vec = (vec.astype(BF).astype(F32) + order.send(place.core, vec.astype(BF)).astype(F32)).astype(BF)
    g_low.last_x()
    vec = (vec.astype(F32) + order.send(place.across, vec).astype(F32)).astype(BF)
    g_self.two()
    g_cross.ring()
    g_high.last_x()
    g_low.last_core()
    g_high.last_core()
    vec = vec.reshape((place.ring, 2) + vec.shape[1:])
    came = order.send(place.pair, at(vec, 1 - place.y, 1))
    vec = (at(vec, place.y, 1).astype(F32) + came.astype(F32)).astype(BF)
    g_self.ring()
    g_cross.last_x()
    vec = order.send(partial(ring_sum, place), vec).astype(F32)
    g_expand, g_down = run(finish, *g_low.parts, parts=(g_high.parts,))
    g_cross.last_core()
    g_self.last_x()
    g_cq, g_ck, g_cv, g_co = run(finish, *g_cross.parts)
    g_self.last_core()
    g_sq, g_sk, g_sv, g_so = run(finish, *g_self.parts)
    return (
        layer_out.reshape(batch, seq, d),
        input_grad.reshape(batch, seq, d),
        encoder_grad.reshape(encoder_out.shape),
        g_sq, g_sk, g_sv, g_so,
        vec[2], vec[3], vec[7],
        g_cq, g_ck, g_cv, g_co,
        vec[6], vec[12], vec[11],
        g_expand, vec[13:].reshape(-1), g_down, vec[10],
        vec[0], vec[1], vec[4], vec[5], vec[8], vec[9],
    )


def solution(mesh):
    groups, rows = mesh.shape["replica"], mesh.shape["fsdp"]
    data = P(("replica", "fsdp"), None, None)
    mat, vec = P("fsdp", None), P("fsdp")
    weights = (
        (mat,) * 4 + (vec,) * 3 + (mat,) * 4 + (vec,) * 3 + (mat, vec, mat, vec) + (vec,) * 6
    )
    return jax.shard_map(
        partial(fast_body if rows == 8 else body, groups, rows),
        mesh=mesh,
        in_specs=(data, data, P(("replica", "fsdp")), data) + weights,
        out_specs=(data, data, data) + weights,
        check_vma=False,
    )
```

```python
from functools import partial

import jax
import jax.numpy as jnp
import numpy as np
from jax import lax
from jax.experimental import pallas as pl
from jax.experimental.pallas import tpu as pltpu
from jax.sharding import PartitionSpec as P

H = 16
EPSILON = 1e-05
MASKED = -1e30
BF = jnp.bfloat16
F32 = jnp.float32


class Place:
    def __init__(self, groups, rows):
        self.groups = groups
        self.rows = rows
        self.ring = rows // 2
        rep = lax.axis_index("replica")
        row = lax.axis_index("fsdp")
        self.c = lax.rem(rep, 2)
        self.x = lax.div(rep, 2)
        self.y = lax.rem(row, 2)
        self.z = lax.div(row, 2)

    def core(self, v):
        return lax.ppermute(v, "replica", [(i, i ^ 1) for i in range(self.groups)])

    def across(self, v):
        return lax.ppermute(v, "replica", [(i, i ^ 2) for i in range(self.groups)])

    def pair(self, v):
        return lax.ppermute(v, "fsdp", [(i, i ^ 1) for i in range(self.rows)])

    def next(self, v):
        return lax.ppermute(v, "fsdp", [(i, (i + 2) % self.rows) for i in range(self.rows)])

    def ring_members(self):
        return [[2 * k + side for k in range(self.ring)] for side in range(2)]


def at(v, i, axis=0):
    return lax.dynamic_index_in_dim(v, i, axis, keepdims=False)


class Lane:
    def __init__(self, width):
        self.width = width
        self.past = []

    def __call__(self, send, v):
        if len(self.past) >= self.width:
            v, _ = lax.optimization_barrier((v, self.past[-self.width]))
        got = send(v)
        self.past.append(got)
        return got


def ring_gather(place, piece):
    if place.ring <= 4:
        copies = jnp.broadcast_to(piece[None], (place.ring,) + piece.shape)
        return lax.all_to_all(copies, "fsdp", 0, 0, axis_index_groups=place.ring_members())
    return lax.all_gather(piece, "fsdp", axis_index_groups=place.ring_members())


def order_kernel(ring, split, mine, theirs, out, sems):
    rep = lax.axis_index("replica")
    c, x = lax.rem(rep, 2), lax.div(rep, 2)
    y = lax.rem(lax.axis_index("fsdp"), 2)
    copies = []
    for dc, block in enumerate((mine, theirs)):
        cc = 1 - c if dc else c
        for dx in range(2 if split else 1):
            for dy in range(2):
                yy = 1 - y if dy else y
                for z in range(ring):
                    if split:
                        xx = 1 - x if dx else x
                        src, dst = block.at[dx, dy, z], out.at[z, yy, xx, cc]
                    else:
                        src, dst = block.at[dy, z], out.at[z, yy, cc]
                    copies.append(pltpu.make_async_copy(src, dst, sems.at[len(copies)]))
    for copy in copies:
        copy.start()
    for copy in copies:
        copy.wait()


def in_order(place, split, mine, theirs):
    ring, rows, n = mine.shape[-3:]
    dims = (ring, 2, 2, 2) if split else (ring, 2, 2)
    if rows % 16 == 0:
        count = 2 * mine.size // (rows * n)
        out = pl.pallas_call(
            partial(order_kernel, ring, split),
            out_shape=jax.ShapeDtypeStruct(dims + (rows, n), mine.dtype),
            in_specs=[pl.BlockSpec(memory_space=pl.ANY)] * 2,
            out_specs=pl.BlockSpec(memory_space=pltpu.VMEM),
            scratch_shapes=[pltpu.SemaphoreType.DMA((count,))],
            cost_estimate=pl.CostEstimate(
                flops=0, transcendentals=0, bytes_accessed=4 * count * rows * n
            ),
            name="order",
        )(mine, theirs)
    else:
        both = jnp.stack([mine, theirs])
        at_c = (place.c, 1 - place.c)
        both = jnp.stack([at(both, i, 0) for i in at_c])
        if split:
            both = jnp.stack([at(both, i, 1) for i in (place.x, 1 - place.x)], 1)
        both = jnp.stack([at(both, i, both.ndim - 4) for i in (place.y, 1 - place.y)], both.ndim - 4)
        out = jnp.transpose(both, (3, 2, 1, 0, 4, 5) if split else (2, 1, 0, 3, 4))
    return out.reshape(-1, n)


class Gather:
    def __init__(self, place, lane, ring_lane, shard, split):
        self.place, self.lane, self.ring_lane, self.split = place, lane, ring_lane, split
        m, n = shard.shape
        if split:
            self.v = at(shard.reshape(4, m // 4, n), 2 * place.x + place.c)
        else:
            self.v = at(shard.reshape(2, m // 2, n), place.c)
        self.steps = [self.ring, self.pair] + ([self.across] if split else []) + [self.core]

    def ring(self):
        self.v = self.ring_lane(partial(ring_gather, self.place), self.v)

    def pair(self):
        self.v = jnp.stack([self.v, self.lane(self.place.pair, self.v)])

    def across(self):
        self.v = jnp.stack([self.v, self.lane(self.place.across, self.v)])

    def core(self):
        self.v = in_order(self.place, self.split, self.v, self.lane(self.place.core, self.v))


def run_steps(units):
    last = max(i + len(u.steps) for i, u in enumerate(units))
    for t in range(last):
        for i, u in enumerate(units):
            if 0 <= t - i < len(u.steps):
                u.steps[t - i]()


def gather_vectors(place, packed):
    a = ring_gather(place, packed)
    b = place.pair(a)
    both = jnp.stack([jnp.where(place.y == 0, a, b), jnp.where(place.y == 0, b, a)], 1)
    return both.reshape((place.rows,) + packed.shape)


def product_t(left, right):
    return lax.dot_general(
        left, right, (((0,), (0,)), ((), ())), preferred_element_type=F32
    )


def columns(v, k, i):
    w = v.shape[1] // k
    return lax.dynamic_slice(v, (0, i * w), (v.shape[0], w))


def join2(own, other, bit):
    first = jnp.where(bit == 0, own, other)
    second = jnp.where(bit == 0, other, own)
    return jnp.concatenate([first, second], -1)


def ring_sum(place, parts):
    if place.ring <= 4:
        came = lax.all_to_all(parts, "fsdp", 0, 0, axis_index_groups=place.ring_members())
        return jnp.sum(came.astype(F32), 0).astype(BF)
    return lax.psum_scatter(
        parts, "fsdp", scatter_dimension=0, axis_index_groups=place.ring_members()
    )


class Scatter:
    def __init__(self, place, lane, ring_lane, left, right, split):
        self.place, self.lane, self.ring_lane, self.split = place, lane, ring_lane, split
        self.left, self.right = left, right
        self.steps = [self.core] + ([self.across] if split else []) + [self.pair, self.ring]

    def core(self):
        c = self.place.c
        away = product_t(self.left, columns(self.right, 2, 1 - c)).astype(BF)
        self.right = columns(self.right, 2, c)
        self.came = self.lane(self.place.core, away)

    def across(self):
        x = self.place.x
        away = product_t(self.left, columns(self.right, 2, 1 - x))
        away = (away + columns(self.came, 2, 1 - x).astype(F32)).astype(BF)
        self.right, self.came = columns(self.right, 2, x), columns(self.came, 2, x)
        self.came_x = self.lane(self.place.across, away)

    def pair(self):
        part = product_t(self.left, self.right) + self.came.astype(F32)
        if self.split:
            part = part + self.came_x.astype(F32)
        part = part.astype(BF)
        part = part.reshape(self.place.ring, 2, -1, part.shape[1])
        y = self.place.y
        came = self.lane(self.place.pair, at(part, 1 - y, 1))
        self.kept = (at(part, y, 1).astype(F32) + came.astype(F32)).astype(BF)

    def ring(self):
        self.own = self.ring_lane(partial(ring_sum, self.place), self.kept)


def finish_all(place, lane, units):
    flat = [u.own.reshape(-1, 128) for u in units]
    sizes = [f.shape[0] for f in flat]
    own = jnp.concatenate(flat)
    came = lane(place.across, own)
    pieces, at_row = [], 0
    for u, size in zip(units, sizes):
        mine, other = own[at_row : at_row + size], came[at_row : at_row + size]
        at_row += size
        mine, other = mine.reshape(u.own.shape), other.reshape(u.own.shape)
        if u.split:
            pieces.append(join2(mine, other, place.x))
        else:
            pieces.append((mine.astype(F32) + other.astype(F32)).astype(BF))
    own = jnp.concatenate([p.reshape(-1, 128) for p in pieces])
    came = lane(place.core, own)
    out, at_row = [], 0
    for p in pieces:
        size = p.size // 128
        out.append(join2(p, came[at_row : at_row + size].reshape(p.shape), place.c).astype(F32))
        at_row += size
    return out


def scatter_vectors(place, lane, ring_lane, v):
    own = v.astype(BF)
    own = (own.astype(F32) + lane(place.core, own).astype(F32)).astype(BF)
    own = (own.astype(F32) + lane(place.across, own).astype(F32)).astype(BF)
    own = own.reshape((place.ring, 2) + own.shape[1:])
    came = lane(place.pair, at(own, 1 - place.y, 1))
    own = (at(own, place.y, 1).astype(F32) + came.astype(F32)).astype(BF)
    return ring_lane(partial(ring_sum, place), own).astype(F32)


PAIR = 128


def half_masks(rows):
    lane = lax.broadcasted_iota(jnp.int32, (rows, PAIR), 1)
    return (lane < PAIR // 2, lane >= PAIR // 2)


def dot_nt(a, b):
    return lax.dot_general(a, b, (((1,), (1,)), ((), ())), preferred_element_type=F32)


def attend_kernel(masked, scale, prefix_ref, q_ref, k_ref, v_ref, o_ref, p_ref):
    rows, keys = q_ref.shape[0], k_ref.shape[0]
    masks = half_masks(rows)
    if masked:
        i = lax.broadcasted_iota(jnp.int32, (rows, keys), 0)
        j = lax.broadcasted_iota(jnp.int32, (rows, keys), 1)
        allowed = (j <= i) | (j < prefix_ref[pl.program_id(0)])
    for pair in range(q_ref.shape[1] // PAIR):
        lanes = slice(pair * PAIR, (pair + 1) * PAIR)
        q, k, v = q_ref[:, lanes], k_ref[:, lanes], v_ref[:, lanes]
        both = []
        for h in range(2):
            s = dot_nt(jnp.where(masks[h], q, jnp.zeros_like(q)), k)
            if masked:
                s = jnp.where(allowed, s, MASKED)
            e = jnp.exp((s - jnp.max(s, -1, keepdims=True)) * scale)
            p = (e * (1.0 / jnp.sum(e, -1, keepdims=True))).astype(BF)
            p_ref[2 * pair + h] = p
            both.append(jnp.dot(p, v, preferred_element_type=F32))
        o_ref[:, lanes] = jnp.where(masks[0], both[0], both[1]).astype(BF)


def attend(q, k, v, prefix, batch, masked, group=4):
    rows, keys, d = q.shape[0] // batch, k.shape[0] // batch, q.shape[1]
    wide = group * d // H
    spec = lambda n: pl.BlockSpec((n, wide), lambda b, g, *_: (b, g))
    return pl.pallas_call(
        partial(attend_kernel, masked, (d // H) ** -0.5),
        grid_spec=pltpu.PrefetchScalarGridSpec(
            num_scalar_prefetch=1,
            grid=(batch, H // group),
            in_specs=[spec(rows), spec(keys), spec(keys)],
            out_specs=[
                spec(rows),
                pl.BlockSpec((None, group, rows, keys), lambda b, g, *_: (b, g, 0, 0)),
            ],
        ),
        out_shape=[
            jax.ShapeDtypeStruct(q.shape, BF),
            jax.ShapeDtypeStruct((batch, H, rows, keys), BF),
        ],
        compiler_params=pltpu.CompilerParams(vmem_limit_bytes=40 * 2**20),
        cost_estimate=pl.CostEstimate(
            flops=16 * q.size * keys * URGENT,
            transcendentals=0,
            bytes_accessed=(4 * q.size + 4 * k.size + 2 * batch * H * rows * keys) * URGENT,
        ),
        name="attend",
    )(prefix, q, k, v)


def attend_back_kernel(scale, do_ref, q_ref, k_ref, v_ref, p_ref, dq_ref, dk_ref, dv_ref):
    rows = q_ref.shape[0]
    half = PAIR // 2
    masks = half_masks(rows)
    for pair in range(q_ref.shape[1] // PAIR):
        lanes = slice(pair * PAIR, (pair + 1) * PAIR)
        do, q, k, v = do_ref[:, lanes], q_ref[:, lanes], k_ref[:, lanes], v_ref[:, lanes]
        do_t, q_t = do.T, q.T
        dq, dk_t, dv_t = [], [], []
        for h in range(2):
            p = p_ref[2 * pair + h]
            dp = dot_nt(jnp.where(masks[h], do, jnp.zeros_like(do)), v)
            pf = p.astype(F32)
            ds = (pf * (dp - jnp.sum(dp * pf, -1, keepdims=True))).astype(BF)
            dq.append(jnp.dot(ds, k, preferred_element_type=F32))
            part = slice(h * half, (h + 1) * half)
            dk_t.append(jnp.dot(q_t[part], ds, preferred_element_type=F32))
            dv_t.append(jnp.dot(do_t[part], p, preferred_element_type=F32))
        dq_ref[:, lanes] = (jnp.where(masks[0], dq[0], dq[1]) * scale).astype(BF)
        dk_ref[:, lanes] = (jnp.concatenate(dk_t, 0) * scale).astype(BF).T
        dv_ref[:, lanes] = jnp.concatenate(dv_t, 0).astype(BF).T


def attend_back(do, q, k, v, p, batch, group=4):
    rows, keys, d = q.shape[0] // batch, k.shape[0] // batch, q.shape[1]
    wide = group * d // H
    spec = lambda n: pl.BlockSpec((n, wide), lambda b, g: (b, g))
    return pl.pallas_call(
        partial(attend_back_kernel, (d // H) ** -0.5),
        grid=(batch, H // group),
        in_specs=[
            spec(rows), spec(rows), spec(keys), spec(keys),
            pl.BlockSpec((None, group, rows, keys), lambda b, g: (b, g, 0, 0)),
        ],
        out_specs=[spec(rows), spec(keys), spec(keys)],
        out_shape=[
            jax.ShapeDtypeStruct(q.shape, BF),
            jax.ShapeDtypeStruct(k.shape, BF),
            jax.ShapeDtypeStruct(v.shape, BF),
        ],
        compiler_params=pltpu.CompilerParams(vmem_limit_bytes=40 * 2**20),
        cost_estimate=pl.CostEstimate(
            flops=32 * q.size * keys * URGENT,
            transcendentals=0,
            bytes_accessed=(6 * q.size + 8 * k.size + 2 * batch * H * rows * keys) * URGENT,
        ),
        name="attend_back",
    )(do, q, k, v, p)


BIG = pltpu.CompilerParams(vmem_limit_bytes=58 * 2**20)
SPOT = pl.BlockSpec(memory_space=pl.ANY)
WHOLE = pl.BlockSpec(memory_space=pltpu.VMEM)
CHUNK = 128


def here():
    rep, row = lax.axis_index("replica"), lax.axis_index("fsdp")
    return lax.div(rep, 2), lax.rem(rep, 2), lax.div(row, 2), lax.rem(row, 2)


def flip(bit, by):
    return 1 - bit if by else bit


def pieces_of(refs, number, w, sems, act):
    x, c, _, y = here()
    rows, half = w.shape[2], w.shape[3] // 2
    dx, dc = flip(x, number // 2), flip(c, number % 2)
    halves = len(refs[0].shape) == 4

    def copy(src, dy, g):
        to = w.at[:, flip(y, dy), :, pl.ds(g * half, half)] if halves else w.at[:, flip(y, dy)]
        src = src.at[:, pl.ds(0, rows)]
        getattr(pltpu.make_async_copy(src, to, sems.at[2 * dy + g]), act)()

    if act == "wait":
        for dy in range(2):
            for g in range(2 if halves else 1):
                copy(refs[0].at[0] if halves else refs[0], dy, g)
        return
    for far in range(2):
        group = refs[4 * far : 4 * far + 4]
        if halves:
            p0, q0, p1, q1 = group

            @pl.when(dc == far)
            def _(p1=p1, q1=q1):
                copy(p1.at[dx], 0, 1)
                copy(q1.at[dx], 1, 1)

        for side in range(2):

            @pl.when((dc == far) & (dx == side))
            def _(group=group, side=side):
                if halves:
                    copy(group[side].at[0], 0, 0)
                    copy(group[side].at[1], 1, 0)
                else:
                    copy(group[2 * side], 0, 0)
                    copy(group[2 * side + 1], 1, 0)


def row_sum(v):
    return jnp.sum(v, 0, keepdims=True)


def normal(v):
    centered = v - jnp.mean(v, -1, keepdims=True)
    inverse = lax.rsqrt(jnp.mean(centered * centered, -1, keepdims=True) + EPSILON)
    return centered * inverse, inverse


def chunks(rows, step, do):
    def one(i, carry):
        do(pl.ds(pl.multiple_of(i * step, step), step))
        return carry

    lax.fori_loop(0, rows // step, one, 0)


def weight(w_ref, *lead):
    v = w_ref[lead] if lead else w_ref[...]
    return v.reshape(v.shape[-4] * v.shape[-3] * v.shape[-2], v.shape[-1])


def times(a_ref, w_ref, put):
    put(slice(None), jnp.dot(a_ref[...], weight(w_ref), preferred_element_type=F32))


def times_t(pairs, put):
    total = None
    for a_ref, w_ref in pairs:
        part = dot_nt(a_ref[...], weight(w_ref))
        total = part if total is None else total + part
    put(slice(None), total)


def loaded(m, n, count):
    return [pltpu.VMEM((4, 2, m, n), BF)] * count + [pltpu.SemaphoreType.DMA((count, 4))]


URGENT = 400


def cost(flops, *arrays):
    return pl.CostEstimate(
        flops=flops * URGENT,
        transcendentals=0,
        bytes_accessed=sum(a.size * a.dtype.itemsize for a in arrays) * URGENT,
    )


def shape(dims, dtype):
    return jax.ShapeDtypeStruct(dims, dtype)


def pack_kernel(count, *rest):
    mats, vectors, out = rest[:4], rest[4 : 4 + count], rest[-1]
    x, c, _, _ = here()
    m, n = mats[0].shape
    half = n // 2
    for number, mat in enumerate(mats):

        @pl.when(2 * x + c == number)
        def _(mat=mat):
            for g in range(2):
                out[g, :m, :] = mat[:, g * half : (g + 1) * half]

    parts = []
    for v in vectors:
        parts += [v[i : i + m].reshape(1, m) for i in range(0, v.shape[0], m)]
    parts += [jnp.zeros((1, m), BF)] * (8 * n // m - len(parts))
    row = half // m
    rows = [jnp.concatenate(parts[row * i : row * (i + 1)], 1) for i in range(16)]
    for g in range(2):
        out[g, m:, :] = jnp.concatenate(rows[8 * g : 8 * g + 8], 0)


def pack(mats, vectors):
    m, n = mats[0].shape
    return pl.pallas_call(
        partial(pack_kernel, len(vectors)),
        in_specs=[WHOLE] * (4 + len(vectors)),
        out_specs=WHOLE,
        out_shape=shape((2, m + 8, n // 2), BF),
        compiler_params=BIG,
        name="pack",
    )(*mats, *vectors)


def first_kernel(x_ref, vec_ref, *rest):
    refs, (act_ref, q_ref, k_ref, v_ref), (wq, wk, wv, sems) = rest[:8], rest[8:12], rest[12:]
    for i, w in enumerate((wq, wk, wv)):
        pieces_of(refs, i, w, sems.at[i], "start")

    def norm(rows):
        n, _ = normal(x_ref[rows, :].astype(F32))
        act_ref[rows, :] = (n * vec_ref[0:1] + vec_ref[1:2]).astype(BF)

    chunks(x_ref.shape[0], CHUNK, norm)
    for i, (w, out, bias) in enumerate(((wq, q_ref, 2), (wk, k_ref, None), (wv, v_ref, 3))):
        pieces_of(refs, i, w, sems.at[i], "wait")

        def put(lanes, v, out=out, bias=bias):
            if bias is not None:
                v = v + vec_ref[bias : bias + 1, lanes]
            out[:, lanes] = v.astype(BF)

        times(act_ref, w, put)


def first(x, vecs, unit, m):
    like = shape(x.shape, BF)
    return pl.pallas_call(
        first_kernel,
        in_specs=[WHOLE, WHOLE] + [SPOT] * 8,
        out_specs=[WHOLE] * 4,
        out_shape=[like] * 4,
        scratch_shapes=loaded(m, x.shape[1], 3),
        compiler_params=BIG,
        cost_estimate=cost(6 * x.size * x.shape[1], x, x, x, x, x, *unit),
        name="first",
    )(x, vecs, *unit)


def project_kernel(second, numbers, rows_of, a_ref, res_ref, vec_ref, *rest):
    refs = rest[:16] if second else rest[:8]
    rest = rest[len(refs) :]
    outs, (w1, *rest) = rest[: 3 if second else 2], rest[3 if second else 2 :]
    mid_ref, act_ref = outs[:2]
    sems = rest[-1]
    bias, gain, shift, bias2 = rows_of
    pieces_of(refs[:8], numbers[0], w1, sems.at[0], "start")
    if second:
        w2 = rest[0]
        pieces_of(refs[8:], numbers[1], w2, sems.at[1], "start")
    pieces_of(refs[:8], numbers[0], w1, sems.at[0], "wait")

    def put(lanes, v):
        mid_ref[:, lanes] = res_ref[:, lanes].astype(F32) + (v + vec_ref[bias : bias + 1, lanes])

    times(a_ref, w1, put)

    def norm(rows):
        n, _ = normal(mid_ref[rows, :])
        act_ref[rows, :] = (n * vec_ref[gain : gain + 1] + vec_ref[shift : shift + 1]).astype(BF)

    chunks(a_ref.shape[0], CHUNK, norm)
    if second:
        pieces_of(refs[8:], numbers[1], w2, sems.at[1], "wait")

        def put2(lanes, v):
            outs[2][:, lanes] = (v + vec_ref[bias2 : bias2 + 1, lanes]).astype(BF)

        times(act_ref, w2, put2)


def project(a, residual, vecs, rows_of, units, numbers, m, name):
    second = len(units) == 2
    refs = [r for u in units for r in u]
    return pl.pallas_call(
        partial(project_kernel, second, numbers, rows_of),
        in_specs=[WHOLE] * 3 + [SPOT] * len(refs),
        out_specs=[WHOLE] * (3 if second else 2),
        out_shape=[shape(a.shape, F32), shape(a.shape, BF)] + ([shape(a.shape, BF)] if second else []),
        scratch_shapes=loaded(m, a.shape[1], len(units)),
        compiler_params=BIG,
        cost_estimate=cost(2 * len(units) * a.size * a.shape[1], a, a, a, a, a, a, *refs[:4]),
        name=name,
    )(a, residual, vecs, *refs)


def query_kernel(bias, a_ref, vec_ref, *rest):
    refs, out_ref, (w, sems) = rest[:8], rest[8], rest[9:]
    pieces_of(refs, 0, w, sems.at[0], "start")
    pieces_of(refs, 0, w, sems.at[0], "wait")

    def put(lanes, v):
        out_ref[:, lanes] = (v + vec_ref[bias : bias + 1, lanes]).astype(BF)

    times(a_ref, w, put)


def query(a, vecs, bias, unit, m):
    return pl.pallas_call(
        partial(query_kernel, bias),
        in_specs=[WHOLE] * 2 + [SPOT] * 8,
        out_specs=WHOLE,
        out_shape=shape(a.shape, BF),
        scratch_shapes=loaded(m, a.shape[1], 1),
        compiler_params=BIG,
        cost_estimate=cost(2 * a.size * a.shape[1], a, a, *unit[:2]),
        name="query",
    )(a, vecs, *unit)


def memory_kernel(e_ref, vec_ref, *rest):
    refs, (k_ref, v_ref), (wk, wv, sems) = rest[:8], rest[8:10], rest[10:]

    @pl.when(pl.program_id(0) == 0)
    def _():
        for i, w in enumerate((wk, wv)):
            pieces_of(refs, i + 1, w, sems.at[i], "start")
        for i, w in enumerate((wk, wv)):
            pieces_of(refs, i + 1, w, sems.at[i], "wait")

    def put_k(lanes, v):
        k_ref[:, lanes] = v.astype(BF)

    def put_v(lanes, v):
        v_ref[:, lanes] = (v + vec_ref[8:9, lanes]).astype(BF)

    times(e_ref, wk, put_k)
    times(e_ref, wv, put_v)


def memory(e, vecs, unit, m, step=512):
    d = e.shape[1]
    blk = pl.BlockSpec((step, d), lambda i: (i, 0))
    return pl.pallas_call(
        memory_kernel,
        grid=(e.shape[0] // step,),
        in_specs=[blk, pl.BlockSpec(vecs.shape, lambda i: (0, 0))] + [SPOT] * 8,
        out_specs=[blk, blk],
        out_shape=[shape(e.shape, BF)] * 2,
        scratch_shapes=loaded(m, d, 2),
        compiler_params=BIG,
        cost_estimate=cost(4 * e.size * d, e, e, e, *unit),
        name="memory",
    )(e, vecs, *unit)


def memory_back_kernel(dk_ref, dv_ref, *rest):
    refs, (out_ref, sum_ref), (wk, wv, sems) = rest[:8], rest[8:10], rest[10:]

    @pl.when(pl.program_id(0) == 0)
    def _():
        for i, w in enumerate((wk, wv)):
            pieces_of(refs, i + 1, w, sems.at[i], "start")
        sum_ref[...] = jnp.zeros_like(sum_ref)
        for i, w in enumerate((wk, wv)):
            pieces_of(refs, i + 1, w, sems.at[i], "wait")

    def put(lanes, v):
        out_ref[:, lanes] = v

    times_t([(dk_ref, wk), (dv_ref, wv)], put)
    sum_ref[0:1] += row_sum(dv_ref[...].astype(F32))


def memory_back(dk, dv, unit, m, step=512):
    d = dk.shape[1]
    blk = pl.BlockSpec((step, d), lambda i: (i, 0))
    return pl.pallas_call(
        memory_back_kernel,
        grid=(dk.shape[0] // step,),
        in_specs=[blk, blk] + [SPOT] * 8,
        out_specs=[blk, pl.BlockSpec((8, d), lambda i: (0, 0))],
        out_shape=[shape(dk.shape, F32), shape((8, d), F32)],
        scratch_shapes=loaded(m, d, 2),
        compiler_params=BIG,
        cost_estimate=cost(4 * dk.size * d, dk, dk, dk, dk, *unit),
        name="memory_back",
    )(dk, dv, *unit)


def apply_norm_back(rows, dact, v, gain, residual, sums):
    n, inverse = normal(v)
    sums[0:1] += row_sum(dact * n)
    sums[1:2] += row_sum(dact)
    q = dact * gain
    mean_one = jnp.mean(q, -1, keepdims=True)
    mean_two = jnp.mean(q * n, -1, keepdims=True)
    return residual + inverse * (q - mean_one - n * mean_two)


def cross_back_kernel(dq_ref, mid_ref, dmid_ref, vec_ref, *rest):
    refs, (out_ref, low_ref, do_ref, sum_ref), (dact, w1, w2, sems) = rest[:16], rest[16:20], rest[20:]
    pieces_of(refs[:8], 0, w1, sems.at[0], "start")
    pieces_of(refs[8:], 3, w2, sems.at[1], "start")
    sum_ref[...] = jnp.zeros_like(sum_ref)
    sum_ref[2:3] = row_sum(dq_ref[...].astype(F32))
    pieces_of(refs[:8], 0, w1, sems.at[0], "wait")

    def put(lanes, v):
        dact[:, lanes] = v

    times_t([(dq_ref, w1)], put)

    def back(rows):
        total = apply_norm_back(
            rows, dact[rows, :], mid_ref[rows, :], vec_ref[5:6], dmid_ref[rows, :], sum_ref
        )
        out_ref[rows, :] = total
        low = total.astype(BF)
        low_ref[rows, :] = low
        sum_ref[3:4] += row_sum(low.astype(F32))

    chunks(dq_ref.shape[0], CHUNK, back)
    pieces_of(refs[8:], 3, w2, sems.at[1], "wait")

    def put2(lanes, v):
        do_ref[:, lanes] = v.astype(BF)

    times_t([(low_ref, w2)], put2)


def cross_back(dq, mid, dmid, vecs, cross_unit, self_unit, m):
    d = dq.shape[1]
    return pl.pallas_call(
        cross_back_kernel,
        in_specs=[WHOLE] * 4 + [SPOT] * 16,
        out_specs=[WHOLE] * 4,
        out_shape=[shape(dq.shape, F32), shape(dq.shape, BF), shape(dq.shape, BF), shape((8, d), F32)],
        scratch_shapes=[pltpu.VMEM(dq.shape, F32)] + loaded(m, d, 2),
        compiler_params=BIG,
        cost_estimate=cost(4 * dq.size * d, mid, mid, mid, dq, dq, dq, *cross_unit[:4]),
        name="cross_back",
    )(dq, mid, dmid, vecs, *cross_unit, *self_unit)


def self_back_kernel(dq_ref, dk_ref, dv_ref, x_ref, dmid_ref, vec_ref, *rest):
    refs, (out_ref, sum_ref), (dact, wq, wk, wv, sems) = rest[:8], rest[8:10], rest[10:]
    for i, w in enumerate((wq, wk, wv)):
        pieces_of(refs, i, w, sems.at[i], "start")
    sum_ref[...] = jnp.zeros_like(sum_ref)
    sum_ref[2:3] = row_sum(dq_ref[...].astype(F32))
    sum_ref[3:4] = row_sum(dv_ref[...].astype(F32))
    for i, w in enumerate((wq, wk, wv)):
        pieces_of(refs, i, w, sems.at[i], "wait")

    def put(lanes, v):
        dact[:, lanes] = v

    times_t([(dq_ref, wq), (dk_ref, wk), (dv_ref, wv)], put)

    def back(rows):
        out_ref[rows, :] = apply_norm_back(
            rows, dact[rows, :], x_ref[rows, :].astype(F32), vec_ref[0:1], dmid_ref[rows, :], sum_ref
        )

    chunks(dq_ref.shape[0], CHUNK, back)


def self_back(dq, dk, dv, x, dmid, vecs, unit, m):
    d = dq.shape[1]
    return pl.pallas_call(
        self_back_kernel,
        in_specs=[WHOLE] * 6 + [SPOT] * 8,
        out_specs=[WHOLE] * 2,
        out_shape=[shape(dq.shape, F32), shape((8, d), F32)],
        scratch_shapes=[pltpu.VMEM(dq.shape, F32)] + loaded(m, d, 3),
        compiler_params=BIG,
        cost_estimate=cost(6 * dq.size * d, dmid, dmid, dq, dq, dq, dq, *unit),
        name="self_back",
    )(dq, dk, dv, x, dmid, vecs, *unit)


def output_back_kernel(d_ref, *rest):
    refs, do_ref, (w, sems) = rest[:8], rest[8], rest[9:]
    pieces_of(refs, 3, w, sems.at[0], "start")
    pieces_of(refs, 3, w, sems.at[0], "wait")

    def put(lanes, v):
        do_ref[:, lanes] = v.astype(BF)

    times_t([(d_ref, w)], put)


def output_back(dlow, unit, m):
    d = dlow.shape[1]
    return pl.pallas_call(
        output_back_kernel,
        in_specs=[WHOLE] + [SPOT] * 8,
        out_specs=WHOLE,
        out_shape=shape(dlow.shape, BF),
        scratch_shapes=loaded(m, d, 1),
        compiler_params=BIG,
        cost_estimate=cost(2 * dlow.size * d, dlow, dlow, *unit[:2]),
        name="output_back",
    )(dlow, *unit)


def send_off(block, away, keep, dx, dc, spot, sem):
    @pl.when(dc == 1)
    def _():
        pltpu.make_async_copy(block, away.at[(dx,) + spot], sem).start()

    @pl.when(dc == 0)
    def _():
        pltpu.make_async_copy(block, keep.at[(dx,) + spot], sem).start()


def dot_tn(a, b):
    return lax.dot_general(a, b, (((0,), (0,)), ((), ())), preferred_element_type=F32)


def grads_kernel(sides, *rest):
    count = 1 + max(sides)
    left_refs, right_refs = rest[:count], rest[count : count + 4]
    away, keep, out, sems = rest[count + 4 :]
    x, c, z, y = here()
    half = out.shape[-1]
    for number, side in enumerate(sides):
        for zz in range(4):
            v = dot_tn(left_refs[side][:, zz * 256 : (zz + 1) * 256], right_refs[number][...]).astype(BF)
            for yy in range(2):
                for g in range(2):
                    out[number, g, flip(y, yy), zz] = v[yy * 128 : (yy + 1) * 128, g * half : (g + 1) * half]
        dx, dc = flip(x, number // 2), flip(c, number % 2)
        send_off(out.at[number], away, keep, dx, dc, (), sems.at[number])
    for number in range(4):
        pltpu.make_async_copy(out.at[number], keep.at[0], sems.at[number]).wait()


def grads(lefts, rights, sides, name):
    d, n = lefts[0].shape[1], rights[0].shape[1]
    dims = (2, 2, 2, 4, d // 8, n // 2)
    return pl.pallas_call(
        partial(grads_kernel, sides),
        in_specs=[WHOLE] * (len(lefts) + 4),
        out_specs=[SPOT] * 2,
        out_shape=[shape(dims, BF)] * 2,
        scratch_shapes=[pltpu.VMEM((4,) + dims[1:], BF), pltpu.SemaphoreType.DMA((4,))],
        compiler_params=BIG,
        cost_estimate=cost(2 * sum(r.size for r in rights) * d, *lefts, *rights, *rights, *rights),
        name=name,
    )(*lefts, *rights)


def sums_kernel(counts, joined, *rest):
    ins, outs = rest[: sum(counts)], rest[sum(counts) :]
    at_in = 0
    for i, count in enumerate(counts):
        total = ins[at_in][...].astype(F32)
        for r in ins[at_in + 1 : at_in + count]:
            total = total + r[...].astype(F32)
        at_in += count
        total = total.astype(BF)
        if joined:
            wide = total.shape[-1]
            outs[0][:, :, i * wide : (i + 1) * wide] = total
        else:
            outs[i][...] = total.reshape(outs[i].shape)


def sums(steps, *groups, joined=False):
    ins = [i for _, _, _, members in groups for i in members]
    outs = [g[:3] for g in groups]
    if joined:
        (p, m, n), (q, _, _), to = outs[0]
        outs = [((p, m, n * len(groups)), (q, m, n * len(groups)), to)]
    out = pl.pallas_call(
        partial(sums_kernel, tuple(len(g[3]) for g in groups), joined),
        grid=(steps,),
        in_specs=[pl.BlockSpec(block, to) for _, block, to in ins],
        out_specs=[pl.BlockSpec(o[1], o[2]) for o in outs],
        out_shape=[shape(o[0], BF) for o in outs],
        cost_estimate=pl.CostEstimate(
            flops=0,
            transcendentals=0,
            bytes_accessed=2 * URGENT * sum(int(np.prod(g[0])) * (1 + len(g[3])) for g in groups),
        ),
        name="sums",
    )(*[v for v, _, _ in ins])
    return out[0] if joined else out


def grads_of(left, lefts, rights, sides, name):
    return grads([left] + list(lefts), rights, sides, name)


def ffn_kernel(last, first_row, act_ref, dy_ref, mid_ref, vec_ref, *rest):
    begin = rest[:2] if last else ()
    rest = rest[len(begin) :]
    refs, rest = rest[:8], rest[8:]
    outs, rest = rest[: 4 if last else 2], rest[4 if last else 2 :]
    dbe_ref, away, keep = rest[:3]
    hid_ref, dexp_ref, acc, dact, out, we0, wd0, we1, wd1, sems, out_sems = rest[3:]
    rows, d = act_ref.shape
    half_n = d // 2
    x, c, z, y = here()
    mats = ((we0, wd0), (we1, wd1))
    for t in range(2):
        for n in range(2):
            pieces_of(refs, 2 * t + n, mats[t][n], sems.at[2 * t + n], "start")
    dbe_ref[...] = jnp.zeros_like(dbe_ref)
    if last:
        outs[3][...] = jnp.zeros_like(outs[3])
    for t in range(2):
        for n in range(2):
            pieces_of(refs, 2 * t + n, mats[t][n], sems.at[2 * t + n], "wait")
        bias = vec_ref[first_row + t : first_row + t + 1]

        def half(r, t=t, bias=bias):
            we, wd = weight(mats[t][0]), weight(mats[t][1])
            u = jnp.dot(act_ref[r, :], we, preferred_element_type=F32) + bias
            cdf = 0.5 * (1.0 + lax.erf(u * np.float32(0.5**0.5)))
            pdf = jnp.exp(-0.5 * u * u) * np.float32((2 * np.pi) ** -0.5)
            hid = (u * cdf).astype(BF)
            hid_ref[r, :] = hid
            dexp = (dot_nt(dy_ref[r, :], wd) * (cdf + u * pdf)).astype(BF)
            dexp_ref[r, :] = dexp
            dbe_ref[t : t + 1] += row_sum(dexp.astype(F32))
            down, back = jnp.dot(hid, wd, preferred_element_type=F32), dot_nt(dexp, we)
            if t == 0 and not last:
                acc[r, :], dact[r, :] = down, back
            elif t == 0:
                acc[r, :], dact[r, :] = begin[0][r, :] + down, begin[1][r, :] + back
            else:
                acc[r, :] += down
                dact[r, :] += back

        chunks(rows, 256, half)
        for number, (a_ref, b_ref) in ((2 * t, (act_ref, dexp_ref)), (2 * t + 1, (hid_ref, dy_ref))):
            for zz in range(4):
                v = dot_tn(a_ref[:, zz * 256 : (zz + 1) * 256], b_ref[...]).astype(BF)
                for yy in range(2):
                    for g in range(2):
                        part = v[yy * 128 : (yy + 1) * 128, g * half_n : (g + 1) * half_n]
                        out[number, g, flip(y, yy), zz] = part
            dx, dc = flip(x, number // 2), flip(c, number % 2)
            send_off(out.at[number], away, keep, dx, dc, (), out_sems.at[number])
    if last:
        out_ref, dmid_ref, low_ref, sum_ref = outs

        def back(r):
            mid = mid_ref[r, :]
            out_ref[r, :] = (mid + (acc[r, :] + vec_ref[12:13])).astype(BF)
            dy = dy_ref[r, :].astype(F32)
            total = apply_norm_back(r, dact[r, :], mid, vec_ref[10:11], dy, sum_ref)
            dmid_ref[r, :] = total
            low = total.astype(BF)
            low_ref[r, :] = low
            sum_ref[2:3] += row_sum(dy)
            sum_ref[3:4] += row_sum(low.astype(F32))

        chunks(rows, CHUNK, back)
    else:
        outs[0][...] = acc[...]
        outs[1][...] = dact[...]
    for number in range(4):
        pltpu.make_async_copy(out.at[number], keep.at[0], out_sems.at[number]).wait()


def ffn(act, dy, mid, vecs, unit, m, begin, first_row):
    rows, d = act.shape
    last = bool(begin)
    dims = (2, 2, 2, 4, m, d // 2)
    if last:
        heads = [shape(act.shape, BF), shape(act.shape, F32), shape(act.shape, BF), shape((8, d), F32)]
    else:
        heads = [shape(act.shape, F32)] * 2
    return pl.pallas_call(
        partial(ffn_kernel, last, first_row),
        in_specs=[WHOLE] * (4 + len(begin)) + [SPOT] * 8,
        out_specs=[WHOLE] * (len(heads) + 1) + [SPOT] * 2,
        out_shape=heads + [shape((8, d), F32)] + [shape(dims, BF)] * 2,
        scratch_shapes=[
            pltpu.VMEM((rows, d), BF),
            pltpu.VMEM((rows, d), BF),
            pltpu.VMEM((rows, d), F32),
            pltpu.VMEM((rows, d), F32),
            pltpu.VMEM((4,) + dims[1:], BF),
        ]
        + loaded(m, d, 4)
        + [pltpu.SemaphoreType.DMA((4,))],
        compiler_params=BIG,
        cost_estimate=cost(24 * act.size * d, *unit, *unit, mid, mid),
        name="ffn",
    )(act, dy, mid, vecs, *begin, *unit)


def finish_kernel(count, *rest):
    units, outs, held = [rest[3 * i : 3 * i + 3] for i in range(count)], rest[3 * count : -1], rest[-1]
    x, c, _, _ = here()
    m, n = units[0][0].shape
    for i, (own_ref, x_ref, core_ref) in enumerate(units):
        held[0], held[2] = own_ref[...], x_ref[...]
        held[1], held[3] = core_ref[0], core_ref[1]
        for number in range(4):
            j = flip(x, number // 2) * 2 + flip(c, number % 2)
            v = held[j].astype(F32)
            t = 2 * i + number // 2
            if count == 1:
                outs[number][...] = v
            elif number % 2:
                outs[1][t * m : (t + 1) * m] = v
            else:
                for f in range(n // 128):
                    to = (f * 4 + t) * 128
                    outs[0][:, to : to + 128] = v[:, f * 128 : (f + 1) * 128]


def finish(own, from_x, from_core, parts=()):
    units = ((own, from_x, from_core), *parts)
    m, n = own.shape
    dims = [(m, n)] * 4 if len(units) == 1 else [(m, 4 * n), (4 * m, n)]
    return pl.pallas_call(
        partial(finish_kernel, len(units)),
        in_specs=[WHOLE] * (3 * len(units)),
        out_specs=[WHOLE] * len(dims),
        out_shape=[shape(s, F32) for s in dims],
        scratch_shapes=[pltpu.VMEM((4, m, n), BF)],
        compiler_params=BIG,
        cost_estimate=cost(0, *[v for u in units for v in u] * 3),
        name="finish",
    )(*[v for u in units for v in u])


def product(left, right):
    return jnp.dot(left, right, preferred_element_type=F32)


def product_nt(left, right):
    return lax.dot_general(
        left, right, (((1,), (1,)), ((), ())), preferred_element_type=F32
    )


def moments(values):
    average = jnp.mean(values, -1, keepdims=True)
    centered = values - average
    variance = jnp.mean(centered * centered, -1, keepdims=True)
    inverse = lax.rsqrt(variance + EPSILON)
    return (centered * inverse, inverse)


def norm_back(grad_out, normed, inverse, gain_vec):
    gain_grad = jnp.sum(grad_out * normed, 0)
    shift_grad = jnp.sum(grad_out, 0)
    scaled = grad_out * gain_vec
    mean_one = jnp.mean(scaled, -1, keepdims=True)
    mean_two = jnp.mean(scaled * normed, -1, keepdims=True)
    return (inverse * (scaled - mean_one - normed * mean_two), gain_grad, shift_grad)


def gelu_both(u):
    cdf = 0.5 * (1.0 + lax.erf(u * np.float32(0.5**0.5)))
    pdf = jnp.exp(-0.5 * u * u) * np.float32((2 * np.pi) ** -0.5)
    return (u * cdf).astype(BF), (cdf + u * pdf).astype(BF)


def body(
    groups,
    rows,
    decoder_input,
    encoder_out,
    prefix_length,
    output_grad,
    self_query,
    self_key,
    self_value,
    self_output,
    selfquery_bias,
    selfvalue_bias,
    self_attention_output_bias,
    cross_query,
    cross_key,
    cross_value,
    cross_output,
    crossquery_bias,
    crossvalue_bias,
    crossoutput_bias,
    expand_weight,
    expand_bias,
    down_projection_weight,
    reduce_bias,
    selfnorm_gain,
    selfnorm_bias,
    crossnorm_gain,
    crossnorm_bias,
    finalnorm_gain,
    finalnorm_bias,
):
    place = Place(groups, rows)
    batch, seq, d = decoder_input.shape
    m = self_query.shape[0]
    ff = expand_weight.shape[1]
    fl = ff // rows // 2
    k4 = ff // d

    small = [
        selfnorm_gain, selfnorm_bias, selfquery_bias, selfvalue_bias, self_attention_output_bias,
        crossnorm_gain, crossnorm_bias, crossquery_bias, crossvalue_bias, crossoutput_bias,
        finalnorm_gain, finalnorm_bias, reduce_bias,
    ]
    packed = jnp.concatenate([jnp.stack(small), expand_bias.reshape(k4, m)])
    vecs = gather_vectors(place, packed).astype(F32)
    (g1, b1, bq, bv, bo, g2, b2, bcq, bcv, bco, g3, b3, br) = [
        vecs[:, i].reshape(d) for i in range(13)
    ]
    be = vecs[:, 13:].reshape(rows, 2, fl)

    expand_halves = [
        expand_weight.reshape(m, rows, 2, fl)[:, :, h].reshape(m, rows * fl) for h in range(2)
    ]
    down_halves = [down_projection_weight[h * fl : (h + 1) * fl] for h in range(2)]

    lane, ring_lane = Lane(4), Lane(2)
    gathers = [
        Gather(place, lane, ring_lane, shard, split)
        for shard, split in (
            (jnp.concatenate([self_query, self_key], 1), True),
            (self_value, False),
            (jnp.concatenate([cross_key, cross_value], 1), True),
            (self_output, False),
            (jnp.concatenate([cross_query, cross_output], 1), True),
            (expand_halves[0], True),
            (expand_halves[1], True),
            (down_halves[0], False),
            (down_halves[1], True),
        )
    ]
    run_steps(gathers)
    w_qk, w_v, w_ckv, w_o, w_cqo, *w_ff = [u.v for u in gathers]
    w_e, w_d = w_ff[:2], w_ff[2:]

    x = decoder_input.reshape(batch * seq, d).astype(F32)
    e = encoder_out.reshape(-1, d)
    dy = output_grad.reshape(batch * seq, d)

    n1, i1 = moments(x)
    act1 = (n1 * g1 + b1).astype(BF)
    qk = product(act1, w_qk)
    q = (qk[:, :d] + bq).astype(BF)
    k = qk[:, d:].astype(BF)
    v = (product(act1, w_v) + bv).astype(BF)
    o, p = attend(q, k, v, prefix_length, batch, True)
    mid1 = x + (product(o, w_o) + bo)
    n2, i2 = moments(mid1)
    act2 = (n2 * g2 + b2).astype(BF)
    w_cq, w_co = w_cqo[:, :d], w_cqo[:, d:]
    cq = (product(act2, w_cq) + bcq).astype(BF)
    ckv = product(e, w_ckv)
    ck = ckv[:, :d].astype(BF)
    cv = (ckv[:, d:] + bcv).astype(BF)
    co, cp = attend(cq, ck, cv, prefix_length, batch, False)
    mid2 = mid1 + (product(co, w_co) + bco)
    n3, i3 = moments(mid2)
    act3 = (n3 * g3 + b3).astype(BF)
    hidden, slope = [], []
    for h in range(2):
        hid, slo = gelu_both(product(act3, w_e[h]) + be[:, h].reshape(-1))
        hidden.append(hid)
        slope.append(slo)
    layer_out = (mid2 + (product(hidden[0], w_d[0]) + product(hidden[1], w_d[1]) + br)).astype(BF)

    scatter = partial(Scatter, place, lane, ring_lane)
    dyf = dy.astype(F32)
    g_down = [scatter(hidden[0], dy, True), scatter(hidden[1], dy, False)]
    dexp = [(product_nt(dy, w_d[h]) * slope[h].astype(F32)).astype(BF) for h in range(2)]
    g_exp = [scatter(act3, dexp[0], True), scatter(act3, dexp[1], False)]
    dact3 = product_nt(dexp[0], w_e[0]) + product_nt(dexp[1], w_e[1])
    dn, gg3, gb3 = norm_back(dact3, n3, i3, g3)
    dmid2 = dyf + dn
    dcross = dmid2.astype(BF)
    g_co = scatter(co, dcross, True)
    dco = product_nt(dcross, w_co).astype(BF)
    dcq, dck, dcv = attend_back(dco, cq, ck, cv, cp, batch)
    g_ck = scatter(e, dck, True)
    g_cv = scatter(e, dcv, False)
    g_cq = scatter(act2, dcq, False)
    encoder_grad = product_nt(jnp.concatenate([dck, dcv], 1), w_ckv)
    dn, gg2, gb2 = norm_back(product_nt(dcq, w_cq), n2, i2, g2)
    dmid1 = dmid2 + dn
    dself = dmid1.astype(BF)
    g_so = scatter(o, dself, True)
    dao = product_nt(dself, w_o).astype(BF)
    dq, dk, dv = attend_back(dao, q, k, v, p, batch)
    g_sv = scatter(act1, dv, False)
    g_sq = scatter(act1, dq, True)
    g_sk = scatter(act1, dk, True)
    dact1 = product_nt(jnp.concatenate([dq, dk], 1), w_qk) + product_nt(dv, w_v)
    dn, gg1, gb1 = norm_back(dact1, n1, i1, g1)
    input_grad = dmid1 + dn

    def column_sum(t):
        return jnp.sum(t.astype(F32), 0)

    dbe = jnp.stack([column_sum(t).reshape(rows, fl) for t in dexp], 1).reshape(rows, k4, m)
    early = [
        gg2, gb2, column_sum(dcq), column_sum(dcv), column_sum(dcross),
        gg3, gb3, column_sum(dy), column_sum(dself),
    ]
    early = jnp.concatenate([jnp.stack([t.reshape(rows, m) for t in early], 1), dbe], 1)
    late = [gg1, gb1, column_sum(dq), column_sum(dv)]
    late = jnp.stack([t.reshape(rows, m) for t in late], 1)

    first = g_down + g_exp + [g_co, g_cv, g_ck, g_cq, g_so]
    second = [g_sv, g_sq, g_sk]
    run_steps(first + second)
    early = scatter_vectors(place, lane, ring_lane, early)
    (*g_ff, g_co, g_cv, g_ck, g_cq, g_so) = finish_all(place, lane, first)
    g_down, g_exp = g_ff[:2], g_ff[2:]
    late = scatter_vectors(place, lane, ring_lane, late)
    g_sv, g_sq, g_sk = finish_all(place, lane, second)

    g_exp = jnp.stack([t.reshape(m, rows, fl) for t in g_exp], 2).reshape(m, ff)
    g_down = jnp.concatenate(g_down, 0)
    return (
        layer_out.reshape(batch, seq, d),
        input_grad.reshape(batch, seq, d),
        encoder_grad.reshape(encoder_out.shape),
        g_sq, g_sk, g_sv, g_so,
        late[2], late[3], early[8],
        g_cq, g_ck, g_cv, g_co,
        early[2], early[3], early[4],
        g_exp, early[9:].reshape(-1), g_down, early[7],
        late[0], late[1], early[0], early[1], early[5], early[6],
    )


class Order:
    def __init__(self):
        self.sent, self.ran, self.open = [], [], []

    def send(self, move, v, hold=2):
        v = self.see(v)
        got = move(v)
        self.sent.append(v)
        self.open.append([hold, got])
        return got

    def see(self, v):
        return lax.optimization_barrier((v, *self.ran))[0] if self.ran else v

    def run(self, kernel, v, *rest, **named):
        due = [got for hold, got in self.open if hold == 0]
        self.open = [[hold - 1, got] for hold, got in self.open if hold > 0]
        before = (*self.sent, *self.ran, *due)
        if before:
            v, *_ = lax.optimization_barrier((v, *before))
        out = kernel(v, *rest, **named)
        self.sent, self.ran = [], [out[0] if isinstance(out, (list, tuple)) else out]
        return out


class HalfUnit:
    def __init__(self, place, order, piece):
        self.place, self.order, self.piece = place, order, piece

    def ring(self):
        a = self.order.send(partial(ring_gather, self.place), self.piece)
        self.a0, self.a1 = a[:, 0], a[:, 1]

    def one(self):
        self.p0 = jnp.stack([self.a0, self.order.send(self.place.pair, self.a0)])
        self.p1 = jnp.stack([self.a1, self.order.send(self.place.across, self.a1)])

    def two(self):
        self.q0 = self.order.send(self.place.across, self.p0)
        self.q1 = self.order.send(self.place.pair, self.p1)
        self.c0 = self.order.send(self.place.core, self.p0)
        self.c1 = self.order.send(self.place.core, self.p1)

    def core(self):
        d0 = self.order.send(self.place.core, self.q0)
        d1 = self.order.send(self.place.core, self.q1)
        self.refs = (self.p0, self.q0, self.p1, self.q1, self.c0, d0, self.c1, d1)


class Unit:
    def __init__(self, place, order, piece, flat):
        self.place, self.order, self.piece, self.flat = place, order, piece, flat

    def ring(self):
        self.a = self.order.send(partial(ring_gather, self.place), self.piece)

    def pair(self):
        self.b = self.order.send(self.place.pair, self.order.see(self.a))

    def across(self):
        self.ax = self.order.send(self.place.across, self.order.see(self.a))

    def near(self):
        self.ca = self.order.send(self.place.core, self.order.see(self.a), 1)

    def two(self):
        see, send = self.order.see, self.order.send
        if self.flat:
            self.bx = send(self.place.pair, see(self.ax))
        else:
            self.bx = send(self.place.across, see(self.b))

    def both(self):
        see, send = self.order.see, self.order.send
        self.cb, self.cax = send(self.place.core, see(self.b), 1), send(self.place.core, see(self.ax), 1)

    def core(self):
        far = self.order.send(self.place.core, self.order.see(self.bx))
        self.refs = (self.a, self.b, self.ax, self.bx, self.ca, self.cb, self.cax, far)


class Sum:
    def __init__(self, place, order, away, keep):
        self.place, self.order = place, order
        self.away, self.keep = away, keep

    def core(self):
        self.came = self.order.send(self.place.core, self.away)

    def one(self):
        see, k = self.order.see, self.keep
        self.came = see(self.came)
        block, dims = (None, None, None) + k.shape[3:], k.shape[2:]
        half = (None,) + dims[1:]
        first, second = (lambda i: (1, 0, i, 0, 0, 0)), (lambda i: (i, 1, 1, 0, 0, 0))
        to = lambda i: (i, 0, 0, 0)
        to_x, to_y = sums(
            2,
            (dims, half, to, [(k, block, first), (self.came, block, first)]),
            (dims, half, to, [(k, block, second), (self.came, block, second)]),
        )
        self.from_x = self.order.send(self.place.across, to_x)
        self.from_y = self.order.send(self.place.pair, to_y)

    def rest(self, name, extra):
        k, r = self.keep, self.came
        _, m, half = k.shape[3:]
        block, part = (None, None, None, 2, m, half), (None, 2, m, half)
        first = (lambda i: (0, 0, 1, i, 0, 0)) if name == "go" else (lambda i: (0, 0, 0, i, 0, 0))
        second = (lambda i: (1, 1, 0, i, 0, 0)) if name == "go" else (lambda i: (0, 1, 0, i, 0, 0))
        side = 1 if name == "go" else 0
        third = lambda i: (side, i, 0, 0)
        plain = lambda i: (i, 0, 0)
        groups = []
        for at_k, came, more in ((first, self.from_x, extra[:1]), (second, self.from_y, extra[1:])):
            members = [(k, block, at_k), (r, block, at_k), (came, part, third)]
            members += [(v, (2, m, half), plain) for v in more]
            groups.append(((4, m, half), (2, m, half), plain, members))
        return sums(2, *groups, joined=name == "stay")

    def two(self):
        self.from_x, self.from_y = self.order.see(self.from_x), self.order.see(self.from_y)
        to_y, to_x = self.rest("go", [])
        self.next_y = self.order.send(self.place.pair, to_y)
        self.next_x = self.order.send(self.place.across, to_x)

    def ring(self):
        see = self.order.see
        both = self.rest("stay", [see(self.next_y), see(self.next_x)])
        self.own = self.order.send(partial(ring_sum, self.place), both)

    def last_x(self):
        self.own = self.order.see(self.own)
        self.own_x = self.order.send(self.place.across, self.own)

    def last_core(self):
        came = self.order.send(self.place.core, jnp.stack([self.own, self.order.see(self.own_x)]))
        self.parts = (self.own, self.own_x, came)


def fast_body(
    groups,
    rows,
    decoder_input,
    encoder_out,
    prefix_length,
    output_grad,
    self_query,
    self_key,
    self_value,
    self_output,
    selfquery_bias,
    selfvalue_bias,
    self_attention_output_bias,
    cross_query,
    cross_key,
    cross_value,
    cross_output,
    crossquery_bias,
    crossvalue_bias,
    crossoutput_bias,
    expand_weight,
    expand_bias,
    down_projection_weight,
    reduce_bias,
    selfnorm_gain,
    selfnorm_bias,
    crossnorm_gain,
    crossnorm_bias,
    finalnorm_gain,
    finalnorm_bias,
):
    place = Place(groups, rows)
    batch, seq, d = decoder_input.shape
    m = self_query.shape[0]
    ff = expand_weight.shape[1]
    rank = 2 * place.x + place.c
    order = Order()

    small = [
        selfnorm_gain, selfnorm_bias, selfquery_bias, selfvalue_bias, self_attention_output_bias,
        crossnorm_gain, crossnorm_bias, crossquery_bias, crossvalue_bias, crossoutput_bias,
        finalnorm_gain, finalnorm_bias, reduce_bias, expand_bias,
    ]
    count = 13 + ff // d

    def pick(*shards):
        return at(jnp.stack(shards), rank)

    u_self = HalfUnit(place, order, pack((self_query, self_key, self_value, self_output), small))
    later = (cross_query, cross_key, cross_value, cross_output, expand_weight, down_projection_weight)
    *later, _ = lax.optimization_barrier((*later, u_self.piece))
    w_e = later[4].reshape(m, rows, 4, -1).transpose(2, 0, 1, 3).reshape(4, m, d)
    w_d = later[5].reshape(4, m, d)
    unit = partial(Unit, place, order)
    u_cross = unit(pick(*later[:4]), True)
    u_low = unit(pick(w_e[0], w_d[0], w_e[1], w_d[1]), False)
    u_high = unit(pick(w_e[2], w_d[2], w_e[3], w_d[3]), True)

    x = decoder_input.reshape(batch * seq, d)
    e = encoder_out.reshape(-1, d)
    dy = output_grad.reshape(batch * seq, d)
    run = order.run

    u_self.ring()
    u_cross.ring()
    u_self.one()
    u_self.two()
    u_cross.pair()
    u_cross.across()
    u_low.ring()
    u_self.core()
    u_cross.near()
    self_w = u_self.refs
    both = jnp.stack([v[:, :, m:] for v in (u_self.p0, jnp.stack([u_self.p1[0], u_self.q1[0]]))])
    both = both.transpose(2, 1, 0, 3, 4)
    both = jnp.where(place.y == 0, both, both[:, ::-1]).reshape(rows, -1)
    vecs = both[:, : count * m].reshape(rows, count, m).transpose(1, 0, 2).reshape(count, d).astype(F32)
    act1, q, k, v = run(first, x, vecs, self_w, m)
    u_cross.two()
    o, p = run(attend, q, k, v, prefix_length, batch, True)
    u_high.ring()
    u_low.across()
    u_cross.both()
    mid1, act2 = run(project, o, x, vecs, (4, 5, 6, None), (self_w,), (3,), m, "self_out")
    u_low.pair()
    u_low.near()
    u_cross.core()
    cross_w = u_cross.refs
    ck, cv = run(memory, e, vecs, cross_w, m)
    u_high.across()
    cq = run(query, act2, vecs, 7, cross_w, m)
    u_high.pair()
    u_low.two()
    co, cp = run(attend, cq, ck, cv, prefix_length, batch, False)
    u_high.two()
    u_low.both()
    u_high.near()
    mid2, act3 = run(project, co, mid1, vecs, (9, 10, 11, None), (cross_w,), (3,), m, "cross_out")
    u_low.core()
    u_high.both()
    low_w = u_low.refs

    *begin, dbe_low, away, keep = run(ffn, act3, dy, mid2, vecs, low_w, m, (), 13)
    total = partial(Sum, place, order)
    g_low = total(away, keep)
    u_high.core()
    g_low.core()
    layer_out, dmid2, dcross, sums3, dbe_high, away, keep = run(
        ffn, act3, dy, mid2, vecs, u_high.refs, m, tuple(begin), 15
    )
    g_high = total(away, keep)
    g_low.one()
    g_high.core()
    dco = run(output_back, dcross, cross_w, m)
    dcq, dck, dcv = run(attend_back, dco, cq, ck, cv, cp, batch)
    g_high.one()
    g_cross = total(*run(grads_of, act2, [e, co], [dcq, dck, dcv, dcross], (0, 1, 1, 2), "cross_grads"))
    g_low.two()
    g_cross.core()
    dmid1, dself, dao, sums2 = run(cross_back, dcq, mid1, dmid2, vecs, cross_w, self_w, m)
    g_cross.one()
    dq, dk, dv = run(attend_back, dao, q, k, v, p, batch)
    g_high.two()
    g_low.ring()
    g_self = total(*run(grads_of, act1, [o], [dq, dk, dv, dself], (0, 0, 0, 1), "self_grads"))
    g_self.core()
    input_grad, sums1 = run(self_back, dq, dk, dv, x, dmid1, vecs, self_w, m)

    def by_shard(v):
        return v.reshape(-1, rows, m).transpose(1, 0, 2)

    g_self.one()
    g_cross.two()
    g_high.ring()
    encoder_grad, sums_e = run(memory_back, dck, dcv, cross_w, m)
    dbe = jnp.concatenate([dbe_low[:2], dbe_high[:2]])
    vec = by_shard(jnp.concatenate([sums1[:4], sums2[:4], sums3[:4], sums_e[:1], dbe]))
    vec = (vec.astype(BF).astype(F32) + order.send(place.core, vec.astype(BF)).astype(F32)).astype(BF)
    g_low.last_x()
    vec = (vec.astype(F32) + order.send(place.across, vec).astype(F32)).astype(BF)
    g_self.two()
    g_cross.ring()
    g_high.last_x()
    g_low.last_core()
    g_high.last_core()
    vec = vec.reshape((place.ring, 2) + vec.shape[1:])
    came = order.send(place.pair, at(vec, 1 - place.y, 1))
    vec = (at(vec, place.y, 1).astype(F32) + came.astype(F32)).astype(BF)
    g_self.ring()
    g_cross.last_x()
    vec = order.send(partial(ring_sum, place), vec).astype(F32)
    g_expand, g_down = run(finish, *g_low.parts, parts=(g_high.parts,))
    g_cross.last_core()
    g_self.last_x()
    g_cq, g_ck, g_cv, g_co = run(finish, *g_cross.parts)
    g_self.last_core()
    g_sq, g_sk, g_sv, g_so = run(finish, *g_self.parts)
    return (
        layer_out.reshape(batch, seq, d),
        input_grad.reshape(batch, seq, d),
        encoder_grad.reshape(encoder_out.shape),
        g_sq, g_sk, g_sv, g_so,
        vec[2], vec[3], vec[7],
        g_cq, g_ck, g_cv, g_co,
        vec[6], vec[12], vec[11],
        g_expand, vec[13:].reshape(-1), g_down, vec[10],
        vec[0], vec[1], vec[4], vec[5], vec[8], vec[9],
    )


def solution(mesh):
    groups, rows = mesh.shape["replica"], mesh.shape["fsdp"]
    data = P(("replica", "fsdp"), None, None)
    mat, vec = P("fsdp", None), P("fsdp")
    weights = (
        (mat,) * 4 + (vec,) * 3 + (mat,) * 4 + (vec,) * 3 + (mat, vec, mat, vec) + (vec,) * 6
    )
    return jax.shard_map(
        partial(fast_body if rows == 8 else body, groups, rows),
        mesh=mesh,
        in_specs=(data, data, P(("replica", "fsdp")), data) + weights,
        out_specs=(data, data, data) + weights,
        check_vma=False,
    )
```

```python
from functools import partial

import jax
import jax.numpy as jnp
import numpy as np
from jax import lax
from jax.experimental import pallas as pl
from jax.experimental.pallas import tpu as pltpu
from jax.sharding import PartitionSpec as P

H = 16
EPSILON = 1e-05
MASKED = -1e30
BF = jnp.bfloat16
F32 = jnp.float32


class Place:
    def __init__(self, groups, rows):
        self.groups = groups
        self.rows = rows
        self.ring = rows // 2
        rep = lax.axis_index("replica")
        row = lax.axis_index("fsdp")
        self.c = lax.rem(rep, 2)
        self.x = lax.div(rep, 2)
        self.y = lax.rem(row, 2)
        self.z = lax.div(row, 2)

    def core(self, v):
        return lax.ppermute(v, "replica", [(i, i ^ 1) for i in range(self.groups)])

    def across(self, v):
        return lax.ppermute(v, "replica", [(i, i ^ 2) for i in range(self.groups)])

    def pair(self, v):
        return lax.ppermute(v, "fsdp", [(i, i ^ 1) for i in range(self.rows)])

    def next(self, v):
        return lax.ppermute(v, "fsdp", [(i, (i + 2) % self.rows) for i in range(self.rows)])

    def ring_members(self):
        return [[2 * k + side for k in range(self.ring)] for side in range(2)]


def at(v, i, axis=0):
    return lax.dynamic_index_in_dim(v, i, axis, keepdims=False)


class Lane:
    def __init__(self, width):
        self.width = width
        self.past = []

    def __call__(self, send, v):
        if len(self.past) >= self.width:
            v, _ = lax.optimization_barrier((v, self.past[-self.width]))
        got = send(v)
        self.past.append(got)
        return got


def ring_gather(place, piece):
    if place.ring <= 4:
        copies = jnp.broadcast_to(piece[None], (place.ring,) + piece.shape)
        return lax.all_to_all(copies, "fsdp", 0, 0, axis_index_groups=place.ring_members())
    return lax.all_gather(piece, "fsdp", axis_index_groups=place.ring_members())


def order_kernel(ring, split, mine, theirs, out, sems):
    rep = lax.axis_index("replica")
    c, x = lax.rem(rep, 2), lax.div(rep, 2)
    y = lax.rem(lax.axis_index("fsdp"), 2)
    copies = []
    for dc, block in enumerate((mine, theirs)):
        cc = 1 - c if dc else c
        for dx in range(2 if split else 1):
            for dy in range(2):
                yy = 1 - y if dy else y
                for z in range(ring):
                    if split:
                        xx = 1 - x if dx else x
                        src, dst = block.at[dx, dy, z], out.at[z, yy, xx, cc]
                    else:
                        src, dst = block.at[dy, z], out.at[z, yy, cc]
                    copies.append(pltpu.make_async_copy(src, dst, sems.at[len(copies)]))
    for copy in copies:
        copy.start()
    for copy in copies:
        copy.wait()


def in_order(place, split, mine, theirs):
    ring, rows, n = mine.shape[-3:]
    dims = (ring, 2, 2, 2) if split else (ring, 2, 2)
    if rows % 16 == 0:
        count = 2 * mine.size // (rows * n)
        out = pl.pallas_call(
            partial(order_kernel, ring, split),
            out_shape=jax.ShapeDtypeStruct(dims + (rows, n), mine.dtype),
            in_specs=[pl.BlockSpec(memory_space=pl.ANY)] * 2,
            out_specs=pl.BlockSpec(memory_space=pltpu.VMEM),
            scratch_shapes=[pltpu.SemaphoreType.DMA((count,))],
            cost_estimate=pl.CostEstimate(
                flops=0, transcendentals=0, bytes_accessed=4 * count * rows * n
            ),
            name="order",
        )(mine, theirs)
    else:
        both = jnp.stack([mine, theirs])
        at_c = (place.c, 1 - place.c)
        both = jnp.stack([at(both, i, 0) for i in at_c])
        if split:
            both = jnp.stack([at(both, i, 1) for i in (place.x, 1 - place.x)], 1)
        both = jnp.stack([at(both, i, both.ndim - 4) for i in (place.y, 1 - place.y)], both.ndim - 4)
        out = jnp.transpose(both, (3, 2, 1, 0, 4, 5) if split else (2, 1, 0, 3, 4))
    return out.reshape(-1, n)


class Gather:
    def __init__(self, place, lane, ring_lane, shard, split):
        self.place, self.lane, self.ring_lane, self.split = place, lane, ring_lane, split
        m, n = shard.shape
        if split:
            self.v = at(shard.reshape(4, m // 4, n), 2 * place.x + place.c)
        else:
            self.v = at(shard.reshape(2, m // 2, n), place.c)
        self.steps = [self.ring, self.pair] + ([self.across] if split else []) + [self.core]

    def ring(self):
        self.v = self.ring_lane(partial(ring_gather, self.place), self.v)

    def pair(self):
        self.v = jnp.stack([self.v, self.lane(self.place.pair, self.v)])

    def across(self):
        self.v = jnp.stack([self.v, self.lane(self.place.across, self.v)])

    def core(self):
        self.v = in_order(self.place, self.split, self.v, self.lane(self.place.core, self.v))


def run_steps(units):
    last = max(i + len(u.steps) for i, u in enumerate(units))
    for t in range(last):
        for i, u in enumerate(units):
            if 0 <= t - i < len(u.steps):
                u.steps[t - i]()


def gather_vectors(place, packed):
    a = ring_gather(place, packed)
    b = place.pair(a)
    both = jnp.stack([jnp.where(place.y == 0, a, b), jnp.where(place.y == 0, b, a)], 1)
    return both.reshape((place.rows,) + packed.shape)


def product_t(left, right):
    return lax.dot_general(
        left, right, (((0,), (0,)), ((), ())), preferred_element_type=F32
    )


def columns(v, k, i):
    w = v.shape[1] // k
    return lax.dynamic_slice(v, (0, i * w), (v.shape[0], w))


def join2(own, other, bit):
    first = jnp.where(bit == 0, own, other)
    second = jnp.where(bit == 0, other, own)
    return jnp.concatenate([first, second], -1)


def ring_sum(place, parts):
    if place.ring <= 4:
        came = lax.all_to_all(parts, "fsdp", 0, 0, axis_index_groups=place.ring_members())
        return jnp.sum(came.astype(F32), 0).astype(BF)
    return lax.psum_scatter(
        parts, "fsdp", scatter_dimension=0, axis_index_groups=place.ring_members()
    )


class Scatter:
    def __init__(self, place, lane, ring_lane, left, right, split):
        self.place, self.lane, self.ring_lane, self.split = place, lane, ring_lane, split
        self.left, self.right = left, right
        self.steps = [self.core] + ([self.across] if split else []) + [self.pair, self.ring]

    def core(self):
        c = self.place.c
        away = product_t(self.left, columns(self.right, 2, 1 - c)).astype(BF)
        self.right = columns(self.right, 2, c)
        self.came = self.lane(self.place.core, away)

    def across(self):
        x = self.place.x
        away = product_t(self.left, columns(self.right, 2, 1 - x))
        away = (away + columns(self.came, 2, 1 - x).astype(F32)).astype(BF)
        self.right, self.came = columns(self.right, 2, x), columns(self.came, 2, x)
        self.came_x = self.lane(self.place.across, away)

    def pair(self):
        part = product_t(self.left, self.right) + self.came.astype(F32)
        if self.split:
            part = part + self.came_x.astype(F32)
        part = part.astype(BF)
        part = part.reshape(self.place.ring, 2, -1, part.shape[1])
        y = self.place.y
        came = self.lane(self.place.pair, at(part, 1 - y, 1))
        self.kept = (at(part, y, 1).astype(F32) + came.astype(F32)).astype(BF)

    def ring(self):
        self.own = self.ring_lane(partial(ring_sum, self.place), self.kept)


def finish_all(place, lane, units):
    flat = [u.own.reshape(-1, 128) for u in units]
    sizes = [f.shape[0] for f in flat]
    own = jnp.concatenate(flat)
    came = lane(place.across, own)
    pieces, at_row = [], 0
    for u, size in zip(units, sizes):
        mine, other = own[at_row : at_row + size], came[at_row : at_row + size]
        at_row += size
        mine, other = mine.reshape(u.own.shape), other.reshape(u.own.shape)
        if u.split:
            pieces.append(join2(mine, other, place.x))
        else:
            pieces.append((mine.astype(F32) + other.astype(F32)).astype(BF))
    own = jnp.concatenate([p.reshape(-1, 128) for p in pieces])
    came = lane(place.core, own)
    out, at_row = [], 0
    for p in pieces:
        size = p.size // 128
        out.append(join2(p, came[at_row : at_row + size].reshape(p.shape), place.c).astype(F32))
        at_row += size
    return out


def scatter_vectors(place, lane, ring_lane, v):
    own = v.astype(BF)
    own = (own.astype(F32) + lane(place.core, own).astype(F32)).astype(BF)
    own = (own.astype(F32) + lane(place.across, own).astype(F32)).astype(BF)
    own = own.reshape((place.ring, 2) + own.shape[1:])
    came = lane(place.pair, at(own, 1 - place.y, 1))
    own = (at(own, place.y, 1).astype(F32) + came.astype(F32)).astype(BF)
    return ring_lane(partial(ring_sum, place), own).astype(F32)


PAIR = 128


def half_masks(rows):
    lane = lax.broadcasted_iota(jnp.int32, (rows, PAIR), 1)
    return (lane < PAIR // 2, lane >= PAIR // 2)


def dot_nt(a, b):
    return lax.dot_general(a, b, (((1,), (1,)), ((), ())), preferred_element_type=F32)


def attend_kernel(masked, scale, prefix_ref, q_ref, k_ref, v_ref, o_ref, p_ref):
    rows, keys = q_ref.shape[0], k_ref.shape[0]
    masks = half_masks(rows)
    if masked:
        i = lax.broadcasted_iota(jnp.int32, (rows, keys), 0)
        j = lax.broadcasted_iota(jnp.int32, (rows, keys), 1)
        allowed = (j <= i) | (j < prefix_ref[pl.program_id(0)])
    for pair in range(q_ref.shape[1] // PAIR):
        lanes = slice(pair * PAIR, (pair + 1) * PAIR)
        q, k, v = q_ref[:, lanes], k_ref[:, lanes], v_ref[:, lanes]
        both = []
        for h in range(2):
            s = dot_nt(jnp.where(masks[h], q, jnp.zeros_like(q)), k)
            if masked:
                s = jnp.where(allowed, s, MASKED)
            e = jnp.exp((s - jnp.max(s, -1, keepdims=True)) * scale)
            p = (e * (1.0 / jnp.sum(e, -1, keepdims=True))).astype(BF)
            p_ref[2 * pair + h] = p
            both.append(jnp.dot(p, v, preferred_element_type=F32))
        o_ref[:, lanes] = jnp.where(masks[0], both[0], both[1]).astype(BF)


def attend(q, k, v, prefix, batch, masked, group=8):
    rows, keys, d = q.shape[0] // batch, k.shape[0] // batch, q.shape[1]
    wide = group * d // H
    spec = lambda n: pl.BlockSpec((n, wide), lambda b, g, *_: (b, g))
    return pl.pallas_call(
        partial(attend_kernel, masked, (d // H) ** -0.5),
        grid_spec=pltpu.PrefetchScalarGridSpec(
            num_scalar_prefetch=1,
            grid=(batch, H // group),
            in_specs=[spec(rows), spec(keys), spec(keys)],
            out_specs=[
                spec(rows),
                pl.BlockSpec((None, group, rows, keys), lambda b, g, *_: (b, g, 0, 0)),
            ],
        ),
        out_shape=[
            jax.ShapeDtypeStruct(q.shape, BF),
            jax.ShapeDtypeStruct((batch, H, rows, keys), BF),
        ],
        compiler_params=pltpu.CompilerParams(vmem_limit_bytes=40 * 2**20),
        cost_estimate=pl.CostEstimate(
            flops=16 * q.size * keys * URGENT,
            transcendentals=0,
            bytes_accessed=(4 * q.size + 4 * k.size + 2 * batch * H * rows * keys) * URGENT,
        ),
        name="attend",
    )(prefix, q, k, v)


def attend_back_kernel(scale, do_ref, q_ref, k_ref, v_ref, p_ref, dq_ref, dk_ref, dv_ref):
    rows = q_ref.shape[0]
    half = PAIR // 2
    masks = half_masks(rows)
    for pair in range(q_ref.shape[1] // PAIR):
        lanes = slice(pair * PAIR, (pair + 1) * PAIR)
        do, q, k, v = do_ref[:, lanes], q_ref[:, lanes], k_ref[:, lanes], v_ref[:, lanes]
        do_t, q_t = do.T, q.T
        dq, dk_t, dv_t = [], [], []
        for h in range(2):
            p = p_ref[2 * pair + h]
            dp = dot_nt(jnp.where(masks[h], do, jnp.zeros_like(do)), v)
            pf = p.astype(F32)
            ds = (pf * (dp - jnp.sum(dp * pf, -1, keepdims=True))).astype(BF)
            dq.append(jnp.dot(ds, k, preferred_element_type=F32))
            part = slice(h * half, (h + 1) * half)
            dk_t.append(jnp.dot(q_t[part], ds, preferred_element_type=F32))
            dv_t.append(jnp.dot(do_t[part], p, preferred_element_type=F32))
        dq_ref[:, lanes] = (jnp.where(masks[0], dq[0], dq[1]) * scale).astype(BF)
        dk_ref[:, lanes] = (jnp.concatenate(dk_t, 0) * scale).astype(BF).T
        dv_ref[:, lanes] = jnp.concatenate(dv_t, 0).astype(BF).T


def attend_back(do, q, k, v, p, batch, group=8):
    rows, keys, d = q.shape[0] // batch, k.shape[0] // batch, q.shape[1]
    wide = group * d // H
    spec = lambda n: pl.BlockSpec((n, wide), lambda b, g: (b, g))
    return pl.pallas_call(
        partial(attend_back_kernel, (d // H) ** -0.5),
        grid=(batch, H // group),
        in_specs=[
            spec(rows), spec(rows), spec(keys), spec(keys),
            pl.BlockSpec((None, group, rows, keys), lambda b, g: (b, g, 0, 0)),
        ],
        out_specs=[spec(rows), spec(keys), spec(keys)],
        out_shape=[
            jax.ShapeDtypeStruct(q.shape, BF),
            jax.ShapeDtypeStruct(k.shape, BF),
            jax.ShapeDtypeStruct(v.shape, BF),
        ],
        compiler_params=pltpu.CompilerParams(vmem_limit_bytes=40 * 2**20),
        cost_estimate=pl.CostEstimate(
            flops=32 * q.size * keys * URGENT,
            transcendentals=0,
            bytes_accessed=(6 * q.size + 8 * k.size + 2 * batch * H * rows * keys) * URGENT,
        ),
        name="attend_back",
    )(do, q, k, v, p)


BIG = pltpu.CompilerParams(vmem_limit_bytes=58 * 2**20)
SPOT = pl.BlockSpec(memory_space=pl.ANY)
WHOLE = pl.BlockSpec(memory_space=pltpu.VMEM)
CHUNK = 128


def here():
    rep, row = lax.axis_index("replica"), lax.axis_index("fsdp")
    return lax.div(rep, 2), lax.rem(rep, 2), lax.div(row, 2), lax.rem(row, 2)


def flip(bit, by):
    return 1 - bit if by else bit


def pieces_of(refs, number, w, sems, act):
    x, c, _, y = here()
    rows, half = w.shape[2], w.shape[3] // 2
    dx, dc = flip(x, number // 2), flip(c, number % 2)
    halves = len(refs[0].shape) == 4

    def copy(src, dy, g):
        to = w.at[:, flip(y, dy), :, pl.ds(g * half, half)] if halves else w.at[:, flip(y, dy)]
        src = src.at[:, pl.ds(0, rows)]
        getattr(pltpu.make_async_copy(src, to, sems.at[2 * dy + g]), act)()

    if act == "wait":
        for dy in range(2):
            for g in range(2 if halves else 1):
                copy(refs[0].at[0] if halves else refs[0], dy, g)
        return
    for far in range(2):
        group = refs[4 * far : 4 * far + 4]
        if halves:
            p0, q0, p1, q1 = group

            @pl.when(dc == far)
            def _(p1=p1, q1=q1):
                copy(p1.at[dx], 0, 1)
                copy(q1.at[dx], 1, 1)

        for side in range(2):

            @pl.when((dc == far) & (dx == side))
            def _(group=group, side=side):
                if halves:
                    copy(group[side].at[0], 0, 0)
                    copy(group[side].at[1], 1, 0)
                else:
                    copy(group[2 * side], 0, 0)
                    copy(group[2 * side + 1], 1, 0)


def row_sum(v):
    return jnp.sum(v, 0, keepdims=True)


def normal(v):
    centered = v - jnp.mean(v, -1, keepdims=True)
    inverse = lax.rsqrt(jnp.mean(centered * centered, -1, keepdims=True) + EPSILON)
    return centered * inverse, inverse


def chunks(rows, step, do):
    def one(i, carry):
        do(pl.ds(pl.multiple_of(i * step, step), step))
        return carry

    lax.fori_loop(0, rows // step, one, 0)


def weight(w_ref, *lead):
    v = w_ref[lead] if lead else w_ref[...]
    return v.reshape(v.shape[-4] * v.shape[-3] * v.shape[-2], v.shape[-1])


def times(a_ref, w_ref, put):
    put(slice(None), jnp.dot(a_ref[...], weight(w_ref), preferred_element_type=F32))


def times_t(pairs, put):
    total = None
    for a_ref, w_ref in pairs:
        part = dot_nt(a_ref[...], weight(w_ref))
        total = part if total is None else total + part
    put(slice(None), total)


def loaded(m, n, count):
    return [pltpu.VMEM((4, 2, m, n), BF)] * count + [pltpu.SemaphoreType.DMA((count, 4))]


URGENT = 400


def cost(flops, *arrays):
    return pl.CostEstimate(
        flops=flops * URGENT,
        transcendentals=0,
        bytes_accessed=sum(a.size * a.dtype.itemsize for a in arrays) * URGENT,
    )


def shape(dims, dtype):
    return jax.ShapeDtypeStruct(dims, dtype)


def pack_kernel(count, *rest):
    mats, vectors, out = rest[:4], rest[4 : 4 + count], rest[-1]
    x, c, _, _ = here()
    m, n = mats[0].shape
    half = n // 2
    for number, mat in enumerate(mats):

        @pl.when(2 * x + c == number)
        def _(mat=mat):
            for g in range(2):
                out[g, :m, :] = mat[:, g * half : (g + 1) * half]

    parts = []
    for v in vectors:
        parts += [v[i : i + m].reshape(1, m) for i in range(0, v.shape[0], m)]
    parts += [jnp.zeros((1, m), BF)] * (8 * n // m - len(parts))
    row = half // m
    rows = [jnp.concatenate(parts[row * i : row * (i + 1)], 1) for i in range(16)]
    for g in range(2):
        out[g, m:, :] = jnp.concatenate(rows[8 * g : 8 * g + 8], 0)


def pack(mats, vectors):
    m, n = mats[0].shape
    return pl.pallas_call(
        partial(pack_kernel, len(vectors)),
        in_specs=[WHOLE] * (4 + len(vectors)),
        out_specs=WHOLE,
        out_shape=shape((2, m + 8, n // 2), BF),
        compiler_params=BIG,
        name="pack",
    )(*mats, *vectors)


def first_kernel(x_ref, vec_ref, *rest):
    refs, (act_ref, q_ref, k_ref, v_ref), (wq, wk, wv, sems) = rest[:8], rest[8:12], rest[12:]
    for i, w in enumerate((wq, wk, wv)):
        pieces_of(refs, i, w, sems.at[i], "start")

    def norm(rows):
        n, _ = normal(x_ref[rows, :].astype(F32))
        act_ref[rows, :] = (n * vec_ref[0:1] + vec_ref[1:2]).astype(BF)

    chunks(x_ref.shape[0], CHUNK, norm)
    for i, (w, out, bias) in enumerate(((wq, q_ref, 2), (wk, k_ref, None), (wv, v_ref, 3))):
        pieces_of(refs, i, w, sems.at[i], "wait")

        def put(lanes, v, out=out, bias=bias):
            if bias is not None:
                v = v + vec_ref[bias : bias + 1, lanes]
            out[:, lanes] = v.astype(BF)

        times(act_ref, w, put)


def first(x, vecs, unit, m):
    like = shape(x.shape, BF)
    return pl.pallas_call(
        first_kernel,
        in_specs=[WHOLE, WHOLE] + [SPOT] * 8,
        out_specs=[WHOLE] * 4,
        out_shape=[like] * 4,
        scratch_shapes=loaded(m, x.shape[1], 3),
        compiler_params=BIG,
        cost_estimate=cost(6 * x.size * x.shape[1], x, x, x, x, x, *unit),
        name="first",
    )(x, vecs, *unit)


def project_kernel(second, numbers, rows_of, a_ref, res_ref, vec_ref, *rest):
    refs = rest[:16] if second else rest[:8]
    rest = rest[len(refs) :]
    outs, (w1, *rest) = rest[: 3 if second else 2], rest[3 if second else 2 :]
    mid_ref, act_ref = outs[:2]
    sems = rest[-1]
    bias, gain, shift, bias2 = rows_of
    pieces_of(refs[:8], numbers[0], w1, sems.at[0], "start")
    if second:
        w2 = rest[0]
        pieces_of(refs[8:], numbers[1], w2, sems.at[1], "start")
    pieces_of(refs[:8], numbers[0], w1, sems.at[0], "wait")

    def put(lanes, v):
        mid_ref[:, lanes] = res_ref[:, lanes].astype(F32) + (v + vec_ref[bias : bias + 1, lanes])

    times(a_ref, w1, put)

    def norm(rows):
        n, _ = normal(mid_ref[rows, :])
        act_ref[rows, :] = (n * vec_ref[gain : gain + 1] + vec_ref[shift : shift + 1]).astype(BF)

    chunks(a_ref.shape[0], CHUNK, norm)
    if second:
        pieces_of(refs[8:], numbers[1], w2, sems.at[1], "wait")

        def put2(lanes, v):
            outs[2][:, lanes] = (v + vec_ref[bias2 : bias2 + 1, lanes]).astype(BF)

        times(act_ref, w2, put2)


def project(a, residual, vecs, rows_of, units, numbers, m, name):
    second = len(units) == 2
    refs = [r for u in units for r in u]
    return pl.pallas_call(
        partial(project_kernel, second, numbers, rows_of),
        in_specs=[WHOLE] * 3 + [SPOT] * len(refs),
        out_specs=[WHOLE] * (3 if second else 2),
        out_shape=[shape(a.shape, F32), shape(a.shape, BF)] + ([shape(a.shape, BF)] if second else []),
        scratch_shapes=loaded(m, a.shape[1], len(units)),
        compiler_params=BIG,
        cost_estimate=cost(2 * len(units) * a.size * a.shape[1], a, a, a, a, a, a, *refs[:4]),
        name=name,
    )(a, residual, vecs, *refs)


def query_kernel(bias, a_ref, vec_ref, *rest):
    refs, out_ref, (w, sems) = rest[:8], rest[8], rest[9:]
    pieces_of(refs, 0, w, sems.at[0], "start")
    pieces_of(refs, 0, w, sems.at[0], "wait")

    def put(lanes, v):
        out_ref[:, lanes] = (v + vec_ref[bias : bias + 1, lanes]).astype(BF)

    times(a_ref, w, put)


def query(a, vecs, bias, unit, m):
    return pl.pallas_call(
        partial(query_kernel, bias),
        in_specs=[WHOLE] * 2 + [SPOT] * 8,
        out_specs=WHOLE,
        out_shape=shape(a.shape, BF),
        scratch_shapes=loaded(m, a.shape[1], 1),
        compiler_params=BIG,
        cost_estimate=cost(2 * a.size * a.shape[1], a, a, *unit[:2]),
        name="query",
    )(a, vecs, *unit)


def memory_kernel(e_ref, vec_ref, *rest):
    refs, (k_ref, v_ref), (wk, wv, sems) = rest[:8], rest[8:10], rest[10:]

    @pl.when(pl.program_id(0) == 0)
    def _():
        for i, w in enumerate((wk, wv)):
            pieces_of(refs, i + 1, w, sems.at[i], "start")
        for i, w in enumerate((wk, wv)):
            pieces_of(refs, i + 1, w, sems.at[i], "wait")

    def put_k(lanes, v):
        k_ref[:, lanes] = v.astype(BF)

    def put_v(lanes, v):
        v_ref[:, lanes] = (v + vec_ref[8:9, lanes]).astype(BF)

    times(e_ref, wk, put_k)
    times(e_ref, wv, put_v)


def memory(e, vecs, unit, m, step=512):
    d = e.shape[1]
    blk = pl.BlockSpec((step, d), lambda i: (i, 0))
    return pl.pallas_call(
        memory_kernel,
        grid=(e.shape[0] // step,),
        in_specs=[blk, pl.BlockSpec(vecs.shape, lambda i: (0, 0))] + [SPOT] * 8,
        out_specs=[blk, blk],
        out_shape=[shape(e.shape, BF)] * 2,
        scratch_shapes=loaded(m, d, 2),
        compiler_params=BIG,
        cost_estimate=cost(4 * e.size * d, e, e, e, *unit),
        name="memory",
    )(e, vecs, *unit)


def memory_back_kernel(dk_ref, dv_ref, *rest):
    refs, (out_ref, sum_ref), (wk, wv, sems) = rest[:8], rest[8:10], rest[10:]

    @pl.when(pl.program_id(0) == 0)
    def _():
        for i, w in enumerate((wk, wv)):
            pieces_of(refs, i + 1, w, sems.at[i], "start")
        sum_ref[...] = jnp.zeros_like(sum_ref)
        for i, w in enumerate((wk, wv)):
            pieces_of(refs, i + 1, w, sems.at[i], "wait")

    def put(lanes, v):
        out_ref[:, lanes] = v

    times_t([(dk_ref, wk), (dv_ref, wv)], put)
    sum_ref[0:1] += row_sum(dv_ref[...].astype(F32))


def memory_back(dk, dv, unit, m, step=512):
    d = dk.shape[1]
    blk = pl.BlockSpec((step, d), lambda i: (i, 0))
    return pl.pallas_call(
        memory_back_kernel,
        grid=(dk.shape[0] // step,),
        in_specs=[blk, blk] + [SPOT] * 8,
        out_specs=[blk, pl.BlockSpec((8, d), lambda i: (0, 0))],
        out_shape=[shape(dk.shape, F32), shape((8, d), F32)],
        scratch_shapes=loaded(m, d, 2),
        compiler_params=BIG,
        cost_estimate=cost(4 * dk.size * d, dk, dk, dk, dk, *unit),
        name="memory_back",
    )(dk, dv, *unit)


def apply_norm_back(rows, dact, v, gain, residual, sums):
    n, inverse = normal(v)
    sums[0:1] += row_sum(dact * n)
    sums[1:2] += row_sum(dact)
    q = dact * gain
    mean_one = jnp.mean(q, -1, keepdims=True)
    mean_two = jnp.mean(q * n, -1, keepdims=True)
    return residual + inverse * (q - mean_one - n * mean_two)


def cross_back_kernel(dq_ref, mid_ref, dmid_ref, vec_ref, *rest):
    refs, (out_ref, low_ref, do_ref, sum_ref), (dact, w1, w2, sems) = rest[:16], rest[16:20], rest[20:]
    pieces_of(refs[:8], 0, w1, sems.at[0], "start")
    pieces_of(refs[8:], 3, w2, sems.at[1], "start")
    sum_ref[...] = jnp.zeros_like(sum_ref)
    sum_ref[2:3] = row_sum(dq_ref[...].astype(F32))
    pieces_of(refs[:8], 0, w1, sems.at[0], "wait")

    def put(lanes, v):
        dact[:, lanes] = v

    times_t([(dq_ref, w1)], put)

    def back(rows):
        total = apply_norm_back(
            rows, dact[rows, :], mid_ref[rows, :], vec_ref[5:6], dmid_ref[rows, :], sum_ref
        )
        out_ref[rows, :] = total
        low = total.astype(BF)
        low_ref[rows, :] = low
        sum_ref[3:4] += row_sum(low.astype(F32))

    chunks(dq_ref.shape[0], CHUNK, back)
    pieces_of(refs[8:], 3, w2, sems.at[1], "wait")

    def put2(lanes, v):
        do_ref[:, lanes] = v.astype(BF)

    times_t([(low_ref, w2)], put2)


def cross_back(dq, mid, dmid, vecs, cross_unit, self_unit, m):
    d = dq.shape[1]
    return pl.pallas_call(
        cross_back_kernel,
        in_specs=[WHOLE] * 4 + [SPOT] * 16,
        out_specs=[WHOLE] * 4,
        out_shape=[shape(dq.shape, F32), shape(dq.shape, BF), shape(dq.shape, BF), shape((8, d), F32)],
        scratch_shapes=[pltpu.VMEM(dq.shape, F32)] + loaded(m, d, 2),
        compiler_params=BIG,
        cost_estimate=cost(4 * dq.size * d, mid, mid, mid, dq, dq, dq, *cross_unit[:4]),
        name="cross_back",
    )(dq, mid, dmid, vecs, *cross_unit, *self_unit)


def self_back_kernel(dq_ref, dk_ref, dv_ref, x_ref, dmid_ref, vec_ref, *rest):
    refs, (out_ref, sum_ref), (dact, wq, wk, wv, sems) = rest[:8], rest[8:10], rest[10:]
    for i, w in enumerate((wq, wk, wv)):
        pieces_of(refs, i, w, sems.at[i], "start")
    sum_ref[...] = jnp.zeros_like(sum_ref)
    sum_ref[2:3] = row_sum(dq_ref[...].astype(F32))
    sum_ref[3:4] = row_sum(dv_ref[...].astype(F32))
    for i, w in enumerate((wq, wk, wv)):
        pieces_of(refs, i, w, sems.at[i], "wait")

    def put(lanes, v):
        dact[:, lanes] = v

    times_t([(dq_ref, wq), (dk_ref, wk), (dv_ref, wv)], put)

    def back(rows):
        out_ref[rows, :] = apply_norm_back(
            rows, dact[rows, :], x_ref[rows, :].astype(F32), vec_ref[0:1], dmid_ref[rows, :], sum_ref
        )

    chunks(dq_ref.shape[0], CHUNK, back)


def self_back(dq, dk, dv, x, dmid, vecs, unit, m):
    d = dq.shape[1]
    return pl.pallas_call(
        self_back_kernel,
        in_specs=[WHOLE] * 6 + [SPOT] * 8,
        out_specs=[WHOLE] * 2,
        out_shape=[shape(dq.shape, F32), shape((8, d), F32)],
        scratch_shapes=[pltpu.VMEM(dq.shape, F32)] + loaded(m, d, 3),
        compiler_params=BIG,
        cost_estimate=cost(6 * dq.size * d, dmid, dmid, dq, dq, dq, dq, *unit),
        name="self_back",
    )(dq, dk, dv, x, dmid, vecs, *unit)


def output_back_kernel(d_ref, *rest):
    refs, do_ref, (w, sems) = rest[:8], rest[8], rest[9:]
    pieces_of(refs, 3, w, sems.at[0], "start")
    pieces_of(refs, 3, w, sems.at[0], "wait")

    def put(lanes, v):
        do_ref[:, lanes] = v.astype(BF)

    times_t([(d_ref, w)], put)


def output_back(dlow, unit, m):
    d = dlow.shape[1]
    return pl.pallas_call(
        output_back_kernel,
        in_specs=[WHOLE] + [SPOT] * 8,
        out_specs=WHOLE,
        out_shape=shape(dlow.shape, BF),
        scratch_shapes=loaded(m, d, 1),
        compiler_params=BIG,
        cost_estimate=cost(2 * dlow.size * d, dlow, dlow, *unit[:2]),
        name="output_back",
    )(dlow, *unit)


def send_off(block, away, keep, dx, dc, spot, sem):
    @pl.when(dc == 1)
    def _():
        pltpu.make_async_copy(block, away.at[(dx,) + spot], sem).start()

    @pl.when(dc == 0)
    def _():
        pltpu.make_async_copy(block, keep.at[(dx,) + spot], sem).start()


def dot_tn(a, b):
    return lax.dot_general(a, b, (((0,), (0,)), ((), ())), preferred_element_type=F32)


def grads_kernel(sides, *rest):
    count = 1 + max(sides)
    left_refs, right_refs = rest[:count], rest[count : count + 4]
    away, keep, out, sems = rest[count + 4 :]
    x, c, z, y = here()
    half = out.shape[-1]
    for number, side in enumerate(sides):
        for zz in range(4):
            v = dot_tn(left_refs[side][:, zz * 256 : (zz + 1) * 256], right_refs[number][...]).astype(BF)
            for yy in range(2):
                for g in range(2):
                    out[number, g, flip(y, yy), zz] = v[yy * 128 : (yy + 1) * 128, g * half : (g + 1) * half]
        dx, dc = flip(x, number // 2), flip(c, number % 2)
        send_off(out.at[number], away, keep, dx, dc, (), sems.at[number])
    for number in range(4):
        pltpu.make_async_copy(out.at[number], keep.at[0], sems.at[number]).wait()


def grads(lefts, rights, sides, name):
    d, n = lefts[0].shape[1], rights[0].shape[1]
    dims = (2, 2, 2, 4, d // 8, n // 2)
    return pl.pallas_call(
        partial(grads_kernel, sides),
        in_specs=[WHOLE] * (len(lefts) + 4),
        out_specs=[SPOT] * 2,
        out_shape=[shape(dims, BF)] * 2,
        scratch_shapes=[pltpu.VMEM((4,) + dims[1:], BF), pltpu.SemaphoreType.DMA((4,))],
        compiler_params=BIG,
        cost_estimate=cost(2 * sum(r.size for r in rights) * d, *lefts, *rights, *rights, *rights),
        name=name,
    )(*lefts, *rights)


def sums_kernel(counts, joined, *rest):
    ins, outs = rest[: sum(counts)], rest[sum(counts) :]
    at_in = 0
    for i, count in enumerate(counts):
        total = ins[at_in][...].astype(F32)
        for r in ins[at_in + 1 : at_in + count]:
            total = total + r[...].astype(F32)
        at_in += count
        total = total.astype(BF)
        if joined:
            wide = total.shape[-1]
            outs[0][:, :, i * wide : (i + 1) * wide] = total
        else:
            outs[i][...] = total.reshape(outs[i].shape)


def sums(steps, *groups, joined=False):
    ins = [i for _, _, _, members in groups for i in members]
    outs = [g[:3] for g in groups]
    if joined:
        (p, m, n), (q, _, _), to = outs[0]
        outs = [((p, m, n * len(groups)), (q, m, n * len(groups)), to)]
    out = pl.pallas_call(
        partial(sums_kernel, tuple(len(g[3]) for g in groups), joined),
        grid=(steps,),
        in_specs=[pl.BlockSpec(block, to) for _, block, to in ins],
        out_specs=[pl.BlockSpec(o[1], o[2]) for o in outs],
        out_shape=[shape(o[0], BF) for o in outs],
        cost_estimate=pl.CostEstimate(
            flops=0,
            transcendentals=0,
            bytes_accessed=2 * URGENT * sum(int(np.prod(g[0])) * (1 + len(g[3])) for g in groups),
        ),
        name="sums",
    )(*[v for v, _, _ in ins])
    return out[0] if joined else out


def grads_of(left, lefts, rights, sides, name):
    return grads([left] + list(lefts), rights, sides, name)


def ffn_kernel(last, first_row, act_ref, dy_ref, mid_ref, vec_ref, *rest):
    begin = rest[:2] if last else ()
    rest = rest[len(begin) :]
    refs, rest = rest[:8], rest[8:]
    outs, rest = rest[: 4 if last else 2], rest[4 if last else 2 :]
    dbe_ref, away, keep = rest[:3]
    hid_ref, dexp_ref, acc, dact, out, we0, wd0, we1, wd1, sems, out_sems = rest[3:]
    rows, d = act_ref.shape
    half_n = d // 2
    x, c, z, y = here()
    mats = ((we0, wd0), (we1, wd1))
    for t in range(2):
        for n in range(2):
            pieces_of(refs, 2 * t + n, mats[t][n], sems.at[2 * t + n], "start")
    dbe_ref[...] = jnp.zeros_like(dbe_ref)
    if last:
        outs[3][...] = jnp.zeros_like(outs[3])
    for t in range(2):
        for n in range(2):
            pieces_of(refs, 2 * t + n, mats[t][n], sems.at[2 * t + n], "wait")
        bias = vec_ref[first_row + t : first_row + t + 1]

        def half(r, t=t, bias=bias):
            we, wd = weight(mats[t][0]), weight(mats[t][1])
            u = jnp.dot(act_ref[r, :], we, preferred_element_type=F32) + bias
            cdf = 0.5 * (1.0 + lax.erf(u * np.float32(0.5**0.5)))
            pdf = jnp.exp(-0.5 * u * u) * np.float32((2 * np.pi) ** -0.5)
            hid = (u * cdf).astype(BF)
            hid_ref[r, :] = hid
            dexp = (dot_nt(dy_ref[r, :], wd) * (cdf + u * pdf)).astype(BF)
            dexp_ref[r, :] = dexp
            dbe_ref[t : t + 1] += row_sum(dexp.astype(F32))
            down, back = jnp.dot(hid, wd, preferred_element_type=F32), dot_nt(dexp, we)
            if t == 0 and not last:
                acc[r, :], dact[r, :] = down, back
            elif t == 0:
                acc[r, :], dact[r, :] = begin[0][r, :] + down, begin[1][r, :] + back
            else:
                acc[r, :] += down
                dact[r, :] += back

        chunks(rows, 256, half)
        for number, (a_ref, b_ref) in ((2 * t, (act_ref, dexp_ref)), (2 * t + 1, (hid_ref, dy_ref))):
            for zz in range(4):
                v = dot_tn(a_ref[:, zz * 256 : (zz + 1) * 256], b_ref[...]).astype(BF)
                for yy in range(2):
                    for g in range(2):
                        part = v[yy * 128 : (yy + 1) * 128, g * half_n : (g + 1) * half_n]
                        out[number, g, flip(y, yy), zz] = part
            dx, dc = flip(x, number // 2), flip(c, number % 2)
            send_off(out.at[number], away, keep, dx, dc, (), out_sems.at[number])
    if last:
        out_ref, dmid_ref, low_ref, sum_ref = outs

        def back(r):
            mid = mid_ref[r, :]
            out_ref[r, :] = (mid + (acc[r, :] + vec_ref[12:13])).astype(BF)
            dy = dy_ref[r, :].astype(F32)
            total = apply_norm_back(r, dact[r, :], mid, vec_ref[10:11], dy, sum_ref)
            dmid_ref[r, :] = total
            low = total.astype(BF)
            low_ref[r, :] = low
            sum_ref[2:3] += row_sum(dy)
            sum_ref[3:4] += row_sum(low.astype(F32))

        chunks(rows, CHUNK, back)
    else:
        outs[0][...] = acc[...]
        outs[1][...] = dact[...]
    for number in range(4):
        pltpu.make_async_copy(out.at[number], keep.at[0], out_sems.at[number]).wait()


def ffn(act, dy, mid, vecs, unit, m, begin, first_row):
    rows, d = act.shape
    last = bool(begin)
    dims = (2, 2, 2, 4, m, d // 2)
    if last:
        heads = [shape(act.shape, BF), shape(act.shape, F32), shape(act.shape, BF), shape((8, d), F32)]
    else:
        heads = [shape(act.shape, F32)] * 2
    return pl.pallas_call(
        partial(ffn_kernel, last, first_row),
        in_specs=[WHOLE] * (4 + len(begin)) + [SPOT] * 8,
        out_specs=[WHOLE] * (len(heads) + 1) + [SPOT] * 2,
        out_shape=heads + [shape((8, d), F32)] + [shape(dims, BF)] * 2,
        scratch_shapes=[
            pltpu.VMEM((rows, d), BF),
            pltpu.VMEM((rows, d), BF),
            pltpu.VMEM((rows, d), F32),
            pltpu.VMEM((rows, d), F32),
            pltpu.VMEM((4,) + dims[1:], BF),
        ]
        + loaded(m, d, 4)
        + [pltpu.SemaphoreType.DMA((4,))],
        compiler_params=BIG,
        cost_estimate=cost(24 * act.size * d, *unit, *unit, mid, mid),
        name="ffn",
    )(act, dy, mid, vecs, *begin, *unit)


def finish_kernel(count, *rest):
    units, outs, held = [rest[3 * i : 3 * i + 3] for i in range(count)], rest[3 * count : -1], rest[-1]
    x, c, _, _ = here()
    m, n = units[0][0].shape
    for i, (own_ref, x_ref, core_ref) in enumerate(units):
        held[0], held[2] = own_ref[...], x_ref[...]
        held[1], held[3] = core_ref[0], core_ref[1]
        for number in range(4):
            j = flip(x, number // 2) * 2 + flip(c, number % 2)
            v = held[j].astype(F32)
            t = 2 * i + number // 2
            if count == 1:
                outs[number][...] = v
            elif number % 2:
                outs[1][t * m : (t + 1) * m] = v
            else:
                for f in range(n // 128):
                    to = (f * 4 + t) * 128
                    outs[0][:, to : to + 128] = v[:, f * 128 : (f + 1) * 128]


def finish(own, from_x, from_core, parts=()):
    units = ((own, from_x, from_core), *parts)
    m, n = own.shape
    dims = [(m, n)] * 4 if len(units) == 1 else [(m, 4 * n), (4 * m, n)]
    return pl.pallas_call(
        partial(finish_kernel, len(units)),
        in_specs=[WHOLE] * (3 * len(units)),
        out_specs=[WHOLE] * len(dims),
        out_shape=[shape(s, F32) for s in dims],
        scratch_shapes=[pltpu.VMEM((4, m, n), BF)],
        compiler_params=BIG,
        cost_estimate=cost(0, *[v for u in units for v in u] * 3),
        name="finish",
    )(*[v for u in units for v in u])


def product(left, right):
    return jnp.dot(left, right, preferred_element_type=F32)


def product_nt(left, right):
    return lax.dot_general(
        left, right, (((1,), (1,)), ((), ())), preferred_element_type=F32
    )


def moments(values):
    average = jnp.mean(values, -1, keepdims=True)
    centered = values - average
    variance = jnp.mean(centered * centered, -1, keepdims=True)
    inverse = lax.rsqrt(variance + EPSILON)
    return (centered * inverse, inverse)


def norm_back(grad_out, normed, inverse, gain_vec):
    gain_grad = jnp.sum(grad_out * normed, 0)
    shift_grad = jnp.sum(grad_out, 0)
    scaled = grad_out * gain_vec
    mean_one = jnp.mean(scaled, -1, keepdims=True)
    mean_two = jnp.mean(scaled * normed, -1, keepdims=True)
    return (inverse * (scaled - mean_one - normed * mean_two), gain_grad, shift_grad)


def gelu_both(u):
    cdf = 0.5 * (1.0 + lax.erf(u * np.float32(0.5**0.5)))
    pdf = jnp.exp(-0.5 * u * u) * np.float32((2 * np.pi) ** -0.5)
    return (u * cdf).astype(BF), (cdf + u * pdf).astype(BF)


def body(
    groups,
    rows,
    decoder_input,
    encoder_out,
    prefix_length,
    output_grad,
    self_query,
    self_key,
    self_value,
    self_output,
    selfquery_bias,
    selfvalue_bias,
    self_attention_output_bias,
    cross_query,
    cross_key,
    cross_value,
    cross_output,
    crossquery_bias,
    crossvalue_bias,
    crossoutput_bias,
    expand_weight,
    expand_bias,
    down_projection_weight,
    reduce_bias,
    selfnorm_gain,
    selfnorm_bias,
    crossnorm_gain,
    crossnorm_bias,
    finalnorm_gain,
    finalnorm_bias,
):
    place = Place(groups, rows)
    batch, seq, d = decoder_input.shape
    m = self_query.shape[0]
    ff = expand_weight.shape[1]
    fl = ff // rows // 2
    k4 = ff // d

    small = [
        selfnorm_gain, selfnorm_bias, selfquery_bias, selfvalue_bias, self_attention_output_bias,
        crossnorm_gain, crossnorm_bias, crossquery_bias, crossvalue_bias, crossoutput_bias,
        finalnorm_gain, finalnorm_bias, reduce_bias,
    ]
    packed = jnp.concatenate([jnp.stack(small), expand_bias.reshape(k4, m)])
    vecs = gather_vectors(place, packed).astype(F32)
    (g1, b1, bq, bv, bo, g2, b2, bcq, bcv, bco, g3, b3, br) = [
        vecs[:, i].reshape(d) for i in range(13)
    ]
    be = vecs[:, 13:].reshape(rows, 2, fl)

    expand_halves = [
        expand_weight.reshape(m, rows, 2, fl)[:, :, h].reshape(m, rows * fl) for h in range(2)
    ]
    down_halves = [down_projection_weight[h * fl : (h + 1) * fl] for h in range(2)]

    lane, ring_lane = Lane(4), Lane(2)
    gathers = [
        Gather(place, lane, ring_lane, shard, split)
        for shard, split in (
            (jnp.concatenate([self_query, self_key], 1), True),
            (self_value, False),
            (jnp.concatenate([cross_key, cross_value], 1), True),
            (self_output, False),
            (jnp.concatenate([cross_query, cross_output], 1), True),
            (expand_halves[0], True),
            (expand_halves[1], True),
            (down_halves[0], False),
            (down_halves[1], True),
        )
    ]
    run_steps(gathers)
    w_qk, w_v, w_ckv, w_o, w_cqo, *w_ff = [u.v for u in gathers]
    w_e, w_d = w_ff[:2], w_ff[2:]

    x = decoder_input.reshape(batch * seq, d).astype(F32)
    e = encoder_out.reshape(-1, d)
    dy = output_grad.reshape(batch * seq, d)

    n1, i1 = moments(x)
    act1 = (n1 * g1 + b1).astype(BF)
    qk = product(act1, w_qk)
    q = (qk[:, :d] + bq).astype(BF)
    k = qk[:, d:].astype(BF)
    v = (product(act1, w_v) + bv).astype(BF)
    o, p = attend(q, k, v, prefix_length, batch, True)
    mid1 = x + (product(o, w_o) + bo)
    n2, i2 = moments(mid1)
    act2 = (n2 * g2 + b2).astype(BF)
    w_cq, w_co = w_cqo[:, :d], w_cqo[:, d:]
    cq = (product(act2, w_cq) + bcq).astype(BF)
    ckv = product(e, w_ckv)
    ck = ckv[:, :d].astype(BF)
    cv = (ckv[:, d:] + bcv).astype(BF)
    co, cp = attend(cq, ck, cv, prefix_length, batch, False)
    mid2 = mid1 + (product(co, w_co) + bco)
    n3, i3 = moments(mid2)
    act3 = (n3 * g3 + b3).astype(BF)
    hidden, slope = [], []
    for h in range(2):
        hid, slo = gelu_both(product(act3, w_e[h]) + be[:, h].reshape(-1))
        hidden.append(hid)
        slope.append(slo)
    layer_out = (mid2 + (product(hidden[0], w_d[0]) + product(hidden[1], w_d[1]) + br)).astype(BF)

    scatter = partial(Scatter, place, lane, ring_lane)
    dyf = dy.astype(F32)
    g_down = [scatter(hidden[0], dy, True), scatter(hidden[1], dy, False)]
    dexp = [(product_nt(dy, w_d[h]) * slope[h].astype(F32)).astype(BF) for h in range(2)]
    g_exp = [scatter(act3, dexp[0], True), scatter(act3, dexp[1], False)]
    dact3 = product_nt(dexp[0], w_e[0]) + product_nt(dexp[1], w_e[1])
    dn, gg3, gb3 = norm_back(dact3, n3, i3, g3)
    dmid2 = dyf + dn
    dcross = dmid2.astype(BF)
    g_co = scatter(co, dcross, True)
    dco = product_nt(dcross, w_co).astype(BF)
    dcq, dck, dcv = attend_back(dco, cq, ck, cv, cp, batch)
    g_ck = scatter(e, dck, True)
    g_cv = scatter(e, dcv, False)
    g_cq = scatter(act2, dcq, False)
    encoder_grad = product_nt(jnp.concatenate([dck, dcv], 1), w_ckv)
    dn, gg2, gb2 = norm_back(product_nt(dcq, w_cq), n2, i2, g2)
    dmid1 = dmid2 + dn
    dself = dmid1.astype(BF)
    g_so = scatter(o, dself, True)
    dao = product_nt(dself, w_o).astype(BF)
    dq, dk, dv = attend_back(dao, q, k, v, p, batch)
    g_sv = scatter(act1, dv, False)
    g_sq = scatter(act1, dq, True)
    g_sk = scatter(act1, dk, True)
    dact1 = product_nt(jnp.concatenate([dq, dk], 1), w_qk) + product_nt(dv, w_v)
    dn, gg1, gb1 = norm_back(dact1, n1, i1, g1)
    input_grad = dmid1 + dn

    def column_sum(t):
        return jnp.sum(t.astype(F32), 0)

    dbe = jnp.stack([column_sum(t).reshape(rows, fl) for t in dexp], 1).reshape(rows, k4, m)
    early = [
        gg2, gb2, column_sum(dcq), column_sum(dcv), column_sum(dcross),
        gg3, gb3, column_sum(dy), column_sum(dself),
    ]
    early = jnp.concatenate([jnp.stack([t.reshape(rows, m) for t in early], 1), dbe], 1)
    late = [gg1, gb1, column_sum(dq), column_sum(dv)]
    late = jnp.stack([t.reshape(rows, m) for t in late], 1)

    first = g_down + g_exp + [g_co, g_cv, g_ck, g_cq, g_so]
    second = [g_sv, g_sq, g_sk]
    run_steps(first + second)
    early = scatter_vectors(place, lane, ring_lane, early)
    (*g_ff, g_co, g_cv, g_ck, g_cq, g_so) = finish_all(place, lane, first)
    g_down, g_exp = g_ff[:2], g_ff[2:]
    late = scatter_vectors(place, lane, ring_lane, late)
    g_sv, g_sq, g_sk = finish_all(place, lane, second)

    g_exp = jnp.stack([t.reshape(m, rows, fl) for t in g_exp], 2).reshape(m, ff)
    g_down = jnp.concatenate(g_down, 0)
    return (
        layer_out.reshape(batch, seq, d),
        input_grad.reshape(batch, seq, d),
        encoder_grad.reshape(encoder_out.shape),
        g_sq, g_sk, g_sv, g_so,
        late[2], late[3], early[8],
        g_cq, g_ck, g_cv, g_co,
        early[2], early[3], early[4],
        g_exp, early[9:].reshape(-1), g_down, early[7],
        late[0], late[1], early[0], early[1], early[5], early[6],
    )


class Order:
    def __init__(self):
        self.sent, self.ran, self.open = [], [], []

    def send(self, move, v, hold=2):
        v = self.see(v)
        got = move(v)
        self.sent.append(v)
        self.open.append([hold, got])
        return got

    def see(self, v):
        return lax.optimization_barrier((v, *self.ran))[0] if self.ran else v

    def run(self, kernel, v, *rest, **named):
        due = [got for hold, got in self.open if hold == 0]
        self.open = [[hold - 1, got] for hold, got in self.open if hold > 0]
        before = (*self.sent, *self.ran, *due)
        if before:
            v, *_ = lax.optimization_barrier((v, *before))
        out = kernel(v, *rest, **named)
        self.sent, self.ran = [], [out[0] if isinstance(out, (list, tuple)) else out]
        return out


class HalfUnit:
    def __init__(self, place, order, piece):
        self.place, self.order, self.piece = place, order, piece

    def ring(self):
        a = self.order.send(partial(ring_gather, self.place), self.piece)
        self.a0, self.a1 = a[:, 0], a[:, 1]

    def one(self):
        self.p0 = jnp.stack([self.a0, self.order.send(self.place.pair, self.a0)])
        self.p1 = jnp.stack([self.a1, self.order.send(self.place.across, self.a1)])

    def two(self):
        self.q0 = self.order.send(self.place.across, self.p0)
        self.q1 = self.order.send(self.place.pair, self.p1)
        self.c0 = self.order.send(self.place.core, self.p0)
        self.c1 = self.order.send(self.place.core, self.p1)

    def core(self):
        d0 = self.order.send(self.place.core, self.q0)
        d1 = self.order.send(self.place.core, self.q1)
        self.refs = (self.p0, self.q0, self.p1, self.q1, self.c0, d0, self.c1, d1)


class Unit:
    def __init__(self, place, order, piece, flat):
        self.place, self.order, self.piece, self.flat = place, order, piece, flat

    def ring(self):
        self.a = self.order.send(partial(ring_gather, self.place), self.piece)

    def pair(self):
        self.b = self.order.send(self.place.pair, self.order.see(self.a))

    def across(self):
        self.ax = self.order.send(self.place.across, self.order.see(self.a))

    def near(self):
        self.ca = self.order.send(self.place.core, self.order.see(self.a), 1)

    def two(self):
        see, send = self.order.see, self.order.send
        if self.flat:
            self.bx = send(self.place.pair, see(self.ax))
        else:
            self.bx = send(self.place.across, see(self.b))

    def both(self):
        see, send = self.order.see, self.order.send
        self.cb, self.cax = send(self.place.core, see(self.b), 1), send(self.place.core, see(self.ax), 1)

    def core(self):
        far = self.order.send(self.place.core, self.order.see(self.bx))
        self.refs = (self.a, self.b, self.ax, self.bx, self.ca, self.cb, self.cax, far)


class Sum:
    def __init__(self, place, order, away, keep):
        self.place, self.order = place, order
        self.away, self.keep = away, keep

    def core(self):
        self.came = self.order.send(self.place.core, self.away)

    def one(self):
        see, k = self.order.see, self.keep
        self.came = see(self.came)
        block, dims = (None, None, None) + k.shape[3:], k.shape[2:]
        half = (None,) + dims[1:]
        first, second = (lambda i: (1, 0, i, 0, 0, 0)), (lambda i: (i, 1, 1, 0, 0, 0))
        to = lambda i: (i, 0, 0, 0)
        to_x, to_y = sums(
            2,
            (dims, half, to, [(k, block, first), (self.came, block, first)]),
            (dims, half, to, [(k, block, second), (self.came, block, second)]),
        )
        self.from_x = self.order.send(self.place.across, to_x)
        self.from_y = self.order.send(self.place.pair, to_y)

    def rest(self, name, extra):
        k, r = self.keep, self.came
        _, m, half = k.shape[3:]
        block, part = (None, None, None, 2, m, half), (None, 2, m, half)
        first = (lambda i: (0, 0, 1, i, 0, 0)) if name == "go" else (lambda i: (0, 0, 0, i, 0, 0))
        second = (lambda i: (1, 1, 0, i, 0, 0)) if name == "go" else (lambda i: (0, 1, 0, i, 0, 0))
        side = 1 if name == "go" else 0
        third = lambda i: (side, i, 0, 0)
        plain = lambda i: (i, 0, 0)
        groups = []
        for at_k, came, more in ((first, self.from_x, extra[:1]), (second, self.from_y, extra[1:])):
            members = [(k, block, at_k), (r, block, at_k), (came, part, third)]
            members += [(v, (2, m, half), plain) for v in more]
            groups.append(((4, m, half), (2, m, half), plain, members))
        return sums(2, *groups, joined=name == "stay")

    def two(self):
        self.from_x, self.from_y = self.order.see(self.from_x), self.order.see(self.from_y)
        to_y, to_x = self.rest("go", [])
        self.next_y = self.order.send(self.place.pair, to_y)
        self.next_x = self.order.send(self.place.across, to_x)

    def ring(self):
        see = self.order.see
        both = self.rest("stay", [see(self.next_y), see(self.next_x)])
        self.own = self.order.send(partial(ring_sum, self.place), both)

    def last_x(self):
        self.own = self.order.see(self.own)
        self.own_x = self.order.send(self.place.across, self.own)

    def last_core(self):
        came = self.order.send(self.place.core, jnp.stack([self.own, self.order.see(self.own_x)]))
        self.parts = (self.own, self.own_x, came)


def fast_body(
    groups,
    rows,
    decoder_input,
    encoder_out,
    prefix_length,
    output_grad,
    self_query,
    self_key,
    self_value,
    self_output,
    selfquery_bias,
    selfvalue_bias,
    self_attention_output_bias,
    cross_query,
    cross_key,
    cross_value,
    cross_output,
    crossquery_bias,
    crossvalue_bias,
    crossoutput_bias,
    expand_weight,
    expand_bias,
    down_projection_weight,
    reduce_bias,
    selfnorm_gain,
    selfnorm_bias,
    crossnorm_gain,
    crossnorm_bias,
    finalnorm_gain,
    finalnorm_bias,
):
    place = Place(groups, rows)
    batch, seq, d = decoder_input.shape
    m = self_query.shape[0]
    ff = expand_weight.shape[1]
    rank = 2 * place.x + place.c
    order = Order()

    small = [
        selfnorm_gain, selfnorm_bias, selfquery_bias, selfvalue_bias, self_attention_output_bias,
        crossnorm_gain, crossnorm_bias, crossquery_bias, crossvalue_bias, crossoutput_bias,
        finalnorm_gain, finalnorm_bias, reduce_bias, expand_bias,
    ]
    count = 13 + ff // d

    def pick(*shards):
        return at(jnp.stack(shards), rank)

    u_self = HalfUnit(place, order, pack((self_query, self_key, self_value, self_output), small))
    later = (cross_query, cross_key, cross_value, cross_output, expand_weight, down_projection_weight)
    *later, _ = lax.optimization_barrier((*later, u_self.piece))
    w_e = later[4].reshape(m, rows, 4, -1).transpose(2, 0, 1, 3).reshape(4, m, d)
    w_d = later[5].reshape(4, m, d)
    unit = partial(Unit, place, order)
    u_cross = unit(pick(*later[:4]), True)
    u_low = unit(pick(w_e[0], w_d[0], w_e[1], w_d[1]), False)
    u_high = unit(pick(w_e[2], w_d[2], w_e[3], w_d[3]), True)

    x = decoder_input.reshape(batch * seq, d)
    e = encoder_out.reshape(-1, d)
    dy = output_grad.reshape(batch * seq, d)
    run = order.run

    u_self.ring()
    u_cross.ring()
    u_self.one()
    u_self.two()
    u_cross.pair()
    u_cross.across()
    u_low.ring()
    u_self.core()
    u_cross.near()
    self_w = u_self.refs
    both = jnp.stack([v[:, :, m:] for v in (u_self.p0, jnp.stack([u_self.p1[0], u_self.q1[0]]))])
    both = both.transpose(2, 1, 0, 3, 4)
    both = jnp.where(place.y == 0, both, both[:, ::-1]).reshape(rows, -1)
    vecs = both[:, : count * m].reshape(rows, count, m).transpose(1, 0, 2).reshape(count, d).astype(F32)
    act1, q, k, v = run(first, x, vecs, self_w, m)
    u_cross.two()
    o, p = run(attend, q, k, v, prefix_length, batch, True)
    u_high.ring()
    u_low.across()
    u_cross.both()
    mid1, act2 = run(project, o, x, vecs, (4, 5, 6, None), (self_w,), (3,), m, "self_out")
    u_low.pair()
    u_low.near()
    u_cross.core()
    cross_w = u_cross.refs
    ck, cv = run(memory, e, vecs, cross_w, m)
    u_high.across()
    cq = run(query, act2, vecs, 7, cross_w, m)
    u_high.pair()
    u_low.two()
    co, cp = run(attend, cq, ck, cv, prefix_length, batch, False)
    u_high.two()
    u_low.both()
    u_high.near()
    mid2, act3 = run(project, co, mid1, vecs, (9, 10, 11, None), (cross_w,), (3,), m, "cross_out")
    u_low.core()
    u_high.both()
    low_w = u_low.refs

    *begin, dbe_low, away, keep = run(ffn, act3, dy, mid2, vecs, low_w, m, (), 13)
    total = partial(Sum, place, order)
    g_low = total(away, keep)
    u_high.core()
    g_low.core()
    layer_out, dmid2, dcross, sums3, dbe_high, away, keep = run(
        ffn, act3, dy, mid2, vecs, u_high.refs, m, tuple(begin), 15
    )
    g_high = total(away, keep)
    g_low.one()
    g_high.core()
    dco = run(output_back, dcross, cross_w, m)
    dcq, dck, dcv = run(attend_back, dco, cq, ck, cv, cp, batch)
    g_high.one()
    g_cross = total(*run(grads_of, act2, [e, co], [dcq, dck, dcv, dcross], (0, 1, 1, 2), "cross_grads"))
    g_low.two()
    g_cross.core()
    dmid1, dself, dao, sums2 = run(cross_back, dcq, mid1, dmid2, vecs, cross_w, self_w, m)
    g_cross.one()
    dq, dk, dv = run(attend_back, dao, q, k, v, p, batch)
    g_high.two()
    g_low.ring()
    g_self = total(*run(grads_of, act1, [o], [dq, dk, dv, dself], (0, 0, 0, 1), "self_grads"))
    g_self.core()
    input_grad, sums1 = run(self_back, dq, dk, dv, x, dmid1, vecs, self_w, m)

    def by_shard(v):
        return v.reshape(-1, rows, m).transpose(1, 0, 2)

    g_self.one()
    g_cross.two()
    g_high.ring()
    encoder_grad, sums_e = run(memory_back, dck, dcv, cross_w, m)
    dbe = jnp.concatenate([dbe_low[:2], dbe_high[:2]])
    vec = by_shard(jnp.concatenate([sums1[:4], sums2[:4], sums3[:4], sums_e[:1], dbe]))
    vec = (vec.astype(BF).astype(F32) + order.send(place.core, vec.astype(BF)).astype(F32)).astype(BF)
    g_low.last_x()
    vec = (vec.astype(F32) + order.send(place.across, vec).astype(F32)).astype(BF)
    g_self.two()
    g_cross.ring()
    g_high.last_x()
    g_low.last_core()
    g_high.last_core()
    vec = vec.reshape((place.ring, 2) + vec.shape[1:])
    came = order.send(place.pair, at(vec, 1 - place.y, 1))
    vec = (at(vec, place.y, 1).astype(F32) + came.astype(F32)).astype(BF)
    g_self.ring()
    g_cross.last_x()
    vec = order.send(partial(ring_sum, place), vec).astype(F32)
    g_expand, g_down = run(finish, *g_low.parts, parts=(g_high.parts,))
    g_cross.last_core()
    g_self.last_x()
    g_cq, g_ck, g_cv, g_co = run(finish, *g_cross.parts)
    g_self.last_core()
    g_sq, g_sk, g_sv, g_so = run(finish, *g_self.parts)
    return (
        layer_out.reshape(batch, seq, d),
        input_grad.reshape(batch, seq, d),
        encoder_grad.reshape(encoder_out.shape),
        g_sq, g_sk, g_sv, g_so,
        vec[2], vec[3], vec[7],
        g_cq, g_ck, g_cv, g_co,
        vec[6], vec[12], vec[11],
        g_expand, vec[13:].reshape(-1), g_down, vec[10],
        vec[0], vec[1], vec[4], vec[5], vec[8], vec[9],
    )


def solution(mesh):
    groups, rows = mesh.shape["replica"], mesh.shape["fsdp"]
    data = P(("replica", "fsdp"), None, None)
    mat, vec = P("fsdp", None), P("fsdp")
    weights = (
        (mat,) * 4 + (vec,) * 3 + (mat,) * 4 + (vec,) * 3 + (mat, vec, mat, vec) + (vec,) * 6
    )
    return jax.shard_map(
        partial(fast_body if rows == 8 else body, groups, rows),
        mesh=mesh,
        in_specs=(data, data, P(("replica", "fsdp")), data) + weights,
        out_specs=(data, data, data) + weights,
        check_vma=False,
    )
```
